32 devices in a mesh: seq: 4 (over z), batch: 4 (over x, core), tensor: 2 (over y).
Axes of the slice: x: 2, y: 2, z: 4, core: 2. Of those that a mesh axis runs over, the one named last changes fastest.
Arguments:
- inputs: bfloat16 [4, 1024, 768], P('batch', 'seq'), may hold values from -16 to 16
- history: bfloat16 [8, 4, 1024, 768], P(None, 'batch', 'seq'), may hold values from -6 to 6
- window_lengths: int32 [4, 3], P('batch'), may hold values from 1 to 768, 1024 in all within a row
- block_order: int32 [4], replicated, may hold values from 0 to 3, each once
- first_gain: float32 [768], replicated, may hold values from 0.5 to 1.5
- first_shift: float32 [768], replicated, may hold values from -1.5 to 1.5
- query_weight: bfloat16 [768, 768], P(None, 'tensor'), may hold values from -0.21875 to 0.21875
- key_weight: bfloat16 [768, 768], P(None, 'tensor'), may hold values from -0.21875 to 0.21875
- value_weight: bfloat16 [768, 768], P(None, 'tensor'), may hold values from -0.21875 to 0.21875
- out_weight: bfloat16 [768, 768], P('tensor'), may hold values from -1.75 to 1.75
- second_gain: float32 [768], replicated, may hold values from 0.5 to 1.5
- second_shift: float32 [768], replicated, may hold values from -1.5 to 1.5
- up_weight: bfloat16 [768, 3072], P(None, 'tensor'), may hold values from -0.21875 to 0.21875
- up_bias: float32 [3072], P('tensor'), may hold values from -2.5 to 2.5
- down_weight: bfloat16 [3072, 768], P('tensor'), may hold values from -0.109375 to 0.109375
- down_bias: float32 [768], replicated, may hold values from -1.5 to 1.5
- mix_weights: float32 [9], replicated, may hold values from -2.5 to 2.5
- cotangent_next: bfloat16 [4, 1024, 768], P('batch', 'seq'), may hold values from -6 to 6
- cotangent_block: bfloat16 [4, 1024, 768], P('batch', 'seq'), may hold values from -6 to 6
Outputs:
- next_input: bfloat16 [4, 1024, 768], P('batch', 'seq')
- block_output: bfloat16 [4, 1024, 768], P('batch', 'seq')
- grad_input: bfloat16 [4, 1024, 768], P('batch', 'seq')
- grad_history: bfloat16 [8, 4, 1024, 768], P(None, 'batch', 'seq')
- grad_first_gain: float32 [768], replicated
- grad_first_shift: float32 [768], replicated
- grad_query_weight: float32 [768, 768], P(('seq', 'batch'), 'tensor')
- grad_key_weight: float32 [768, 768], P(('seq', 'batch'), 'tensor')
- grad_value_weight: float32 [768, 768], P(('seq', 'batch'), 'tensor')
- grad_out_weight: float32 [768, 768], P('tensor', ('seq', 'batch'))
- grad_second_gain: float32 [768], replicated
- grad_second_shift: float32 [768], replicated
- grad_up_weight: float32 [768, 3072], P(('seq', 'batch'), 'tensor')
- grad_up_bias: float32 [3072], P('tensor')
- grad_down_weight: float32 [3072, 768], P('tensor', ('seq', 'batch'))
- grad_down_bias: float32 [768], replicated
- grad_mix_weights: float32 [9], replicated
- rms_values: float32 [3], replicated
The draws below stay inside these ranges and needn't reach their ends.
Inputs may be any that keep to these rules, and one draw needn't show every extreme that they name: `window_lengths`: each row sums to 1024; the longest window of each row has exactly 768 tokens. A permutation; index i of seq holds positions block_order[i] * 256 to block_order[i] * 256 + 255 of each sequence.
All inputs are finite; a program needn't handle non-finite values.
Results may differ from the reference program's by a relative error of at most 0.025.
Values may be sent and summed in bfloat16 or wider, within the bound.
A program may use at most 192 MiB of HBM per device.

```python
import math
from functools import partial
import jax
import jax.numpy as jnp
import numpy as np
from jax import lax

D = 768
HEAD_DIM = 64
FF = 3072
HIST = 8
NDOC = 3
TOK_DEV = 256
SEQ_TOK = 1024
NSEQS = 4
BLOCKS = 4
LONGEST = 768


def draw_inputs(key, part):
    rising = jnp.exp(jnp.log(3.0) * jnp.arange(SEQ_TOK, dtype=jnp.float32) / SEQ_TOK)
    base = jnp.clip(jax.random.normal(key, (NSEQS, SEQ_TOK, D), jnp.float32), -5.0, 5.0)
    return (base * rising[None, :, None]).astype(jnp.bfloat16)


def raised(drawn, stream_key, source, target, blocks, factor):
    owner, partner = [(jnp.arange(drawn.shape[dim]) // (drawn.shape[dim] // blocks)).reshape([-1 if axis == dim else 1 for axis in range(drawn.ndim)]) for dim in (source, target)]
    chosen = jax.random.permutation(stream_key, blocks)[partner]
    strong = (owner == chosen) | (owner == (partner + blocks // 2) % blocks)
    return jnp.where(strong, factor * drawn, drawn)


def steps_of(own_key, shape, cuts, smallest, largest):
    def one(dim, parts):
        steps = jax.random.uniform(jax.random.fold_in(jax.random.fold_in(own_key, 6), dim), (parts,), jnp.float32, smallest / len(cuts), largest / len(cuts))
        return jnp.repeat(jnp.exp(steps), shape[dim] // parts).reshape((-1,) + (1,) * (len(shape) - dim - 1))

    loudness = one(*cuts[0])
    for cut in cuts[1:]:
        loudness = loudness * one(*cut)
    return loudness


def split_up(count, total, bound, slope):
    portions = [(1 << 20) // math.isqrt(standing ** slope) + 1 for standing in range(2, count + 1)]
    surplus, holding = total - bound - (count - 1), [1] * (count - 1)
    while surplus > 0:
        free = [i for i in range(count - 1) if holding[i] < bound]
        whole, remaining = sum([portions[i] for i in free]), surplus
        for i in free:
            extra = min(bound - holding[i], max(1, remaining * portions[i] // whole), surplus)
            holding[i] = holding[i] + extra
            surplus = surplus - extra
    return np.array([bound] + holding)


def uneven_parts(key, amount, total, limit, slope):
    if amount == 2:
        one = jax.random.randint(key, (), max(1, total - limit), min(limit, total - 1) + 1)
        return jnp.stack([one, total - one])
    tallies = jnp.asarray(split_up(amount, total, limit, slope), jnp.int32)
    twos = (amount - 1) // 2
    source_of, taker = tallies[1:1 + 2 * twos:2], tallies[2:2 + 2 * twos:2]
    slack = jnp.minimum(source_of - 1, limit - taker)
    moved = jax.random.randint(jax.random.fold_in(key, 1), (twos,), 0, 1 << 20) % (slack + 1)
    tallies = tallies.at[1:1 + 2 * twos:2].set(source_of - moved).at[2:2 + 2 * twos:2].set(taker + moved)
    return tallies[jax.random.permutation(jax.random.fold_in(key, 2), amount)]


def bell_draw(stream_key, dims, scale, reach, cuts=(), held_as=jnp.bfloat16):
    drawn = jax.random.normal(stream_key, dims, jnp.float32) * scale
    if len(cuts) > 0:
        drawn = steps_of(stream_key, dims, cuts, -0.22, 0.18) * drawn
    return jnp.clip(drawn, min=-reach, max=reach).astype(held_as)


def bell_draw_with(rng, extent, scale, limit, shards, heavy, held_as=jnp.bfloat16):
    entries = scale * jax.random.normal(rng, extent, jnp.float32)
    if shards:
        entries = entries * steps_of(rng, extent, shards, -0.22, 0.18)
    return jnp.clip(raised(entries, jax.random.fold_in(rng, 3), *heavy), -limit, limit).astype(held_as)


def setup_inputs(seed: int = 0) -> dict:
    streams_of = jax.random.split(jax.random.key(seed), 20)
    return {
        "inputs": draw_inputs(jax.random.fold_in(streams_of[19], 71), 0),
        "history": bell_draw(streams_of[1], (HIST, NSEQS, SEQ_TOK, D), 1.0, 6.0, ((1, 4), (2, 4))),
        "window_lengths": jax.vmap(lambda own: uneven_parts(own, NDOC, SEQ_TOK, LONGEST, 1))(jax.random.split(streams_of[2], NSEQS)).reshape((NSEQS, NDOC)).astype(jnp.int32),
        "block_order": jax.random.permutation(streams_of[3], BLOCKS).astype(jnp.int32),
        "first_gain": jnp.clip(1.0 + 0.1 * jax.random.normal(streams_of[4], (D,), jnp.float32), 0.5, 1.5),
        "first_shift": bell_draw(streams_of[5], (D,), 0.3, 1.5, (), jnp.float32),
        "query_weight": bell_draw(streams_of[6], (D, D), D ** -0.5, 0.21875, ((1, 2),)),
        "key_weight": bell_draw(streams_of[7], (D, D), D ** -0.5, 0.21875, ((1, 2),)),
        "value_weight": bell_draw(streams_of[8], (D, D), D ** -0.5, 0.21875, ((1, 2),)),
        "out_weight": bell_draw(streams_of[9], (D, D), (D // 64) ** -0.5, 1.75, ((0, 2),)),
        "second_gain": jnp.clip(1.0 + 0.1 * jax.random.normal(streams_of[10], (D,), jnp.float32), 0.5, 1.5),
        "second_shift": bell_draw(streams_of[11], (D,), 0.3, 1.5, (), jnp.float32),
        "up_weight": bell_draw(streams_of[12], (D, FF), D ** -0.5, 0.21875, ((1, 2),)),
        "up_bias": bell_draw(streams_of[13], (FF,), 0.5, 2.5, ((0, 2),), jnp.float32),
        "down_weight": bell_draw(streams_of[14], (FF, D), FF ** -0.5, 0.109375, ((0, 2),)),
        "down_bias": bell_draw(streams_of[15], (D,), 0.3, 1.5, (), jnp.float32),
        "mix_weights": bell_draw(streams_of[16], (HIST + 1,), 0.5, 2.5, (), jnp.float32),
        "cotangent_next": bell_draw(streams_of[17], (NSEQS, SEQ_TOK, D), 1.0, 6.0, ((0, 4), (1, 4))),
        "cotangent_block": bell_draw_with(streams_of[18], (NSEQS, SEQ_TOK, D), 1.0, 6.0, ((0, 4), (1, 4)), (1, 2, 4, 2.0)),
    }


@jax.custom_vjp
def low(v):
    return lax.optimization_barrier(v.astype(jnp.bfloat16)).astype(jnp.float32)

@jax.custom_vjp
def low_back(v):
    return v

def low_keep(v):
    return (low(v), None)

def low_pass(kept, grad):
    return (grad,)

def back_keep(v):
    return (v, None)

def back_low(kept, grad):
    return (low(grad),)
low.defvjp(low_keep, low_pass)
low_back.defvjp(back_keep, back_low)
epsilon = 1e-05
highest = lax.Precision.HIGHEST

def layer_norm(values, gain, shift):
    centre = lax.optimization_barrier(jnp.mean(values, axis=-1, keepdims=True))
    centred = values - centre
    spread = lax.optimization_barrier(jnp.mean(centred * centred, axis=-1, keepdims=True))
    return centred * lax.rsqrt(spread + epsilon) * gain + shift

def gelu_tanh(values):
    return 0.5 * values * (1.0 + jnp.tanh(0.7978845608028654 * (values + 0.044715 * values * values * values)))

def rotate(values, cosine, sine):
    half = values.shape[-1] // 2
    first = values[..., :half]
    second = values[..., half:]
    return jnp.concatenate([first * cosine - second * sine, second * cosine + first * sine], axis=-1)

def project(values, weight):
    return jnp.einsum('bsd,de->bse', values, weight, precision=highest)

def block_attend(queries, keys, values, query_docs, key_docs, offset):
    scores = low_back(jnp.einsum('qhd,khd->hqk', queries, keys, precision=highest))
    query_pos = offset + jnp.arange(queries.shape[0], dtype=jnp.int32)
    key_pos = jnp.arange(keys.shape[0], dtype=jnp.int32)
    allowed = (key_pos[None, :] <= query_pos[:, None]) & (key_docs[None, :] == query_docs[:, None])
    masked = jnp.where(allowed[None], scores, -1e+30)
    peak = lax.optimization_barrier(jnp.max(masked, axis=-1, keepdims=True))
    expo = jnp.exp(masked - peak)
    probs = expo / lax.optimization_barrier(jnp.sum(expo, axis=-1, keepdims=True))
    return jnp.einsum('hqk,khd->qhd', low(probs), values, precision=highest)

def attend_sequence(items):
    queries, keys, values, docs = items
    span = min(512, SEQ_TOK)
    pieces = []
    for block in range(SEQ_TOK // span):
        stop = (block + 1) * span
        step_fn = jax.checkpoint(partial(block_attend, offset=block * span))
        pieces.append(step_fn(queries[block * span:stop], keys[:stop], values[:stop], docs[block * span:stop], docs[:stop]))
    return jnp.concatenate(pieces, axis=0)

def forward(inputs, history, params, cosine, sine, docs):
    first_gain, first_shift, query_weight, key_weight, value_weight, out_weight, second_gain, second_shift, up_weight, up_bias, down_weight, down_bias, mix_weights = params
    seqs, length, width = inputs.shape
    heads = width // HEAD_DIM
    split = (seqs, length, heads, HEAD_DIM)
    normed = low(layer_norm(inputs, first_gain, first_shift))
    queries = low(rotate(low_back(project(normed, query_weight)).reshape(split), cosine, sine) * 0.125)
    keys = low(rotate(low_back(project(normed, key_weight)).reshape(split), cosine, sine))
    values = low(low_back(project(normed, value_weight))).reshape(split)
    mixed = lax.map(attend_sequence, (queries, keys, values, docs))
    mixed = low(low_back(mixed.reshape(seqs, length, width)))
    attn_out = low_back(project(mixed, out_weight))
    hidden = inputs + attn_out
    normed_second = low(layer_norm(hidden, second_gain, second_shift))
    upward = low_back(project(normed_second, up_weight) + up_bias)
    active = low(gelu_tanh(upward))
    mlp_out = low_back(project(active, down_weight) + down_bias)
    block_value = hidden + mlp_out
    next_value = jnp.einsum('j,jbsd->bsd', mix_weights[:HIST], history, precision=highest) + mix_weights[HIST] * block_value
    return ((next_value, block_value), (attn_out, mlp_out))

def reference(inputs, history, window_lengths, block_order, first_gain, first_shift, query_weight, key_weight, value_weight, out_weight, second_gain, second_shift, up_weight, up_bias, down_weight, down_bias, mix_weights, cotangent_next, cotangent_block):
    rows = jnp.arange(SEQ_TOK, dtype=jnp.int32)
    holder = jnp.zeros((BLOCKS,), jnp.int32).at[block_order].set(jnp.arange(BLOCKS, dtype=jnp.int32))
    source = (holder[rows // TOK_DEV] * TOK_DEV + rows % TOK_DEV).astype(jnp.int32)
    target = (block_order[rows // TOK_DEV] * TOK_DEV + rows % TOK_DEV).astype(jnp.int32)
    ends = jnp.cumsum(window_lengths, axis=1)
    docs = lax.optimization_barrier(jnp.sum((rows[None, :, None] >= ends[:, None, :]).astype(jnp.int32), axis=-1))
    half = HEAD_DIM // 2
    rates = jnp.exp(-jnp.log(10000.0) * jnp.arange(half, dtype=jnp.float32) / half)
    angles = rows.astype(jnp.float32)[:, None] * rates[None, :]
    cosine = jnp.cos(angles)[:, None, :]
    sine = jnp.sin(angles)[:, None, :]
    start_inputs = jnp.take(inputs.astype(jnp.float32), source, axis=1)
    start_history = jnp.take(history.astype(jnp.float32), source, axis=2)
    params = (first_gain.astype(jnp.float32), first_shift.astype(jnp.float32), query_weight.astype(jnp.float32), key_weight.astype(jnp.float32), value_weight.astype(jnp.float32), out_weight.astype(jnp.float32), second_gain.astype(jnp.float32), second_shift.astype(jnp.float32), up_weight.astype(jnp.float32), up_bias.astype(jnp.float32), down_weight.astype(jnp.float32), down_bias.astype(jnp.float32), mix_weights.astype(jnp.float32))

    def wrapped(inputs_value, history_value, param_values):
        return forward(inputs_value, history_value, param_values, cosine, sine, docs)
    primal, pull, extras = jax.vjp(wrapped, start_inputs, start_history, params, has_aux=True)
    next_value, block_value = primal
    attn_out, mlp_out = extras
    cot_next = jnp.take(cotangent_next.astype(jnp.float32), source, axis=1)
    cot_block = jnp.take(cotangent_block.astype(jnp.float32), source, axis=1)
    grad_inputs, grad_hist, grads = pull((cot_next, cot_block))
    rms_values = jnp.stack([jnp.sqrt(jnp.mean(block_value * block_value)), jnp.sqrt(jnp.mean(attn_out * attn_out)), jnp.sqrt(jnp.mean(mlp_out * mlp_out))])
    next_input = jnp.take(next_value, target, axis=1).astype(jnp.bfloat16)
    block_output = jnp.take(block_value, target, axis=1).astype(jnp.bfloat16)
    grad_input = jnp.take(grad_inputs, target, axis=1).astype(jnp.bfloat16)
    grad_history = jnp.take(grad_hist, target, axis=2).astype(jnp.bfloat16)
    return (next_input, block_output, grad_input, grad_history, grads[0], grads[1], grads[2], grads[3], grads[4], grads[5], grads[6], grads[7], grads[8], grads[9], grads[10], grads[11], grads[12], rms_values)
```

```python
import functools
from types import SimpleNamespace

import jax
import jax.numpy as jnp
from jax import lax
from jax.experimental import pallas as pl
from jax.experimental.pallas import tpu as pltpu
from jax.sharding import PartitionSpec as P

HEAD_DIM = 64
f32, bf16, i32 = jnp.float32, jnp.bfloat16, jnp.int32
MESH = pl.DeviceIdType.MESH


epsilon = 1e-05


def layer_parts(values, gain, shift):
    centre = jnp.mean(values, axis=-1, keepdims=True)
    centred = values - centre
    spread = jnp.mean(centred * centred, axis=-1, keepdims=True)
    inverse = lax.rsqrt(spread + epsilon)
    unit = centred * inverse
    return (unit * gain + shift, unit, inverse)


def norm_backward(grad_out, unit, inverse, gain):
    scaled = grad_out * gain
    return inverse * (
        scaled
        - jnp.mean(scaled, axis=-1, keepdims=True)
        - unit * jnp.mean(scaled * unit, axis=-1, keepdims=True)
    )


def gelu_tanh(values):
    return (
        0.5
        * values
        * (1.0 + jnp.tanh(0.7978845608028654 * (values + 0.044715 * values * values * values)))
    )


def rotate(values, cosine, sine):
    half = values.shape[-1] // 2
    first = values[..., :half]
    second = values[..., half:]
    return jnp.concatenate(
        [first * cosine - second * sine, second * cosine + first * sine], axis=-1
    )


def keep_state(state):
    return state


def dot(a, b, ca=1, cb=0):
    return lax.dot_general(a, b, (((ca,), (cb,)), ((), ())), preferred_element_type=f32)


def rope_tables(pos, half):
    index = lax.broadcasted_iota(i32, (half, 1), 0).astype(f32)
    rates = jnp.exp(-jnp.log(f32(10000.0)) * index / half)
    angles = rates * pos
    return jnp.cos(angles), jnp.sin(angles)


def rotate_t(lin, cosine, sine):
    width, rows = lin.shape
    parts = lin.reshape(width // HEAD_DIM, 2, HEAD_DIM // 2, rows)
    first, second = parts[:, 0], parts[:, 1]
    turned = [first * cosine - second * sine, second * cosine + first * sine]
    return jnp.stack(turned, axis=1).reshape(width, rows)


def gelu_both(u):
    square = u * u
    t = jnp.tanh(0.7978845608028654 * (u + 0.044715 * square * u))
    half = 0.5 * (1.0 + t)
    slope = half + 0.5 * u * (1.0 - t * t) * (0.7978845608028654 * (1.0 + 3 * 0.044715 * square))
    return u * half, slope


def row_chunks(rows, body, size=64):
    def step(i, _):
        body(pl.ds(pl.multiple_of(i * size, size), size))
        return 0

    lax.fori_loop(0, rows // size, step, 0)


def folded(rows):
    total = jnp.sum(rows, axis=0, keepdims=True)
    return sum(total[:, k : k + 128] for k in range(0, total.shape[1], 128))


ROWS, WIDTH, LOCAL, GROUP, HIDDEN, BLOCK = 256, 768, 384, 192, 1536, 48


def scratch_spec():
    vm = pltpu.VMEM
    heads = (3, HEAD_DIM, ROWS)
    full32, full16, turned = vm((ROWS, WIDTH), f32), vm((ROWS, WIDTH), bf16), vm((WIDTH, ROWS), bf16)

    def job(columns):
        return [
            vm((2, 2, 2, 2, BLOCK, columns), bf16), vm((2, 2, 2, BLOCK, columns), bf16),
            vm((2, 2, BLOCK, columns), bf16), vm((2, BLOCK, columns), bf16), vm((BLOCK, columns), bf16),
        ]

    return dict(
        hist=vm((8, ROWS, WIDTH), bf16), wup=vm((6, WIDTH, 256), bf16), wdown=vm((6, 256, WIDTH), bf16),
        wof=vm((2, 2, GROUP, WIDTH), bf16),
        qown=vm((2, *heads), bf16), kown=vm((2, *heads), bf16), vown=vm((2, *heads), bf16),
        qt=vm((2, *heads), bf16), kt=vm((4, *heads), bf16), vt=vm((4, *heads), bf16),
        scores=vm((3, 2, 4, ROWS, ROWS), f32), bias=vm((ROWS, ROWS), f32),
        peak=vm((3, 2, 1, ROWS), f32), denom=vm((3, 2, 1, ROWS), f32), acc=vm((3, 2, HEAD_DIM, ROWS), f32),
        delta=vm((3, 2, 1, ROWS), f32), cosine=vm((32, ROWS), f32), sine=vm((32, ROWS), f32),
        mix=vm((2, 2, GROUP, ROWS), bf16), mixout=vm((GROUP, ROWS), bf16),
        unit1=full32, inv1=vm((ROWS, 1), f32), norm1=full16, norm1t=turned,
        hidden=full32, attn=full32, unit2=full32, inv2=vm((ROWS, 1), f32), norm2=full16, norm2t=turned,
        gblock=full32, gmlp=full16, gmlpt=turned, hacc=full32, gact=vm((6, ROWS, 256), f32),
        act=vm((6, ROWS, 256), bf16), gup=vm((6, ROWS, 256), bf16), gnorm2=full32, gnew=full32, upsum=vm((6, 1, 256), f32),
        ghid=vm((2, ROWS, WIDTH), bf16), mlp=vm((2, ROWS, WIDTH), bf16), gin=vm((2, ROWS, WIDTH), bf16),
        dpart=vm((2, 2, GROUP, ROWS), bf16), dsend=vm((2, 2, GROUP, ROWS), bf16), dout=vm((2, *heads), bf16),
        dkv=vm((4, 2, GROUP, ROWS), bf16), dkvin=vm((4, 2, GROUP, ROWS), bf16),
        dq=vm((2, 3, HEAD_DIM, ROWS), f32), dqout=vm((GROUP, ROWS), bf16), dqin=vm((GROUP, ROWS), bf16),
        own0=vm((2, GROUP, ROWS), f32), lin=vm((3, 2, GROUP, ROWS), bf16), gattnt=turned,
        small=vm((5, 16, WIDTH), f32), smallin=vm((3, 16, WIDTH), f32), smallz=vm((3, 16, WIDTH), f32),
        job0=job(HIDDEN), job1=job(HIDDEN), job2=job(LOCAL), job3=job(640), job4=job(512),
        ssem=pltpu.SemaphoreType.DMA((64,)), rsem=pltpu.SemaphoreType.DMA((64,)), lsem=pltpu.SemaphoreType.DMA((16,)),
    )


def layer_kernel(make, *refs):
    R = make(refs)
    z, b, y = lax.axis_index("seq"), lax.axis_index("batch"), lax.axis_index("tensor")
    near, flip, far = z + 1 - 2 * (z % 2), (z + 2) % 4, 3 - z
    m, p, xbit, core = z % 2, z // 2, b // 2, b % 2
    to_near, to_flip, to_far = dict(seq=near), dict(seq=flip), dict(seq=far)
    to_y, to_diag = dict(tensor=1 - y), dict(seq=near, tensor=1 - y)
    to_x, to_core = dict(batch=(b + 2) % 4), dict(batch=b + 1 - 2 * core)
    barrier = pltpu.get_barrier_semaphore()
    everyone = [to_near, to_flip, to_far, to_y, to_diag, to_x, to_core]
    for there in everyone:
        pl.semaphore_signal(barrier, inc=1, device_id=there, device_id_type=MESH)
    started = []

    def send(src, dst, there):
        i = len(started)
        copy = pltpu.make_async_remote_copy(
            src, dst, R.ssem.at[i], R.rsem.at[i], device_id=there, device_id_type=MESH
        )
        copy.start()
        started.append(copy)
        return copy

    def fetch(src, dst, i):
        copy = pltpu.make_async_copy(src, dst, R.lsem.at[i])
        copy.start()
        return copy

    get_out = fetch(R.wout, R.wof.at[0], 0)
    get_hist = fetch(R.history, R.hist, 1)
    get_down = fetch(R.wdown_h, R.wdown, 2)
    get_up = [fetch(R.wup_h.at[:, pl.ds(256 * n, 256)], R.wup.at[n], 3 + n) for n in range(6)]
    ends, total = [], 0
    for i in range(R.windows.shape[0]):
        total = total + R.windows[i]
        ends.append(total)
    base = [R.order[k] * ROWS for k in (z, near, flip, far)]
    lane = lax.broadcasted_iota(i32, (1, ROWS), 1)

    def norm_first(rows):
        x = R.x[rows].astype(f32)
        centred = x - jnp.mean(x, axis=-1, keepdims=True)
        inverse = lax.rsqrt(jnp.mean(centred * centred, axis=-1, keepdims=True) + epsilon)
        unit = centred * inverse
        R.unit1[rows] = unit
        R.inv1[rows] = inverse
        R.norm1[rows] = (unit * R.gain1[...] + R.shift1[...]).astype(bf16)

    row_chunks(ROWS, norm_first)
    cosine, sine = rope_tables((base[0] + lane).astype(f32), HEAD_DIM // 2)
    R.cosine[...] = cosine
    R.sine[...] = sine
    split = (2, 3, HEAD_DIM, ROWS)
    R.kown[...] = rotate_t(dot(R.norm1[...], R.wk[...]).T, cosine, sine).astype(bf16).reshape(split)
    pl.semaphore_wait(barrier, len(everyone))
    k_in = [send(R.kown.at[m], R.kt.at[2], to_flip), send(R.kown.at[1 - m], R.kt.at[3], to_far)]
    k_in.append(send(R.kown.at[1 - m], R.kt.at[1], to_near))
    R.vown[...] = dot(R.norm1[...], R.wv[...]).T.astype(bf16).reshape(split)
    v_in = [send(R.vown.at[m], R.vt.at[2], to_flip), send(R.vown.at[1 - m], R.vt.at[3], to_far)]
    v_in.append(send(R.vown.at[1 - m], R.vt.at[1], to_near))
    queries = rotate_t(dot(R.norm1[...], R.wq[...]).T, cosine, sine) * 0.125
    R.qown[...] = queries.astype(bf16).reshape(split)
    q_in = send(R.qown.at[1 - m], R.qt.at[1], to_near)
    get_out.wait()
    out_in = send(R.wof.at[0], R.wof.at[1], to_y)
    R.qt[0] = R.qown[m]
    R.kt[0] = R.kown[m]
    R.vt[0] = R.vown[m]

    def tile(j, r, first=False):
        qpos = base[j] + lane
        start = 0 * qpos
        for end in ends:
            start = jnp.maximum(start, jnp.where(qpos >= end, end, 0))
        kpos = base[r] + lax.broadcasted_iota(i32, (ROWS, ROWS), 0)
        R.bias[...] = jnp.where((kpos <= qpos) & (kpos >= start), 0.0, -1e30).astype(f32)
        for h in range(3):
            s = dot(R.kt[r, h], R.qt[j, h], 0, 0) + R.bias[...]
            R.scores[h, j, r] = s
            top = jnp.max(s, axis=0, keepdims=True)
            if first:
                e = jnp.exp(s - top)
                R.denom[h, j] = jnp.sum(e, axis=0, keepdims=True)
                R.acc[h, j] = dot(R.vt[r, h], e.astype(bf16))
            else:
                old = R.peak[h, j]
                top = jnp.maximum(top, old)
                e = jnp.exp(s - top)
                alpha = jnp.exp(old - top)
                R.denom[h, j] = R.denom[h, j] * alpha + jnp.sum(e, axis=0, keepdims=True)
                R.acc[h, j] = R.acc[h, j] * alpha + dot(R.vt[r, h], e.astype(bf16))
            R.peak[h, j] = top

    tile(0, 0, True)
    R.small[0] = jnp.zeros((16, WIDTH), f32)
    mix_last = R.mixw[8]

    def block_grads(rows):
        g = R.cotb[rows].astype(f32) + mix_last * R.cotn[rows].astype(f32)
        R.gblock[rows] = g
        low = g.astype(bf16)
        R.gmlp[rows] = low
        R.small[0, 4:5] += 0.5 * jnp.sum(low.astype(f32), axis=0, keepdims=True)

    row_chunks(ROWS, block_grads)
    R.gmlpt[...] = R.gmlp[...].T
    R.norm1t[...] = R.norm1[...].T
    for c in (k_in[2], v_in[2], q_in):
        c.wait_recv()
    tile(0, 1)
    tile(1, 1, True)
    tile(1, 0)
    get_hist.wait()

    def history_sum(rows):
        cot = R.cotn[rows].astype(f32)
        total = 0
        for j in range(8):
            h = R.hist[j, rows].astype(f32)
            total = total + R.mixw[j] * h
            R.small[0, 5 + j // 6 : 6 + j // 6, 128 * (j % 6) : 128 * (j % 6) + 128] += 0.5 * folded(h * cot)
        R.hacc[rows] = total

    row_chunks(ROWS, history_sum, 32)
    get_down.wait()

    def active_grad(n, _):
        R.gact[n] = dot(R.gmlp[...], R.wdown[n], 1, 1)
        return 0

    lax.fori_loop(0, 6, active_grad, 0)
    for c in (k_in[0], v_in[0]):
        c.wait_recv()
    tile(1, 2)
    tile(0, 2)
    for c in (k_in[1], v_in[1]):
        c.wait_recv()
    tile(1, 3)

    def finish(j):
        for h in range(3):
            R.acc[h, j] = R.acc[h, j] * (1.0 / R.denom[h, j])
            R.peak[h, j] = R.peak[h, j] + jnp.log(R.denom[h, j])
        return jnp.concatenate([R.acc[h, j] for h in range(3)], axis=0).astype(bf16)

    R.mixout[...] = finish(1)
    mix_in = [send(R.mixout, R.mix.at[1, 1], to_diag), send(R.mixout, R.mix.at[0, 1], to_near)]
    tile(0, 3)
    R.mix[0, 0] = finish(0)
    mix_in.append(send(R.mix.at[0, 0], R.mix.at[1, 0], to_y))
    for c in get_up:
        c.wait()
    out_in.wait_recv()
    for c in mix_in:
        c.wait_recv()
    out = 0
    for t in range(2):
        for a in range(2):
            out = out + dot(R.mix[(t + y) % 2, (a + m) % 2], R.wof[(t + y) % 2, a], 0, 0)
    R.attn[...] = out

    def norm_second(rows):
        hidden = R.x[rows].astype(f32) + R.attn[rows]
        R.hidden[rows] = hidden
        centred = hidden - jnp.mean(hidden, axis=-1, keepdims=True)
        inverse = lax.rsqrt(jnp.mean(centred * centred, axis=-1, keepdims=True) + epsilon)
        unit = centred * inverse
        R.unit2[rows] = unit
        R.inv2[rows] = inverse
        R.norm2[rows] = (unit * R.gain2[...] + R.shift2[...]).astype(bf16)

    row_chunks(ROWS, norm_second)

    def mlp_step(n, _):
        u = dot(R.norm2[...], R.wup[n]) + R.upb[n]
        active, slope = gelu_both(u)
        R.act[n] = active.astype(bf16)
        grad = (R.gact[n] * slope).astype(bf16)
        R.gup[n] = grad
        R.upsum[n] = jnp.sum(grad.astype(f32), axis=0, keepdims=True)
        back = dot(grad, R.wup[n], 1, 1)

        @pl.when(n == 0)
        def _():
            R.gnorm2[...] = back

        @pl.when(n > 0)
        def _():
            R.gnorm2[...] += back

        return 0

    lax.fori_loop(0, 6, mlp_step, 0)

    def norm_back(grad, unit, inverse, gain):
        scaled = grad * gain
        return inverse * (
            scaled
            - jnp.mean(scaled, axis=-1, keepdims=True)
            - unit * jnp.mean(scaled * unit, axis=-1, keepdims=True)
        )

    def second_back(rows):
        back = norm_back(R.gnorm2[rows], R.unit2[rows], R.inv2[rows], R.gain2[...])
        R.ghid[0, rows] = (0.5 * R.gblock[rows] + back).astype(bf16)

    row_chunks(ROWS, second_back)
    for t in (1, 0):
        for a in (1, 0):
            part = dot(R.wof[t, (a + m) % 2], R.ghid[0], 1, 1).astype(bf16)
            if t == 0 and a == 0:
                R.dpart[0, 0] = part
            else:
                R.dsend[t, a] = part
    d_in = [
        send(R.dsend.at[1, 1], R.dpart.at[1, 1], to_diag),
        send(R.dsend.at[1, 0], R.dpart.at[0, 1], to_y),
        send(R.dsend.at[0, 1], R.dpart.at[1, 0], to_near),
    ]
    ghid_in = send(R.ghid.at[0], R.ghid.at[1], to_y)

    bits = dict(core=core, x=xbit, near=m, flip=p)
    where = dict(core=to_core, x=to_x, near=to_near, flip=to_flip)
    place = dict(core=0, x=1, near=2, flip=3)

    class Job:
        def __init__(self, bufs, route):
            self.grads, self.landing, self.route, self.copy, self.step = bufs[0], bufs[1:], route, None, 0

        def put(self, value, columns):
            for k in range(16):
                at = tuple((k >> place[axis]) & 1 for axis in self.route)
                self.grads[(*at, slice(None), columns)] = value[BLOCK * k : BLOCK * k + BLOCK].astype(bf16)

        def mine(self):
            return tuple(bits[axis] for axis in self.route[: self.step])

        def push(self):
            axis = self.route[self.step]
            self.copy = send(self.grads.at[(*self.mine(), 1 - bits[axis])], self.landing[self.step], where[axis])

        def pull(self, out=None):
            self.copy.wait_recv()
            landing = self.landing[self.step]
            self.step += 1
            kept = self.mine()
            left = 4 - self.step

            def add(i, _):
                at = tuple((i // 2**k) % 2 for k in range(left))
                both = self.grads[(*kept, *at)].astype(f32) + landing[at if at else Ellipsis].astype(f32)
                if out is None:
                    self.grads[(*kept, *at)] = both.astype(bf16)
                else:
                    out[...] = both
                return 0

            if left:
                lax.fori_loop(0, 2**left, add, 0)
            else:
                add(0, 0)

        def turn(self):
            self.pull()
            self.push()

    usual = tuple(dict(core=0, x=0, near=0, flip=0))
    x_last = tuple(dict(core=0, near=0, flip=0, x=0))
    job_down, job_up = Job(R.job0, usual), Job(R.job1, usual)
    job_out, job_a, job_b = Job(R.job2, usual), Job(R.job3, usual), Job(R.job4, x_last)

    def wide(job, left, right):
        def step(n, _):
            job.put(dot(left[...], right[n]), pl.ds(pl.multiple_of(256 * n, 256), 256))
            return 0

        lax.fori_loop(0, 6, step, 0)

    wide(job_down, R.gmlpt, R.act)
    job_down.push()
    R.norm2t[...] = R.norm2[...].T
    wide(job_up, R.norm2t, R.gup)
    job_up.push()

    R.gnew[...] = jnp.zeros((ROWS, WIDTH), f32)

    def down_step(n, _):
        R.gnew[...] += dot(R.act[n], R.wdown[n])
        return 0

    lax.fori_loop(0, 6, down_step, 0)
    R.mlp[0] = R.gnew[...].astype(bf16)
    mlp_in = send(R.mlp.at[0], R.mlp.at[1], to_y)
    job_down.turn()

    for c in d_in:
        c.wait_recv()
    for j in range(2):
        both = R.dpart[j, 0].astype(f32) + R.dpart[j, 1].astype(f32)
        R.dout[j] = both.astype(bf16).reshape(3, HEAD_DIM, ROWS)
        for h in range(3):
            R.delta[h, j] = jnp.sum(R.dout[j, h].astype(f32) * R.acc[h, j], axis=0, keepdims=True)

    def back_block(r, first):
        for h in range(3):
            dk, dv = 0, 0
            for j in range(2):
                probs = jnp.exp(R.scores[h, j, r] - R.peak[h, j])
                grad = dot(R.vt[r, h], R.dout[j, h], 0, 0)
                low = (probs * (grad - R.delta[h, j])).astype(bf16)
                dv = dv + dot(R.dout[j, h], probs.astype(bf16), 1, 1)
                dk = dk + dot(R.qt[j, h], low, 1, 1)
                dq = dot(R.kt[r, h], low)
                R.dq[j, h] = dq if first else R.dq[j, h] + dq
            at = pl.ds(HEAD_DIM * h, HEAD_DIM)
            if r:
                R.dkv[r, 0, at] = dk.astype(bf16)
                R.dkv[r, 1, at] = dv.astype(bf16)
            else:
                R.own0[0, at] = dk
                R.own0[1, at] = dv

    back_block(2, True)
    kv_in = [send(R.dkv.at[2], R.dkvin.at[2], to_flip)]
    back_block(3, False)
    kv_in.append(send(R.dkv.at[3], R.dkvin.at[3], to_far))
    back_block(1, False)
    kv_in.append(send(R.dkv.at[1], R.dkvin.at[1], to_near))
    back_block(0, False)
    R.dqout[...] = (0.125 * R.dq[1].reshape(GROUP, ROWS)).astype(bf16)
    dq_in = send(R.dqout, R.dqin, to_near)
    job_up.turn()

    mlp_in.wait_recv()
    ghid_in.wait_recv()

    def block_out(rows):
        both = R.mlp[0, rows].astype(f32) + R.mlp[1, rows].astype(f32) + R.downb[...]
        value = R.hidden[rows] + both
        R.o_block[rows] = value.astype(bf16)
        R.o_next[rows] = (R.hacc[rows] + mix_last * value).astype(bf16)
        attn = R.attn[rows]
        for k, term in enumerate((value * R.cotn[rows].astype(f32), value * value, attn * attn, both * both)):
            R.small[0, 6:7, 128 * (2 + k) : 128 * (3 + k)] += 0.5 * folded(term)
        hid = R.ghid[0, rows].astype(f32) + R.ghid[1, rows].astype(f32)
        R.gblock[rows] = hid
        R.gmlp[rows] = hid.astype(bf16)
        back = R.gnorm2[rows]
        R.small[0, 2:3] += jnp.sum(back * R.unit2[rows], axis=0, keepdims=True)
        R.small[0, 3:4] += jnp.sum(back, axis=0, keepdims=True)

    row_chunks(ROWS, block_out, 32)
    for n in range(6):
        R.small[0, 8 + n // 3 : 9 + n // 3, 256 * (n % 3) : 256 * (n % 3) + 256] = R.upsum[n]
    R.gattnt[...] = R.gmlp[...].T
    mixed = jnp.concatenate([R.mix[0, (a + m) % 2] for a in range(2)], axis=0)
    job_out.put(dot(R.gattnt[...], mixed, 1, 1), slice(None))
    job_out.push()
    job_out.turn()

    for c in (*kv_in, dq_in):
        c.wait_recv()
    cosine, sine = R.cosine[...], -R.sine[...]
    for k in range(2):
        ours = R.own0[k] + R.dkvin[2, k].astype(f32)
        theirs = R.dkvin[1, k].astype(f32) + R.dkvin[3, k].astype(f32)
        if k == 0:
            ours, theirs = rotate_t(ours, cosine, sine), rotate_t(theirs, cosine, sine)
        R.lin[1 + k, m] = ours.astype(bf16)
        R.lin[1 + k, 1 - m] = theirs.astype(bf16)
    R.lin[0, m] = rotate_t(0.125 * R.dq[0].reshape(GROUP, ROWS), cosine, sine).astype(bf16)
    R.lin[0, 1 - m] = rotate_t(R.dqin[...].astype(f32), cosine, sine).astype(bf16)
    lins = [R.lin[k].reshape(LOCAL, ROWS) for k in range(3)]
    first = dot(R.wq[...], lins[0]) + dot(R.wk[...], lins[1]) + dot(R.wv[...], lins[2])
    R.gnew[...] = first.T

    def first_back(rows):
        grad = R.gnew[rows]
        R.gin[0, rows] = norm_back(grad, R.unit1[rows], R.inv1[rows], R.gain1[...]).astype(bf16)
        R.small[0, 0:1] += jnp.sum(grad * R.unit1[rows], axis=0, keepdims=True)
        R.small[0, 1:2] += jnp.sum(grad, axis=0, keepdims=True)

    row_chunks(ROWS, first_back)
    gin_in = send(R.gin.at[0], R.gin.at[1], to_y)
    small_in = send(R.small.at[0, pl.ds(0, 8)], R.smallin.at[0, pl.ds(0, 8)], to_y)
    every = jnp.concatenate(lins, axis=0)
    job_a.put(dot(R.norm1t[...], every[:640], 1, 1), slice(None))
    job_a.push()
    job_b.put(dot(R.norm1t[...], every[640:], 1, 1), slice(None))
    job_b.push()
    job_a.turn()
    job_b.turn()
    small_in.wait_recv()
    R.small[1, 0:8] = R.small[0, 0:8] + R.smallin[0, 0:8]
    R.small[1, 8:16] = R.small[0, 8:16]
    small_in = send(R.small.at[1], R.smallin.at[1], to_core)
    job_down.turn()
    job_up.turn()
    small_in.wait_recv()
    R.small[2] = R.small[1] + R.smallin[1]
    small_in = send(R.small.at[2], R.smallin.at[2], to_x)
    job_out.turn()
    small_in.wait_recv()
    R.small[3] = R.small[2] + R.smallin[2]
    small_in = [
        send(R.small.at[3], R.smallz.at[k], there) for k, there in enumerate((to_near, to_flip, to_far))
    ]
    job_down.turn()
    job_up.turn()
    job_out.turn()
    job_a.turn()
    job_b.turn()
    job_a.turn()
    job_b.turn()
    gin_in.wait_recv()

    def grad_in(rows):
        both = R.gin[0, rows].astype(f32) + R.gin[1, rows].astype(f32)
        R.o_gin[rows] = (R.gblock[rows] + both).astype(bf16)

    row_chunks(ROWS, grad_in)
    for c in small_in:
        c.wait_recv()
    R.o_small[...] = (R.small[3] + R.smallz[0]) + (R.smallz[1] + R.smallz[2])
    job_down.pull(R.o_down)
    job_up.pull(R.o_up)
    job_out.pull(R.o_out)
    job_a.pull(R.o_a)
    job_b.pull(R.o_b)
    for c in started:
        c.wait_send()


def last_kernel(make, *refs):
    R = make(refs)
    R.next[0] = R.o_next[...]
    R.block[0] = R.o_block[...]
    R.gin[0] = R.o_gin[...]

    def history_back(rows):
        cot = R.cotn[rows].astype(f32)
        for j in range(8):
            R.ghist[j, 0, rows] = (R.mixw[j] * cot).astype(bf16)

    row_chunks(ROWS, history_back)
    R.gq[...] = R.o_a[:, :LOCAL]
    R.gk[...] = jnp.concatenate([R.o_a[:, LOCAL:], R.o_b[:, :128]], axis=1)
    R.gv[...] = R.o_b[:, 128:]
    R.gup[...] = R.o_up[...]
    R.gout[...] = R.o_out[...].T
    R.gdown[...] = R.o_down[...].T
    for i, ref in enumerate((R.gain1, R.shift1, R.gain2, R.shift2, R.downb)):
        ref[...] = R.o_small[i]
    R.upb[0:WIDTH] = R.o_small[8]
    R.upb[WIDTH:HIDDEN] = R.o_small[9]
    parts = [R.o_small[5 + k // 6 : 6 + k // 6, 128 * (k % 6) : 128 * (k % 6) + 128] for k in range(12)]
    sums = jnp.sum(jnp.concatenate(parts, axis=0), axis=1, keepdims=True)
    row = jnp.broadcast_to(sums, (12, 128)).T[0:1]
    R.sums[...] = row


def out_spec(shape, dtype=f32):
    return jax.ShapeDtypeStruct(shape, dtype)


def namer(*groups):
    names = [name for group in groups for name in group]
    return lambda refs: SimpleNamespace(**dict(zip(names, refs)))


def per_device_block(
    inputs,
    history,
    window_lengths,
    block_order,
    first_gain,
    first_shift,
    query_weight,
    key_weight,
    value_weight,
    out_weight,
    second_gain,
    second_shift,
    up_weight,
    up_bias,
    down_weight,
    down_bias,
    mix_weights,
    cotangent_next,
    cotangent_block,
):
    vmem, hbm, smem = (pl.BlockSpec(memory_space=s) for s in (pltpu.VMEM, pl.ANY, pltpu.SMEM))
    args = dict(
        x=inputs[0], cotn=cotangent_next[0], cotb=cotangent_block[0],
        wq=query_weight, wk=key_weight, wv=value_weight,
        gain1=first_gain[None], shift1=first_shift[None], gain2=second_gain[None], shift2=second_shift[None],
        upb=up_bias.reshape(6, 1, 256), downb=down_bias[None],
        wout=out_weight.reshape(2, GROUP, WIDTH), history=history[:, 0], wup_h=up_weight,
        wdown_h=down_weight.reshape(6, 256, WIDTH),
        windows=window_lengths[0], order=block_order, mixw=mix_weights,
    )
    specs = [vmem] * 12 + [hbm] * 4 + [smem] * 3
    outs = dict(
        o_next=out_spec((ROWS, WIDTH), bf16), o_block=out_spec((ROWS, WIDTH), bf16), o_gin=out_spec((ROWS, WIDTH), bf16),
        o_down=out_spec((BLOCK, HIDDEN)), o_up=out_spec((BLOCK, HIDDEN)), o_out=out_spec((BLOCK, LOCAL)),
        o_a=out_spec((BLOCK, 640)), o_b=out_spec((BLOCK, 512)), o_small=out_spec((16, WIDTH)),
    )
    scratch = scratch_spec()
    tree = jax.tree.structure(scratch)
    flat, names = [], []
    for name, spec in scratch.items():
        several = isinstance(spec, list)
        names.append((name, len(spec) if several else 0))
        flat.extend(spec if several else [spec])

    def make(refs):
        R, k = dict(zip([*args, *outs], refs)), len(args) + len(outs)
        for name, count in names:
            R[name] = refs[k : k + count] if count else refs[k]
            k += max(count, 1)
        return SimpleNamespace(**R)

    held = pl.pallas_call(
        functools.partial(layer_kernel, make),
        out_shape=list(outs.values()),
        in_specs=specs,
        out_specs=[vmem] * len(outs),
        scratch_shapes=flat,
        compiler_params=pltpu.CompilerParams(
            collective_id=1, has_side_effects=True, vmem_limit_bytes=63 * 2**20
        ),
    )(*args.values())
    held = dict(zip(outs, held))
    rows3 = (1, ROWS, WIDTH)
    results = dict(
        next=out_spec(rows3, bf16), block=out_spec(rows3, bf16), gin=out_spec(rows3, bf16),
        ghist=out_spec((8, *rows3), bf16), gain1=out_spec((WIDTH,)), shift1=out_spec((WIDTH,)),
        gq=out_spec((BLOCK, LOCAL)), gk=out_spec((BLOCK, LOCAL)), gv=out_spec((BLOCK, LOCAL)),
        gout=out_spec((LOCAL, BLOCK)), gain2=out_spec((WIDTH,)), shift2=out_spec((WIDTH,)),
        gup=out_spec((BLOCK, HIDDEN)), upb=out_spec((HIDDEN,)), gdown=out_spec((HIDDEN, BLOCK)),
        downb=out_spec((WIDTH,)), sums=out_spec((1, 12)),
    )
    given = dict(cotn=cotangent_next[0], mixw=mix_weights, **held)
    done = pl.pallas_call(
        functools.partial(last_kernel, namer(given, results)),
        out_shape=list(results.values()),
        in_specs=[vmem, smem] + [vmem] * len(held),
        out_specs=[vmem] * len(results),
        compiler_params=pltpu.CompilerParams(vmem_limit_bytes=40 * 2**20),
    )(*given.values())
    sums = done[-1][0]
    entries = float(lax.axis_size("batch") * lax.axis_size("seq") * ROWS * WIDTH)
    return (*done[:-1], sums[:9], jnp.sqrt(sums[9:12] / entries))


def device_function(mesh):
    return per_device_block if mesh.shape["seq"] == 4 else per_device_general


def per_device_general(
    inputs,
    history,
    window_lengths,
    block_order,
    first_gain,
    first_shift,
    query_weight,
    key_weight,
    value_weight,
    out_weight,
    second_gain,
    second_shift,
    up_weight,
    up_bias,
    down_weight,
    down_bias,
    mix_weights,
    cotangent_next,
    cotangent_block,
):
    rows = inputs.shape[1]
    width = inputs.shape[2]
    local_width = query_weight.shape[1]
    heads = local_width // HEAD_DIM
    half = HEAD_DIM // 2
    depth = history.shape[0]
    total = rows * lax.axis_size("seq")
    size = min(1024, total)
    count = total // size
    split = (rows, heads, HEAD_DIM)
    offsets = jnp.arange(rows, dtype=jnp.int32)
    own_pos = block_order[lax.axis_index("seq")] * rows + offsets
    every_row = jnp.arange(total, dtype=jnp.int32)
    every_pos = block_order[every_row // rows] * rows + every_row % rows
    ends = jnp.cumsum(window_lengths[0])
    own_docs = jnp.sum((own_pos[:, None] >= ends[None, :]).astype(jnp.int32), axis=1)
    every_docs = jnp.sum((every_pos[:, None] >= ends[None, :]).astype(jnp.int32), axis=1)
    rates = jnp.exp(-jnp.log(10000.0) * jnp.arange(half, dtype=jnp.float32) / half)
    angles = own_pos.astype(jnp.float32)[:, None] * rates[None, :]
    cosine = jnp.cos(angles)[:, None, :]
    sine = jnp.sin(angles)[:, None, :]
    residual = inputs[0].astype(jnp.float32)
    normed_first, unit_first, scale_first = layer_parts(residual, first_gain, first_shift)
    normed_first = normed_first.astype(jnp.bfloat16)
    query_lin = jnp.dot(normed_first, query_weight, preferred_element_type=jnp.float32)
    key_lin = jnp.dot(normed_first, key_weight, preferred_element_type=jnp.float32)
    value_lin = jnp.dot(normed_first, value_weight, preferred_element_type=jnp.float32)
    queries = (rotate(query_lin.reshape(split), cosine, sine) * 0.125).astype(jnp.bfloat16)
    keys = (
        rotate(key_lin.reshape(split), cosine, sine).reshape(rows, local_width).astype(jnp.bfloat16)
    )
    values = value_lin.astype(jnp.bfloat16)
    all_keys, all_values = (
        lax.all_gather(keys, "seq", axis=0, tiled=True),
        lax.all_gather(values, "seq", axis=0, tiled=True),
    )

    def block_mask(index):
        key_pos = lax.dynamic_slice_in_dim(every_pos, index * size, size)
        key_docs = lax.dynamic_slice_in_dim(every_docs, index * size, size)
        return (key_pos[None, :] <= own_pos[:, None]) & (key_docs[None, :] == own_docs[:, None])

    def block_rows(array, index):
        return lax.dynamic_slice_in_dim(array, index * size, size).reshape(size, heads, HEAD_DIM)

    def block_scores(index, key_rows):
        return jnp.einsum(
            "qhd,khd->hqk", queries, block_rows(key_rows, index), preferred_element_type=jnp.float32
        )

    def stats_step(index, carry):
        allowed = block_mask(index)

        def update(state):
            peak, denom = state
            masked = jnp.where(allowed[None], block_scores(index, all_keys), -1e30)
            fresh = jnp.maximum(peak, jnp.max(masked, axis=-1))
            weights = jnp.where(allowed[None], jnp.exp(masked - fresh[..., None]), 0.0)
            return (fresh, denom * jnp.exp(peak - fresh) + jnp.sum(weights, axis=-1))

        return lax.cond(jnp.any(allowed), update, keep_state, carry)

    start_stats = (
        jnp.full((heads, rows), -1e30, jnp.float32),
        jnp.zeros((heads, rows), jnp.float32),
    )
    peak, denom = lax.fori_loop(0, count, stats_step, start_stats)

    def block_probs(index, allowed, key_rows):
        scores = block_scores(index, key_rows)
        return jnp.where(allowed[None], jnp.exp(scores - peak[..., None]), 0.0) / denom[..., None]

    def output_step(index, carry):
        allowed = block_mask(index)

        def output_accumulate(state):
            probs_low = block_probs(index, allowed, all_keys).astype(jnp.bfloat16)
            return state + jnp.einsum(
                "hqk,khd->qhd",
                probs_low,
                block_rows(all_values, index),
                preferred_element_type=jnp.float32,
            )

        return lax.cond(jnp.any(allowed), output_accumulate, keep_state, carry)

    running = lax.fori_loop(0, count, output_step, jnp.zeros(split, jnp.float32))
    mixed = running.reshape(rows, local_width).astype(jnp.bfloat16)
    attn_out = lax.psum(
        jnp.dot(mixed, out_weight, preferred_element_type=jnp.float32).astype(jnp.bfloat16),
        "tensor",
    ).astype(jnp.float32)
    hidden = residual + attn_out
    normed_second, unit_second, scale_second = layer_parts(hidden, second_gain, second_shift)
    normed_second = normed_second.astype(jnp.bfloat16)
    upward = jnp.dot(normed_second, up_weight, preferred_element_type=jnp.float32) + up_bias
    active_full, gelu_pull = jax.vjp(gelu_tanh, upward)
    active = active_full.astype(jnp.bfloat16)
    mlp_out = (
        lax.psum(
            jnp.dot(active, down_weight, preferred_element_type=jnp.float32).astype(jnp.bfloat16),
            "tensor",
        ).astype(jnp.float32)
        + down_bias
    )
    block_value = hidden + mlp_out
    history_low = history[:, 0]
    next_value = (
        jnp.sum(mix_weights[:depth, None, None] * history_low.astype(jnp.float32), axis=0)
        + mix_weights[depth] * block_value
    )
    cot_low = cotangent_next[0]
    cot_next = cot_low.astype(jnp.float32)
    cot_block = cotangent_block[0].astype(jnp.float32)
    grad_history = (mix_weights[:depth, None, None] * cot_next[None]).astype(jnp.bfloat16)
    mix_terms = jnp.concatenate(
        [
            jnp.einsum("jsd,sd->j", history_low, cot_low, preferred_element_type=jnp.float32),
            jnp.sum(block_value * cot_next)[None],
        ]
    )
    grad_block = cot_block + mix_weights[depth] * cot_next
    grad_mlp = grad_block.astype(jnp.bfloat16)
    grad_down = jnp.einsum("sf,sd->fd", active, grad_mlp, preferred_element_type=jnp.float32)
    grad_active = jnp.einsum("sd,fd->sf", grad_mlp, down_weight, preferred_element_type=jnp.float32)
    grad_up = gelu_pull(grad_active)[0].astype(jnp.bfloat16)
    grad_upw = jnp.einsum("sd,sf->df", normed_second, grad_up, preferred_element_type=jnp.float32)
    grad_normed_second = lax.psum(
        jnp.einsum("sf,df->sd", grad_up, up_weight, preferred_element_type=jnp.float32).astype(
            jnp.bfloat16
        ),
        "tensor",
    ).astype(jnp.float32)
    grad_hidden = grad_block + norm_backward(
        grad_normed_second, unit_second, scale_second, second_gain
    )
    grad_attn = grad_hidden.astype(jnp.bfloat16)
    grad_outw = jnp.einsum("sk,sd->kd", mixed, grad_attn, preferred_element_type=jnp.float32)
    grad_mixed = (
        jnp.einsum("sd,kd->sk", grad_attn, out_weight, preferred_element_type=jnp.float32)
        .astype(jnp.bfloat16)
        .reshape(split)
    )
    back_keys, back_values = (
        lax.all_gather(keys, "seq", axis=0, tiled=True),
        lax.all_gather(values, "seq", axis=0, tiled=True),
    )

    def delta_step(index, carry):
        allowed = block_mask(index)

        def delta_accumulate(state):
            probs = block_probs(index, allowed, back_keys)
            grad_probs = jnp.einsum(
                "qhd,khd->hqk",
                grad_mixed,
                block_rows(back_values, index),
                preferred_element_type=jnp.float32,
            )
            return state + jnp.sum(probs * grad_probs, axis=-1)

        return lax.cond(jnp.any(allowed), delta_accumulate, keep_state, carry)

    delta = lax.fori_loop(0, count, delta_step, jnp.zeros((heads, rows), jnp.float32))

    def grad_step(index, carry):
        allowed = block_mask(index)

        def grad_accumulate(state):
            grad_queries, key_buffer, value_buffer = state
            key_rows = block_rows(back_keys, index)
            value_rows = block_rows(back_values, index)
            probs = block_probs(index, allowed, back_keys)
            grad_probs = jnp.einsum(
                "qhd,khd->hqk", grad_mixed, value_rows, preferred_element_type=jnp.float32
            )
            grad_scores = (probs * (grad_probs - delta[..., None])).astype(jnp.bfloat16)
            grad_queries = grad_queries + jnp.einsum(
                "hqk,khd->qhd", grad_scores, key_rows, preferred_element_type=jnp.float32
            )
            key_part = jnp.einsum(
                "hqk,qhd->khd", grad_scores, queries, preferred_element_type=jnp.float32
            ).reshape(size, local_width)
            value_part = jnp.einsum(
                "hqk,qhd->khd",
                probs.astype(jnp.bfloat16),
                grad_mixed,
                preferred_element_type=jnp.float32,
            ).reshape(size, local_width)
            key_buffer = lax.dynamic_update_slice_in_dim(key_buffer, key_part, index * size, 0)
            value_buffer = lax.dynamic_update_slice_in_dim(
                value_buffer, value_part, index * size, 0
            )
            return (grad_queries, key_buffer, value_buffer)

        return lax.cond(jnp.any(allowed), grad_accumulate, keep_state, carry)

    start_grads = (
        jnp.zeros(split, jnp.float32),
        jnp.zeros((total, local_width), jnp.float32),
        jnp.zeros((total, local_width), jnp.float32),
    )
    grad_queries, key_buffer, value_buffer = lax.fori_loop(0, count, grad_step, start_grads)
    grad_keys, grad_values = (
        lax.psum_scatter(
            key_buffer.astype(jnp.bfloat16), "seq", scatter_dimension=0, tiled=True
        ).astype(jnp.float32),
        lax.psum_scatter(
            value_buffer.astype(jnp.bfloat16), "seq", scatter_dimension=0, tiled=True
        ).astype(jnp.float32),
    )
    grad_query_lin = (
        rotate(grad_queries * 0.125, cosine, -sine).reshape(rows, local_width).astype(jnp.bfloat16)
    )
    grad_key_lin = (
        rotate(grad_keys.reshape(split), cosine, -sine)
        .reshape(rows, local_width)
        .astype(jnp.bfloat16)
    )
    grad_value_lin = grad_values.astype(jnp.bfloat16)
    grad_queryw = jnp.einsum(
        "sd,se->de", normed_first, grad_query_lin, preferred_element_type=jnp.float32
    )
    grad_keyw = jnp.einsum(
        "sd,se->de", normed_first, grad_key_lin, preferred_element_type=jnp.float32
    )
    grad_valuew = jnp.einsum(
        "sd,se->de", normed_first, grad_value_lin, preferred_element_type=jnp.float32
    )
    local_normed = jnp.einsum(
        "se,de->sd", grad_query_lin, query_weight, preferred_element_type=jnp.float32
    )
    local_normed = local_normed + jnp.einsum(
        "se,de->sd", grad_key_lin, key_weight, preferred_element_type=jnp.float32
    )
    local_normed = local_normed + jnp.einsum(
        "se,de->sd", grad_value_lin, value_weight, preferred_element_type=jnp.float32
    )
    grad_normed_first = lax.psum(local_normed.astype(jnp.bfloat16), "tensor").astype(jnp.float32)
    grad_input = grad_hidden + norm_backward(grad_normed_first, unit_first, scale_first, first_gain)
    shared_grads = (
        lax.psum_scatter(grad_queryw, ("seq", "batch"), scatter_dimension=0, tiled=True),
        lax.psum_scatter(grad_keyw, ("seq", "batch"), scatter_dimension=0, tiled=True),
        lax.psum_scatter(grad_valuew, ("seq", "batch"), scatter_dimension=0, tiled=True),
        lax.psum_scatter(grad_outw, ("seq", "batch"), scatter_dimension=1, tiled=True),
        lax.psum_scatter(grad_upw, ("seq", "batch"), scatter_dimension=0, tiled=True),
        lax.psum_scatter(grad_down, ("seq", "batch"), scatter_dimension=1, tiled=True),
    )
    square_terms = jnp.stack(
        [
            jnp.sum(block_value * block_value),
            jnp.sum(attn_out * attn_out),
            jnp.sum(mlp_out * mlp_out),
        ]
    )
    small_terms = lax.psum(
        (
            jnp.sum(grad_normed_first * unit_first, axis=0),
            jnp.sum(grad_normed_first, axis=0),
            jnp.sum(grad_normed_second * unit_second, axis=0),
            jnp.sum(grad_normed_second, axis=0),
            jnp.sum(grad_up.astype(jnp.float32), axis=0),
            jnp.sum(grad_mlp.astype(jnp.float32), axis=0),
            mix_terms,
            square_terms,
        ),
        ("seq", "batch"),
    )
    entries = float(lax.axis_size("batch") * total * width)
    rms_values = jnp.sqrt(small_terms[7] / entries)
    return (
        next_value.astype(jnp.bfloat16)[None],
        block_value.astype(jnp.bfloat16)[None],
        grad_input.astype(jnp.bfloat16)[None],
        grad_history[:, None],
        small_terms[0],
        small_terms[1],
        shared_grads[0],
        shared_grads[1],
        shared_grads[2],
        shared_grads[3],
        small_terms[2],
        small_terms[3],
        shared_grads[4],
        small_terms[4],
        shared_grads[5],
        small_terms[5],
        small_terms[6],
        rms_values,
    )


def solution(mesh):
    in_specs = (
        P("batch", "seq", None),
        P(None, "batch", "seq", None),
        P("batch", None),
        P(),
        P(),
        P(),
        P(None, "tensor"),
        P(None, "tensor"),
        P(None, "tensor"),
        P("tensor", None),
        P(),
        P(),
        P(None, "tensor"),
        P("tensor"),
        P("tensor", None),
        P(),
        P(),
        P("batch", "seq", None),
        P("batch", "seq", None),
    )
    out_specs = (
        P("batch", "seq", None),
        P("batch", "seq", None),
        P("batch", "seq", None),
        P(None, "batch", "seq", None),
        P(),
        P(),
        P(("seq", "batch"), "tensor"),
        P(("seq", "batch"), "tensor"),
        P(("seq", "batch"), "tensor"),
        P("tensor", ("seq", "batch")),
        P(),
        P(),
        P(("seq", "batch"), "tensor"),
        P("tensor"),
        P("tensor", ("seq", "batch")),
        P(),
        P(),
        P(),
    )
    return jax.shard_map(
        device_function(mesh), mesh=mesh, in_specs=in_specs, out_specs=out_specs, check_vma=False
    )
```

```python
import functools
from types import SimpleNamespace

import jax
import jax.numpy as jnp
from jax import lax
from jax.experimental import pallas as pl
from jax.experimental.pallas import tpu as pltpu
from jax.sharding import PartitionSpec as P

HEAD_DIM = 64
f32, bf16, i32 = jnp.float32, jnp.bfloat16, jnp.int32
MESH = pl.DeviceIdType.MESH


epsilon = 1e-05


def layer_parts(values, gain, shift):
    centre = jnp.mean(values, axis=-1, keepdims=True)
    centred = values - centre
    spread = jnp.mean(centred * centred, axis=-1, keepdims=True)
    inverse = lax.rsqrt(spread + epsilon)
    unit = centred * inverse
    return (unit * gain + shift, unit, inverse)


def norm_backward(grad_out, unit, inverse, gain):
    scaled = grad_out * gain
    return inverse * (
        scaled
        - jnp.mean(scaled, axis=-1, keepdims=True)
        - unit * jnp.mean(scaled * unit, axis=-1, keepdims=True)
    )


def gelu_tanh(values):
    return (
        0.5
        * values
        * (1.0 + jnp.tanh(0.7978845608028654 * (values + 0.044715 * values * values * values)))
    )


def rotate(values, cosine, sine):
    half = values.shape[-1] // 2
    first = values[..., :half]
    second = values[..., half:]
    return jnp.concatenate(
        [first * cosine - second * sine, second * cosine + first * sine], axis=-1
    )


def keep_state(state):
    return state


def dot(a, b, ca=1, cb=0):
    return lax.dot_general(a, b, (((ca,), (cb,)), ((), ())), preferred_element_type=f32)


def rope_tables(pos, half):
    index = lax.broadcasted_iota(i32, (half, 1), 0).astype(f32)
    rates = jnp.exp(-jnp.log(f32(10000.0)) * index / half)
    angles = rates * pos
    return jnp.cos(angles), jnp.sin(angles)


def rotate_t(lin, cosine, sine):
    width, rows = lin.shape
    parts = lin.reshape(width // HEAD_DIM, 2, HEAD_DIM // 2, rows)
    first, second = parts[:, 0], parts[:, 1]
    turned = [first * cosine - second * sine, second * cosine + first * sine]
    return jnp.stack(turned, axis=1).reshape(width, rows)


def gelu_both(u):
    square = u * u
    t = jnp.tanh(0.7978845608028654 * (u + 0.044715 * square * u))
    half = 0.5 * (1.0 + t)
    slope = half + 0.5 * u * (1.0 - t * t) * (0.7978845608028654 * (1.0 + 3 * 0.044715 * square))
    return u * half, slope


def row_chunks(rows, body, size=64):
    def step(i, _):
        body(pl.ds(pl.multiple_of(i * size, size), size))
        return 0

    lax.fori_loop(0, rows // size, step, 0)


def folded(rows):
    total = jnp.sum(rows, axis=0, keepdims=True)
    return sum(total[:, k : k + 128] for k in range(0, total.shape[1], 128))


ROWS, WIDTH, LOCAL, GROUP, HIDDEN, BLOCK = 256, 768, 384, 192, 1536, 48


def scratch_spec():
    vm = pltpu.VMEM
    heads = (3, HEAD_DIM, ROWS)
    full32, full16, turned = vm((ROWS, WIDTH), f32), vm((ROWS, WIDTH), bf16), vm((WIDTH, ROWS), bf16)

    def job(columns):
        return [
            vm((2, 2, 2, 2, BLOCK, columns), bf16), vm((2, 2, 2, BLOCK, columns), bf16),
            vm((2, 2, BLOCK, columns), bf16), vm((2, BLOCK, columns), bf16), vm((BLOCK, columns), bf16),
        ]

    return dict(
        cotn=full16, cotb=full16, wq=vm((WIDTH, LOCAL), bf16), wk=vm((WIDTH, LOCAL), bf16), wv=vm((WIDTH, LOCAL), bf16),
        hist=vm((8, ROWS, WIDTH), bf16), wup=vm((WIDTH, HIDDEN), bf16), wdown=vm((HIDDEN, WIDTH), bf16),
        wof=vm((2, 2, 3, HEAD_DIM, WIDTH), bf16),
        vectors=vm((5, 1, WIDTH), f32), upb=vm((1, HIDDEN), f32), upsum=vm((1, HIDDEN), f32),
        qown=vm((2, *heads), bf16), kvown=vm((2, 3, 2, HEAD_DIM, ROWS), bf16),
        qt=vm((2, *heads), bf16), kv=vm((4, 3, 2, HEAD_DIM, ROWS), bf16),
        scores=vm((3, 2, 4, ROWS, ROWS), f32), bias=vm((2, 4, ROWS, ROWS), f32),
        peak=vm((3, 2, 1, ROWS), f32), denom=vm((3, 2, 1, ROWS), f32), acc=vm((3, 2, HEAD_DIM, ROWS), f32),
        delta=vm((3, 2, 1, ROWS), f32), cosine=vm((32, ROWS), f32), sine=vm((32, ROWS), f32),
        mix=vm((2, 2, *heads), bf16), mixout=vm(heads, bf16),
        unit1=full32, inv1=vm((ROWS, 1), f32), norm1=full16, norm1t=turned,
        hidden=full32, attn=full32, unit2=full32, inv2=vm((ROWS, 1), f32), norm2=full16, norm2t=turned,
        gblock=full32, gmlp=full16, gmlpt=turned, hacc=full32, gact=vm((ROWS, HIDDEN), f32),
        act=vm((ROWS, HIDDEN), bf16), gup=vm((ROWS, HIDDEN), bf16), gnorm2=full32, gnew=full32,
        ghid=vm((2, ROWS, WIDTH), bf16), mlp=vm((2, ROWS, WIDTH), bf16), gin=vm((2, ROWS, WIDTH), bf16),
        dpart=vm((2, 2, *heads), bf16), dsend=vm((2, 2, *heads), bf16), dout=vm((2, *heads), bf16),
        dkv=vm((4, 3, 2, HEAD_DIM, ROWS), bf16), dkvin=vm((4, 3, 2, HEAD_DIM, ROWS), bf16),
        dq=vm((3, HEAD_DIM, ROWS), f32), dqout=vm(heads, bf16), dqin=vm(heads, bf16),
        own0=vm((3, 2, HEAD_DIM, ROWS), f32), lin=vm((3, 2, *heads), bf16), gattnt=turned,
        small=vm((5, 16, WIDTH), f32), smallin=vm((3, 16, WIDTH), f32), smallz=vm((3, 16, WIDTH), f32),
        job0=job(HIDDEN), job1=job(HIDDEN), job2=job(LOCAL), job3=job(640), job4=job(512),
        ssem=pltpu.SemaphoreType.DMA((96,)), rsem=pltpu.SemaphoreType.DMA((96,)), lsem=pltpu.SemaphoreType.DMA((16,)),
    )


def layer_kernel(make, *refs):
    R = make(refs)
    z, b, y = lax.axis_index("seq"), lax.axis_index("batch"), lax.axis_index("tensor")
    near, flip, far = z + 1 - 2 * (z % 2), (z + 2) % 4, 3 - z
    m, p, xbit, core = z % 2, z // 2, b // 2, b % 2
    to_near, to_flip, to_far = dict(seq=near), dict(seq=flip), dict(seq=far)
    to_y, to_diag = dict(tensor=1 - y), dict(seq=near, tensor=1 - y)
    to_x, to_core = dict(batch=(b + 2) % 4), dict(batch=b + 1 - 2 * core)
    barrier = pltpu.get_barrier_semaphore()
    everyone = [to_near, to_flip, to_far, to_y, to_diag, to_x, to_core]
    for there in everyone:
        pl.semaphore_signal(barrier, inc=1, device_id=there, device_id_type=MESH)
    started = []

    def send(src, dst, there):
        i = len(started)
        copy = pltpu.make_async_remote_copy(
            src, dst, R.ssem.at[i], R.rsem.at[i], device_id=there, device_id_type=MESH
        )
        copy.start()
        started.append(copy)
        return copy

    def fetch(src, dst, i):
        copy = pltpu.make_async_copy(src, dst, R.lsem.at[i])
        copy.start()
        return copy

    get_q = fetch(R.wq_h, R.wq, 0)
    get_k = fetch(R.wk_h, R.wk, 1)
    get_v = fetch(R.wv_h, R.wv, 2)
    get_cot = [fetch(R.cotn_h, R.cotn, 3), fetch(R.cotb_h, R.cotb, 4)]
    get_out = fetch(R.wout, R.wof.at[0], 5)
    get_hist = fetch(R.history, R.hist, 6)
    get_down = fetch(R.wdown_h, R.wdown, 7)
    get_up = fetch(R.wup_h, R.wup, 8)
    ends, total = [], 0
    for i in range(R.windows.shape[0]):
        total = total + R.windows[i]
        ends.append(total)
    for i, ref in enumerate((R.gain1_in, R.shift1_in, R.gain2_in, R.shift2_in, R.downb_in)):
        R.vectors[i] = ref[...][None]
    R.upb[...] = R.upb_in[...][None]
    R.gain1, R.shift1, R.gain2, R.shift2, R.downb = (R.vectors.at[i] for i in range(5))
    base = [R.order[k] * ROWS for k in (z, near, flip, far)]
    lane = lax.broadcasted_iota(i32, (1, ROWS), 1)

    def norm_first(rows):
        x = R.x[rows].astype(f32)
        centred = x - jnp.mean(x, axis=-1, keepdims=True)
        inverse = lax.rsqrt(jnp.mean(centred * centred, axis=-1, keepdims=True) + epsilon)
        unit = centred * inverse
        R.unit1[rows] = unit
        R.inv1[rows] = inverse
        R.norm1[rows] = (unit * R.gain1[...] + R.shift1[...]).astype(bf16)

    row_chunks(ROWS, norm_first)
    cosine, sine = rope_tables((base[0] + lane).astype(f32), HEAD_DIM // 2)
    R.cosine[...] = cosine
    R.sine[...] = sine
    split = (2, 3, HEAD_DIM, ROWS)
    get_k.wait()
    R.kvown[:, :, 0] = rotate_t(dot(R.norm1[...], R.wk[...]).T, cosine, sine).astype(bf16).reshape(split)
    get_v.wait()
    R.kvown[:, :, 1] = dot(R.norm1[...], R.wv[...]).T.astype(bf16).reshape(split)
    pl.semaphore_wait(barrier, len(everyone))
    near_in, flip_in, far_in = [], [], []

    def kv_out(h):
        near_in.append(send(R.kvown.at[1 - m, h], R.kv.at[1, h], to_near))
        flip_in.append(send(R.kvown.at[m, h], R.kv.at[2, h], to_flip))
        far_in.append(send(R.kvown.at[1 - m, h], R.kv.at[3, h], to_far))

    kv_out(0)
    get_q.wait()
    queries = rotate_t(dot(R.norm1[...], R.wq[...]).T, cosine, sine) * 0.125
    R.qown[...] = queries.astype(bf16).reshape(split)
    q_in = [send(R.qown.at[1 - m, h], R.qt.at[1, h], to_near) for h in range(1)]
    kv_out(1)
    q_in.append(send(R.qown.at[1 - m, 1], R.qt.at[1, 1], to_near))
    kv_out(2)
    q_in.append(send(R.qown.at[1 - m, 2], R.qt.at[1, 2], to_near))
    get_out.wait()
    out_in = send(R.wof.at[0], R.wof.at[1], to_y)
    R.qt[0] = R.qown[m]
    R.kv[0] = R.kvown[m]

    for j in range(2):
        qpos = base[j] + lane
        start = 0 * qpos
        for end in ends:
            start = jnp.maximum(start, jnp.where(qpos >= end, end, 0))
        for r in range(4):
            kpos = base[r] + lax.broadcasted_iota(i32, (ROWS, ROWS), 0)
            R.bias[j, r] = jnp.where((kpos <= qpos) & (kpos >= start), 0.0, -1e30).astype(f32)
    for c in get_cot:
        c.wait()
    R.small[0] = jnp.zeros((16, WIDTH), f32)
    mix_last = R.mixw[8]

    def block_grads(rows):
        g = R.cotb[rows].astype(f32) + mix_last * R.cotn[rows].astype(f32)
        R.gblock[rows] = g
        low = g.astype(bf16)
        R.gmlp[rows] = low
        R.small[0, 4:5] += 0.5 * jnp.sum(low.astype(f32), axis=0, keepdims=True)

    row_chunks(ROWS, block_grads)
    R.gmlpt[...] = R.gmlp[...].T
    R.norm1t[...] = R.norm1[...].T
    get_hist.wait()

    def history_sum(rows):
        cot = R.cotn[rows].astype(f32)
        total = 0
        for j in range(8):
            h = R.hist[j, rows].astype(f32)
            total = total + R.mixw[j] * h
            R.small[0, 5 + j // 6 : 6 + j // 6, 128 * (j % 6) : 128 * (j % 6) + 128] += 0.5 * folded(h * cot)
        R.hacc[rows] = total

    row_chunks(ROWS, history_sum, 32)
    get_down.wait()

    def active_grad(n, _):
        at = pl.ds(pl.multiple_of(256 * n, 256), 256)
        R.gact[:, at] = dot(R.gmlp[...], R.wdown[at], 1, 1)
        return 0

    lax.fori_loop(0, 6, active_grad, 0)

    def tile(h, j, r, first=False):
        s = dot(R.kv[r, h, 0], R.qt[j, h], 0, 0) + R.bias[j, r]
        R.scores[h, j, r] = s
        top = jnp.max(s, axis=0, keepdims=True)
        if first:
            e = jnp.exp(s - top)
            R.denom[h, j] = jnp.sum(e, axis=0, keepdims=True)
            R.acc[h, j] = dot(R.kv[r, h, 1], e.astype(bf16))
        else:
            old = R.peak[h, j]
            top = jnp.maximum(top, old)
            e = jnp.exp(s - top)
            alpha = jnp.exp(old - top)
            R.denom[h, j] = R.denom[h, j] * alpha + jnp.sum(e, axis=0, keepdims=True)
            R.acc[h, j] = R.acc[h, j] * alpha + dot(R.kv[r, h, 1], e.astype(bf16))
        R.peak[h, j] = top

    def finish(h, j):
        R.acc[h, j] = R.acc[h, j] * (1.0 / R.denom[h, j])
        R.peak[h, j] = R.peak[h, j] + jnp.log(R.denom[h, j])
        return R.acc[h, j].astype(bf16)

    mix_in = []
    for h in range(3):
        tile(h, 0, 0, True)
    for h in range(3):
        near_in[h].wait_recv()
        q_in[h].wait_recv()
        tile(h, 0, 1)
        tile(h, 1, 1, True)
        tile(h, 1, 0)
        flip_in[h].wait_recv()
        tile(h, 1, 2)
        tile(h, 0, 2)
        far_in[h].wait_recv()
        tile(h, 1, 3)
        tile(h, 0, 3)
        R.mixout[h] = finish(h, 1)
        R.mix[0, 0, h] = finish(h, 0)
        mix_in.append(send(R.mixout.at[h], R.mix.at[1, 1, h], to_diag))
        mix_in.append(send(R.mix.at[0, 0, h], R.mix.at[1, 0, h], to_y))
        mix_in.append(send(R.mixout.at[h], R.mix.at[0, 1, h], to_near))
    get_up.wait()
    out_in.wait_recv()
    for c in mix_in:
        c.wait_recv()
    group = (GROUP, ROWS)
    out = 0
    for t in range(2):
        for a in range(2):
            side = R.mix[(t + y) % 2, (a + m) % 2].reshape(group)
            out = out + dot(side, R.wof[(t + y) % 2, a].reshape(GROUP, WIDTH), 0, 0)
    R.attn[...] = out

    def norm_second(rows):
        hidden = R.x[rows].astype(f32) + R.attn[rows]
        R.hidden[rows] = hidden
        centred = hidden - jnp.mean(hidden, axis=-1, keepdims=True)
        inverse = lax.rsqrt(jnp.mean(centred * centred, axis=-1, keepdims=True) + epsilon)
        unit = centred * inverse
        R.unit2[rows] = unit
        R.inv2[rows] = inverse
        R.norm2[rows] = (unit * R.gain2[...] + R.shift2[...]).astype(bf16)

    row_chunks(ROWS, norm_second)
    for n in range(6):
        at = slice(256 * n, 256 * n + 256)
        u = dot(R.norm2[...], R.wup[:, at]) + R.upb[:, at]
        active, slope = gelu_both(u)
        R.act[:, at] = active.astype(bf16)
        grad = (R.gact[:, at] * slope).astype(bf16)
        R.gup[:, at] = grad
        R.upsum[:, at] = jnp.sum(grad.astype(f32), axis=0, keepdims=True)
        if n == 2:
            R.gnorm2[...] = dot(R.gup[:, :WIDTH], R.wup[:, :WIDTH], 1, 1)
    R.gnorm2[...] += dot(R.gup[:, WIDTH:], R.wup[:, WIDTH:], 1, 1)

    def norm_back(grad, unit, inverse, gain):
        scaled = grad * gain
        return inverse * (
            scaled
            - jnp.mean(scaled, axis=-1, keepdims=True)
            - unit * jnp.mean(scaled * unit, axis=-1, keepdims=True)
        )

    def second_back(rows):
        back = norm_back(R.gnorm2[rows], R.unit2[rows], R.inv2[rows], R.gain2[...])
        R.ghid[0, rows] = (0.5 * R.gblock[rows] + back).astype(bf16)

    row_chunks(ROWS, second_back)
    d_in = []
    order = [(1, 1), (1, 0), (0, 1), (0, 0)]
    for h in range(3):
        weights = jnp.concatenate([R.wof[t, (a + m) % 2, h] for t, a in order], axis=0)
        parts = dot(weights, R.ghid[0], 1, 1).astype(bf16).reshape(4, HEAD_DIM, ROWS)
        for k in range(3):
            R.dsend[(*order[k], h)] = parts[k]
        R.dpart[0, 0, h] = parts[3]
        d_in.append(
            [
                send(R.dsend.at[1, 1, h], R.dpart.at[1, 1, h], to_diag),
                send(R.dsend.at[1, 0, h], R.dpart.at[0, 1, h], to_y),
                send(R.dsend.at[0, 1, h], R.dpart.at[1, 0, h], to_near),
            ]
        )
    ghid_in = send(R.ghid.at[0], R.ghid.at[1], to_y)

    bits = dict(core=core, x=xbit, near=m, flip=p)
    where = dict(core=to_core, x=to_x, near=to_near, flip=to_flip)
    place = dict(core=0, x=1, near=2, flip=3)

    class Job:
        def __init__(self, bufs, route):
            self.grads, self.landing, self.route, self.copy, self.step = bufs[0], bufs[1:], route, None, 0

        def put(self, value, columns):
            for k in range(16):
                at = tuple((k >> place[axis]) & 1 for axis in self.route)
                self.grads[(*at, slice(None), columns)] = value[BLOCK * k : BLOCK * k + BLOCK].astype(bf16)

        def mine(self):
            return tuple(bits[axis] for axis in self.route[: self.step])

        def push(self):
            axis = self.route[self.step]
            self.copy = send(self.grads.at[(*self.mine(), 1 - bits[axis])], self.landing[self.step], where[axis])

        def pull(self, out=None):
            self.copy.wait_recv()
            landing = self.landing[self.step]
            self.step += 1
            kept = self.mine()
            left = 4 - self.step

            def add(i, _):
                at = tuple((i // 2**k) % 2 for k in range(left))
                mine, theirs = self.grads[(*kept, *at)], landing[at if at else Ellipsis]
                if out is None:
                    self.grads[(*kept, *at)] = mine + theirs
                else:
                    out[...] = mine.astype(f32) + theirs.astype(f32)
                return 0

            if left:
                lax.fori_loop(0, 2**left, add, 0)
            else:
                add(0, 0)

        def turn(self):
            self.pull()
            self.push()

    usual = tuple(place)
    job_down, job_up = Job(R.job0, usual), Job(R.job1, usual)
    job_out, job_a, job_b = Job(R.job2, usual), Job(R.job3, usual), Job(R.job4, usual)

    def wide(job, left, right):
        def step(n, _):
            at = pl.ds(pl.multiple_of(256 * n, 256), 256)
            job.put(dot(left[...], right[:, at]), at)
            return 0

        lax.fori_loop(0, 6, step, 0)

    wide(job_down, R.gmlpt, R.act)
    job_down.push()

    kv_in, dq_in = [], []

    def back_head(h):
        for c in d_in[h]:
            c.wait_recv()
        for j in range(2):
            both = R.dpart[j, 0, h].astype(f32) + R.dpart[j, 1, h].astype(f32)
            R.dout[j, h] = both.astype(bf16)
            R.delta[h, j] = jnp.sum(R.dout[j, h].astype(f32) * R.acc[h, j], axis=0, keepdims=True)
        total = [0, 0]
        for r in (2, 3, 1, 0):
            dk, dv = 0, 0
            for j in range(2):
                probs = jnp.exp(R.scores[h, j, r] - R.peak[h, j])
                grad = dot(R.kv[r, h, 1], R.dout[j, h], 0, 0)
                low = (probs * (grad - R.delta[h, j])).astype(bf16)
                dv = dv + dot(R.dout[j, h], probs.astype(bf16), 1, 1)
                dk = dk + dot(R.qt[j, h], low, 1, 1)
                total[j] = total[j] + dot(R.kv[r, h, 0], low)
            if r:
                R.dkv[r, h, 0] = dk.astype(bf16)
                R.dkv[r, h, 1] = dv.astype(bf16)
                kv_in.append(send(R.dkv.at[r, h], R.dkvin.at[r, h], (to_near, to_flip, to_far)[r - 1]))
            else:
                R.own0[h, 0] = dk
                R.own0[h, 1] = dv
        R.dqout[h] = (0.125 * total[1]).astype(bf16)
        dq_in.append(send(R.dqout.at[h], R.dqin.at[h], to_near))
        R.dq[h] = 0.125 * total[0]

    back_head(0)
    job_down.turn()
    back_head(1)
    back_head(2)
    R.norm2t[...] = R.norm2[...].T
    wide(job_up, R.norm2t, R.gup)
    job_up.push()
    R.mlp[0] = dot(R.act[...], R.wdown[...]).astype(bf16)
    mlp_in = send(R.mlp.at[0], R.mlp.at[1], to_y)
    job_up.turn()

    ghid_in.wait_recv()

    def whole_hidden(rows):
        hid = R.ghid[0, rows].astype(f32) + R.ghid[1, rows].astype(f32)
        R.gblock[rows] = hid
        R.gmlp[rows] = hid.astype(bf16)
        back = R.gnorm2[rows]
        R.small[0, 2:3] += jnp.sum(back * R.unit2[rows], axis=0, keepdims=True)
        R.small[0, 3:4] += jnp.sum(back, axis=0, keepdims=True)

    row_chunks(ROWS, whole_hidden)
    R.gattnt[...] = R.gmlp[...].T
    mixed = jnp.concatenate([R.mix[0, (a + m) % 2].reshape(group) for a in range(2)], axis=0)
    job_out.put(dot(R.gattnt[...], mixed, 1, 1), slice(None))
    job_out.push()
    job_out.turn()
    job_down.turn()

    mlp_in.wait_recv()

    def block_out(rows):
        both = R.mlp[0, rows].astype(f32) + R.mlp[1, rows].astype(f32) + R.downb[...]
        value = R.hidden[rows] + both
        R.o_block[rows] = value.astype(bf16)
        R.o_next[rows] = (R.hacc[rows] + mix_last * value).astype(bf16)
        attn = R.attn[rows]
        for k, term in enumerate((value * R.cotn[rows].astype(f32), value * value, attn * attn, both * both)):
            R.small[0, 6:7, 128 * (2 + k) : 128 * (3 + k)] += 0.5 * folded(term)

    row_chunks(ROWS, block_out, 32)
    R.small[0, 8:9] = R.upsum[:, :WIDTH]
    R.small[0, 9:10] = R.upsum[:, WIDTH:]

    cosine, sine = R.cosine[...], -R.sine[...]
    for h in range(3):
        for c in (*kv_in[3 * h : 3 * h + 3], dq_in[h]):
            c.wait_recv()
        for k in range(2):
            ours = R.own0[h, k] + R.dkvin[2, h, k].astype(f32)
            theirs = R.dkvin[1, h, k].astype(f32) + R.dkvin[3, h, k].astype(f32)
            if k == 0:
                ours, theirs = rotate_t(ours, cosine, sine), rotate_t(theirs, cosine, sine)
            R.lin[1 + k, m, h] = ours.astype(bf16)
            R.lin[1 + k, 1 - m, h] = theirs.astype(bf16)
        R.lin[0, m, h] = rotate_t(R.dq[h], cosine, sine).astype(bf16)
        R.lin[0, 1 - m, h] = rotate_t(R.dqin[h].astype(f32), cosine, sine).astype(bf16)
    lins = [R.lin[k].reshape(LOCAL, ROWS) for k in range(3)]
    first = dot(R.wq[...], lins[0]) + dot(R.wk[...], lins[1]) + dot(R.wv[...], lins[2])
    R.gnew[...] = first.T

    def first_back(rows):
        grad = R.gnew[rows]
        R.gin[0, rows] = norm_back(grad, R.unit1[rows], R.inv1[rows], R.gain1[...]).astype(bf16)
        R.small[0, 0:1] += jnp.sum(grad * R.unit1[rows], axis=0, keepdims=True)
        R.small[0, 1:2] += jnp.sum(grad, axis=0, keepdims=True)

    row_chunks(ROWS, first_back)
    small_in = send(R.small.at[0, pl.ds(0, 8)], R.smallin.at[0, pl.ds(0, 8)], to_y)
    gin_in = send(R.gin.at[0], R.gin.at[1], to_y)
    every = jnp.concatenate(lins, axis=0)
    job_a.put(dot(R.norm1t[...], every[:640], 1, 1), slice(None))
    job_a.push()
    job_b.put(dot(R.norm1t[...], every[640:], 1, 1), slice(None))
    job_b.push()
    small_in.wait_recv()
    R.small[1, 0:8] = R.small[0, 0:8] + R.smallin[0, 0:8]
    R.small[1, 8:16] = R.small[0, 8:16]
    small_in = send(R.small.at[1], R.smallin.at[1], to_core)
    job_down.turn()
    job_up.turn()
    small_in.wait_recv()
    R.small[2] = R.small[1] + R.smallin[1]
    small_in = send(R.small.at[2], R.smallin.at[2], to_x)
    job_a.turn()
    job_b.turn()
    job_out.turn()
    small_in.wait_recv()
    R.small[3] = R.small[2] + R.smallin[2]
    small_in = [
        send(R.small.at[3], R.smallz.at[k], there) for k, there in enumerate((to_near, to_flip, to_far))
    ]
    job_up.turn()
    job_out.turn()
    job_down.pull(R.o_down)
    job_a.turn()
    job_b.turn()
    gin_in.wait_recv()

    def grad_in(rows):
        both = R.gin[0, rows].astype(f32) + R.gin[1, rows].astype(f32)
        R.o_gin[rows] = (R.gblock[rows] + both).astype(bf16)

    row_chunks(ROWS, grad_in)
    job_a.turn()
    job_b.turn()
    for c in small_in:
        c.wait_recv()
    R.o_small[...] = (R.small[3] + R.smallz[0]) + (R.smallz[1] + R.smallz[2])
    job_up.pull(R.o_up)
    job_out.pull(R.o_out)
    job_a.pull(R.o_a)
    job_b.pull(R.o_b)
    for c in started:
        c.wait_send()


def last_kernel(make, entries, *refs):
    R = make(refs)
    R.next[0] = R.o_next[...]
    R.block[0] = R.o_block[...]
    R.gin[0] = R.o_gin[...]

    def history_back(rows):
        cot = R.cotn[rows].astype(f32)
        for j in range(8):
            R.ghist[j, 0, rows] = (R.mixw[j] * cot).astype(bf16)

    row_chunks(ROWS, history_back)
    R.gq[...] = R.o_a[:, :LOCAL]
    R.gk[...] = jnp.concatenate([R.o_a[:, LOCAL:], R.o_b[:, :128]], axis=1)
    R.gv[...] = R.o_b[:, 128:]
    R.gup[...] = R.o_up[...]
    R.gout[...] = R.o_out[...]
    R.gdown[...] = R.o_down[...]
    for i, ref in enumerate((R.gain1, R.shift1, R.gain2, R.shift2, R.downb)):
        ref[...] = R.o_small[i]
    R.upb[0:WIDTH] = R.o_small[8]
    R.upb[WIDTH:HIDDEN] = R.o_small[9]
    parts = [R.o_small[5 + k // 6 : 6 + k // 6, 128 * (k % 6) : 128 * (k % 6) + 128] for k in range(12)]
    sums = jnp.sum(jnp.concatenate(parts, axis=0), axis=1, keepdims=True)
    row = jnp.broadcast_to(sums, (12, 128)).T[0:1]
    R.gmix[...] = row[0, :9]
    R.rms[...] = jnp.sqrt(row / entries)[0, 9:]


def out_spec(shape, dtype=f32):
    return jax.ShapeDtypeStruct(shape, dtype)


def namer(*groups):
    names = [name for group in groups for name in group]
    return lambda refs: SimpleNamespace(**dict(zip(names, refs)))


def per_device_block(
    inputs,
    history,
    window_lengths,
    block_order,
    first_gain,
    first_shift,
    query_weight,
    key_weight,
    value_weight,
    out_weight,
    second_gain,
    second_shift,
    up_weight,
    up_bias,
    down_weight,
    down_bias,
    mix_weights,
    cotangent_next,
    cotangent_block,
):
    vmem, hbm, smem = (pl.BlockSpec(memory_space=s) for s in (pltpu.VMEM, pl.ANY, pltpu.SMEM))
    args = dict(
        x=inputs[0], gain1_in=first_gain, shift1_in=first_shift, gain2_in=second_gain, shift2_in=second_shift,
        upb_in=up_bias, downb_in=down_bias,
        cotn_h=cotangent_next[0], cotb_h=cotangent_block[0], wq_h=query_weight, wk_h=key_weight, wv_h=value_weight,
        wout=out_weight.reshape(2, 3, HEAD_DIM, WIDTH), history=history[:, 0], wup_h=up_weight, wdown_h=down_weight,
        windows=window_lengths[0], order=block_order, mixw=mix_weights,
    )
    specs = [vmem] * 7 + [hbm] * 9 + [smem] * 3
    outs = dict(
        o_next=out_spec((ROWS, WIDTH), bf16), o_block=out_spec((ROWS, WIDTH), bf16), o_gin=out_spec((ROWS, WIDTH), bf16),
        o_down=out_spec((BLOCK, HIDDEN)), o_up=out_spec((BLOCK, HIDDEN)), o_out=out_spec((BLOCK, LOCAL)),
        o_a=out_spec((BLOCK, 640)), o_b=out_spec((BLOCK, 512)), o_small=out_spec((16, WIDTH)),
    )
    scratch = scratch_spec()
    flat, names = [], []
    for name, spec in scratch.items():
        several = isinstance(spec, list)
        names.append((name, len(spec) if several else 0))
        flat.extend(spec if several else [spec])

    def make(refs):
        R, k = dict(zip([*args, *outs], refs)), len(args) + len(outs)
        for name, count in names:
            R[name] = refs[k : k + count] if count else refs[k]
            k += max(count, 1)
        return SimpleNamespace(**R)

    held = pl.pallas_call(
        functools.partial(layer_kernel, make),
        out_shape=list(outs.values()),
        in_specs=specs,
        out_specs=[vmem] * len(outs),
        scratch_shapes=flat,
        compiler_params=pltpu.CompilerParams(
            collective_id=1, has_side_effects=True, vmem_limit_bytes=63 * 2**20
        ),
    )(*args.values())
    held = dict(zip(outs, held))
    rows3 = (1, ROWS, WIDTH)
    results = dict(
        next=out_spec(rows3, bf16), block=out_spec(rows3, bf16), gin=out_spec(rows3, bf16),
        ghist=out_spec((8, *rows3), bf16), gain1=out_spec((WIDTH,)), shift1=out_spec((WIDTH,)),
        gq=out_spec((BLOCK, LOCAL)), gk=out_spec((BLOCK, LOCAL)), gv=out_spec((BLOCK, LOCAL)),
        gout=out_spec((BLOCK, LOCAL)), gain2=out_spec((WIDTH,)), shift2=out_spec((WIDTH,)),
        gup=out_spec((BLOCK, HIDDEN)), upb=out_spec((HIDDEN,)), gdown=out_spec((BLOCK, HIDDEN)),
        downb=out_spec((WIDTH,)), gmix=out_spec((9,)), rms=out_spec((3,)),
    )
    entries = float(lax.axis_size("batch") * lax.axis_size("seq") * ROWS * WIDTH)
    given = dict(cotn=cotangent_next[0], mixw=mix_weights, **held)
    done = pl.pallas_call(
        functools.partial(last_kernel, namer(given, results), entries),
        out_shape=list(results.values()),
        in_specs=[vmem, smem] + [vmem] * len(held),
        out_specs=[vmem] * len(results),
        compiler_params=pltpu.CompilerParams(vmem_limit_bytes=63 * 2**20),
    )(*given.values())
    done = dict(zip(results, done))
    turned = dict(gout=done[list(results)[9]].T, gdown=done[list(results)[14]].T)
    return tuple((done | turned).values())


def device_function(mesh):
    return per_device_block if mesh.shape["seq"] == 4 else per_device_general


def per_device_general(
    inputs,
    history,
    window_lengths,
    block_order,
    first_gain,
    first_shift,
    query_weight,
    key_weight,
    value_weight,
    out_weight,
    second_gain,
    second_shift,
    up_weight,
    up_bias,
    down_weight,
    down_bias,
    mix_weights,
    cotangent_next,
    cotangent_block,
):
    rows = inputs.shape[1]
    width = inputs.shape[2]
    local_width = query_weight.shape[1]
    heads = local_width // HEAD_DIM
    half = HEAD_DIM // 2
    depth = history.shape[0]
    total = rows * lax.axis_size("seq")
    size = min(1024, total)
    count = total // size
    split = (rows, heads, HEAD_DIM)
    offsets = jnp.arange(rows, dtype=jnp.int32)
    own_pos = block_order[lax.axis_index("seq")] * rows + offsets
    every_row = jnp.arange(total, dtype=jnp.int32)
    every_pos = block_order[every_row // rows] * rows + every_row % rows
    ends = jnp.cumsum(window_lengths[0])
    own_docs = jnp.sum((own_pos[:, None] >= ends[None, :]).astype(jnp.int32), axis=1)
    every_docs = jnp.sum((every_pos[:, None] >= ends[None, :]).astype(jnp.int32), axis=1)
    rates = jnp.exp(-jnp.log(10000.0) * jnp.arange(half, dtype=jnp.float32) / half)
    angles = own_pos.astype(jnp.float32)[:, None] * rates[None, :]
    cosine = jnp.cos(angles)[:, None, :]
    sine = jnp.sin(angles)[:, None, :]
    residual = inputs[0].astype(jnp.float32)
    normed_first, unit_first, scale_first = layer_parts(residual, first_gain, first_shift)
    normed_first = normed_first.astype(jnp.bfloat16)
    query_lin = jnp.dot(normed_first, query_weight, preferred_element_type=jnp.float32)
    key_lin = jnp.dot(normed_first, key_weight, preferred_element_type=jnp.float32)
    value_lin = jnp.dot(normed_first, value_weight, preferred_element_type=jnp.float32)
    queries = (rotate(query_lin.reshape(split), cosine, sine) * 0.125).astype(jnp.bfloat16)
    keys = (
        rotate(key_lin.reshape(split), cosine, sine).reshape(rows, local_width).astype(jnp.bfloat16)
    )
    values = value_lin.astype(jnp.bfloat16)
    all_keys, all_values = (
        lax.all_gather(keys, "seq", axis=0, tiled=True),
        lax.all_gather(values, "seq", axis=0, tiled=True),
    )

    def block_mask(index):
        key_pos = lax.dynamic_slice_in_dim(every_pos, index * size, size)
        key_docs = lax.dynamic_slice_in_dim(every_docs, index * size, size)
        return (key_pos[None, :] <= own_pos[:, None]) & (key_docs[None, :] == own_docs[:, None])

    def block_rows(array, index):
        return lax.dynamic_slice_in_dim(array, index * size, size).reshape(size, heads, HEAD_DIM)

    def block_scores(index, key_rows):
        return jnp.einsum(
            "qhd,khd->hqk", queries, block_rows(key_rows, index), preferred_element_type=jnp.float32
        )

    def stats_step(index, carry):
        allowed = block_mask(index)

        def update(state):
            peak, denom = state
            masked = jnp.where(allowed[None], block_scores(index, all_keys), -1e30)
            fresh = jnp.maximum(peak, jnp.max(masked, axis=-1))
            weights = jnp.where(allowed[None], jnp.exp(masked - fresh[..., None]), 0.0)
            return (fresh, denom * jnp.exp(peak - fresh) + jnp.sum(weights, axis=-1))

        return lax.cond(jnp.any(allowed), update, keep_state, carry)

    start_stats = (
        jnp.full((heads, rows), -1e30, jnp.float32),
        jnp.zeros((heads, rows), jnp.float32),
    )
    peak, denom = lax.fori_loop(0, count, stats_step, start_stats)

    def block_probs(index, allowed, key_rows):
        scores = block_scores(index, key_rows)
        return jnp.where(allowed[None], jnp.exp(scores - peak[..., None]), 0.0) / denom[..., None]

    def output_step(index, carry):
        allowed = block_mask(index)

        def output_accumulate(state):
            probs_low = block_probs(index, allowed, all_keys).astype(jnp.bfloat16)
            return state + jnp.einsum(
                "hqk,khd->qhd",
                probs_low,
                block_rows(all_values, index),
                preferred_element_type=jnp.float32,
            )

        return lax.cond(jnp.any(allowed), output_accumulate, keep_state, carry)

    running = lax.fori_loop(0, count, output_step, jnp.zeros(split, jnp.float32))
    mixed = running.reshape(rows, local_width).astype(jnp.bfloat16)
    attn_out = lax.psum(
        jnp.dot(mixed, out_weight, preferred_element_type=jnp.float32).astype(jnp.bfloat16),
        "tensor",
    ).astype(jnp.float32)
    hidden = residual + attn_out
    normed_second, unit_second, scale_second = layer_parts(hidden, second_gain, second_shift)
    normed_second = normed_second.astype(jnp.bfloat16)
    upward = jnp.dot(normed_second, up_weight, preferred_element_type=jnp.float32) + up_bias
    active_full, gelu_pull = jax.vjp(gelu_tanh, upward)
    active = active_full.astype(jnp.bfloat16)
    mlp_out = (
        lax.psum(
            jnp.dot(active, down_weight, preferred_element_type=jnp.float32).astype(jnp.bfloat16),
            "tensor",
        ).astype(jnp.float32)
        + down_bias
    )
    block_value = hidden + mlp_out
    history_low = history[:, 0]
    next_value = (
        jnp.sum(mix_weights[:depth, None, None] * history_low.astype(jnp.float32), axis=0)
        + mix_weights[depth] * block_value
    )
    cot_low = cotangent_next[0]
    cot_next = cot_low.astype(jnp.float32)
    cot_block = cotangent_block[0].astype(jnp.float32)
    grad_history = (mix_weights[:depth, None, None] * cot_next[None]).astype(jnp.bfloat16)
    mix_terms = jnp.concatenate(
        [
            jnp.einsum("jsd,sd->j", history_low, cot_low, preferred_element_type=jnp.float32),
            jnp.sum(block_value * cot_next)[None],
        ]
    )
    grad_block = cot_block + mix_weights[depth] * cot_next
    grad_mlp = grad_block.astype(jnp.bfloat16)
    grad_down = jnp.einsum("sf,sd->fd", active, grad_mlp, preferred_element_type=jnp.float32)
    grad_active = jnp.einsum("sd,fd->sf", grad_mlp, down_weight, preferred_element_type=jnp.float32)
    grad_up = gelu_pull(grad_active)[0].astype(jnp.bfloat16)
    grad_upw = jnp.einsum("sd,sf->df", normed_second, grad_up, preferred_element_type=jnp.float32)
    grad_normed_second = lax.psum(
        jnp.einsum("sf,df->sd", grad_up, up_weight, preferred_element_type=jnp.float32).astype(
            jnp.bfloat16
        ),
        "tensor",
    ).astype(jnp.float32)
    grad_hidden = grad_block + norm_backward(
        grad_normed_second, unit_second, scale_second, second_gain
    )
    grad_attn = grad_hidden.astype(jnp.bfloat16)
    grad_outw = jnp.einsum("sk,sd->kd", mixed, grad_attn, preferred_element_type=jnp.float32)
    grad_mixed = (
        jnp.einsum("sd,kd->sk", grad_attn, out_weight, preferred_element_type=jnp.float32)
        .astype(jnp.bfloat16)
        .reshape(split)
    )
    back_keys, back_values = (
        lax.all_gather(keys, "seq", axis=0, tiled=True),
        lax.all_gather(values, "seq", axis=0, tiled=True),
    )

    def delta_step(index, carry):
        allowed = block_mask(index)

        def delta_accumulate(state):
            probs = block_probs(index, allowed, back_keys)
            grad_probs = jnp.einsum(
                "qhd,khd->hqk",
                grad_mixed,
                block_rows(back_values, index),
                preferred_element_type=jnp.float32,
            )
            return state + jnp.sum(probs * grad_probs, axis=-1)

        return lax.cond(jnp.any(allowed), delta_accumulate, keep_state, carry)

    delta = lax.fori_loop(0, count, delta_step, jnp.zeros((heads, rows), jnp.float32))

    def grad_step(index, carry):
        allowed = block_mask(index)

        def grad_accumulate(state):
            grad_queries, key_buffer, value_buffer = state
            key_rows = block_rows(back_keys, index)
            value_rows = block_rows(back_values, index)
            probs = block_probs(index, allowed, back_keys)
            grad_probs = jnp.einsum(
                "qhd,khd->hqk", grad_mixed, value_rows, preferred_element_type=jnp.float32
            )
            grad_scores = (probs * (grad_probs - delta[..., None])).astype(jnp.bfloat16)
            grad_queries = grad_queries + jnp.einsum(
                "hqk,khd->qhd", grad_scores, key_rows, preferred_element_type=jnp.float32
            )
            key_part = jnp.einsum(
                "hqk,qhd->khd", grad_scores, queries, preferred_element_type=jnp.float32
            ).reshape(size, local_width)
            value_part = jnp.einsum(
                "hqk,qhd->khd",
                probs.astype(jnp.bfloat16),
                grad_mixed,
                preferred_element_type=jnp.float32,
            ).reshape(size, local_width)
            key_buffer = lax.dynamic_update_slice_in_dim(key_buffer, key_part, index * size, 0)
            value_buffer = lax.dynamic_update_slice_in_dim(
                value_buffer, value_part, index * size, 0
            )
            return (grad_queries, key_buffer, value_buffer)

        return lax.cond(jnp.any(allowed), grad_accumulate, keep_state, carry)

    start_grads = (
        jnp.zeros(split, jnp.float32),
        jnp.zeros((total, local_width), jnp.float32),
        jnp.zeros((total, local_width), jnp.float32),
    )
    grad_queries, key_buffer, value_buffer = lax.fori_loop(0, count, grad_step, start_grads)
    grad_keys, grad_values = (
        lax.psum_scatter(
            key_buffer.astype(jnp.bfloat16), "seq", scatter_dimension=0, tiled=True
        ).astype(jnp.float32),
        lax.psum_scatter(
            value_buffer.astype(jnp.bfloat16), "seq", scatter_dimension=0, tiled=True
        ).astype(jnp.float32),
    )
    grad_query_lin = (
        rotate(grad_queries * 0.125, cosine, -sine).reshape(rows, local_width).astype(jnp.bfloat16)
    )
    grad_key_lin = (
        rotate(grad_keys.reshape(split), cosine, -sine)
        .reshape(rows, local_width)
        .astype(jnp.bfloat16)
    )
    grad_value_lin = grad_values.astype(jnp.bfloat16)
    grad_queryw = jnp.einsum(
        "sd,se->de", normed_first, grad_query_lin, preferred_element_type=jnp.float32
    )
    grad_keyw = jnp.einsum(
        "sd,se->de", normed_first, grad_key_lin, preferred_element_type=jnp.float32
    )
    grad_valuew = jnp.einsum(
        "sd,se->de", normed_first, grad_value_lin, preferred_element_type=jnp.float32
    )
    local_normed = jnp.einsum(
        "se,de->sd", grad_query_lin, query_weight, preferred_element_type=jnp.float32
    )
    local_normed = local_normed + jnp.einsum(
        "se,de->sd", grad_key_lin, key_weight, preferred_element_type=jnp.float32
    )
    local_normed = local_normed + jnp.einsum(
        "se,de->sd", grad_value_lin, value_weight, preferred_element_type=jnp.float32
    )
    grad_normed_first = lax.psum(local_normed.astype(jnp.bfloat16), "tensor").astype(jnp.float32)
    grad_input = grad_hidden + norm_backward(grad_normed_first, unit_first, scale_first, first_gain)
    shared_grads = (
        lax.psum_scatter(grad_queryw, ("seq", "batch"), scatter_dimension=0, tiled=True),
        lax.psum_scatter(grad_keyw, ("seq", "batch"), scatter_dimension=0, tiled=True),
        lax.psum_scatter(grad_valuew, ("seq", "batch"), scatter_dimension=0, tiled=True),
        lax.psum_scatter(grad_outw, ("seq", "batch"), scatter_dimension=1, tiled=True),
        lax.psum_scatter(grad_upw, ("seq", "batch"), scatter_dimension=0, tiled=True),
        lax.psum_scatter(grad_down, ("seq", "batch"), scatter_dimension=1, tiled=True),
    )
    square_terms = jnp.stack(
        [
            jnp.sum(block_value * block_value),
            jnp.sum(attn_out * attn_out),
            jnp.sum(mlp_out * mlp_out),
        ]
    )
    small_terms = lax.psum(
        (
            jnp.sum(grad_normed_first * unit_first, axis=0),
            jnp.sum(grad_normed_first, axis=0),
            jnp.sum(grad_normed_second * unit_second, axis=0),
            jnp.sum(grad_normed_second, axis=0),
            jnp.sum(grad_up.astype(jnp.float32), axis=0),
            jnp.sum(grad_mlp.astype(jnp.float32), axis=0),
            mix_terms,
            square_terms,
        ),
        ("seq", "batch"),
    )
    entries = float(lax.axis_size("batch") * total * width)
    rms_values = jnp.sqrt(small_terms[7] / entries)
    return (
        next_value.astype(jnp.bfloat16)[None],
        block_value.astype(jnp.bfloat16)[None],
        grad_input.astype(jnp.bfloat16)[None],
        grad_history[:, None],
        small_terms[0],
        small_terms[1],
        shared_grads[0],
        shared_grads[1],
        shared_grads[2],
        shared_grads[3],
        small_terms[2],
        small_terms[3],
        shared_grads[4],
        small_terms[4],
        shared_grads[5],
        small_terms[5],
        small_terms[6],
        rms_values,
    )


def solution(mesh):
    in_specs = (
        P("batch", "seq", None),
        P(None, "batch", "seq", None),
        P("batch", None),
        P(),
        P(),
        P(),
        P(None, "tensor"),
        P(None, "tensor"),
        P(None, "tensor"),
        P("tensor", None),
        P(),
        P(),
        P(None, "tensor"),
        P("tensor"),
        P("tensor", None),
        P(),
        P(),
        P("batch", "seq", None),
        P("batch", "seq", None),
    )
    out_specs = (
        P("batch", "seq", None),
        P("batch", "seq", None),
        P("batch", "seq", None),
        P(None, "batch", "seq", None),
        P(),
        P(),
        P(("seq", "batch"), "tensor"),
        P(("seq", "batch"), "tensor"),
        P(("seq", "batch"), "tensor"),
        P("tensor", ("seq", "batch")),
        P(),
        P(),
        P(("seq", "batch"), "tensor"),
        P("tensor"),
        P("tensor", ("seq", "batch")),
        P(),
        P(),
        P(),
    )
    return jax.shard_map(
        device_function(mesh), mesh=mesh, in_specs=in_specs, out_specs=out_specs, check_vma=False
    )
```

```python
import functools
from types import SimpleNamespace

import jax
import jax.numpy as jnp
from jax import lax
from jax.experimental import pallas as pl
from jax.experimental.pallas import tpu as pltpu
from jax.sharding import PartitionSpec as P

HEAD_DIM = 64
f32, bf16, i32 = jnp.float32, jnp.bfloat16, jnp.int32
MESH = pl.DeviceIdType.MESH


epsilon = 1e-05


def layer_parts(values, gain, shift):
    centre = jnp.mean(values, axis=-1, keepdims=True)
    centred = values - centre
    spread = jnp.mean(centred * centred, axis=-1, keepdims=True)
    inverse = lax.rsqrt(spread + epsilon)
    unit = centred * inverse
    return (unit * gain + shift, unit, inverse)


def norm_backward(grad_out, unit, inverse, gain):
    scaled = grad_out * gain
    return inverse * (
        scaled
        - jnp.mean(scaled, axis=-1, keepdims=True)
        - unit * jnp.mean(scaled * unit, axis=-1, keepdims=True)
    )


def gelu_tanh(values):
    return (
        0.5
        * values
        * (1.0 + jnp.tanh(0.7978845608028654 * (values + 0.044715 * values * values * values)))
    )


def rotate(values, cosine, sine):
    half = values.shape[-1] // 2
    first = values[..., :half]
    second = values[..., half:]
    return jnp.concatenate(
        [first * cosine - second * sine, second * cosine + first * sine], axis=-1
    )


def keep_state(state):
    return state


def dot(a, b, ca=1, cb=0):
    return lax.dot_general(a, b, (((ca,), (cb,)), ((), ())), preferred_element_type=f32)


def rope_tables(pos, half):
    index = lax.broadcasted_iota(i32, (half, 1), 0).astype(f32)
    rates = jnp.exp(-jnp.log(f32(10000.0)) * index / half)
    angles = rates * pos
    return jnp.cos(angles), jnp.sin(angles)


def rotate_t(lin, cosine, sine):
    width, rows = lin.shape
    parts = lin.reshape(width // HEAD_DIM, 2, HEAD_DIM // 2, rows)
    first, second = parts[:, 0], parts[:, 1]
    turned = [first * cosine - second * sine, second * cosine + first * sine]
    return jnp.stack(turned, axis=1).reshape(width, rows)


def gelu_both(u):
    square = u * u
    t = jnp.tanh(0.7978845608028654 * (u + 0.044715 * square * u))
    half = 0.5 * (1.0 + t)
    slope = half + 0.5 * u * (1.0 - t * t) * (0.7978845608028654 * (1.0 + 3 * 0.044715 * square))
    return u * half, slope


def row_chunks(rows, body, size=64):
    def step(i, _):
        body(pl.ds(pl.multiple_of(i * size, size), size))
        return 0

    lax.fori_loop(0, rows // size, step, 0)


def folded(rows):
    total = jnp.sum(rows, axis=0, keepdims=True)
    return sum(total[:, k : k + 128] for k in range(0, total.shape[1], 128))


ROWS, WIDTH, LOCAL, GROUP, HIDDEN, BLOCK = 256, 768, 384, 192, 1536, 48


def scratch_spec(windows):
    vm = pltpu.VMEM
    heads = (3, HEAD_DIM, ROWS)
    full32, full16, turned = vm((ROWS, WIDTH), f32), vm((ROWS, WIDTH), bf16), vm((WIDTH, ROWS), bf16)

    def job(columns):
        return [
            vm((2, 2, 2, 2, BLOCK, columns), bf16), vm((2, 2, 2, BLOCK, columns), bf16),
            vm((2, 2, BLOCK, columns), bf16), vm((2, BLOCK, columns), bf16), vm((BLOCK, columns), bf16),
        ]

    return dict(
        x=full16, gain1_v=vm((WIDTH,), f32), shift1_v=vm((WIDTH,), f32), gain2_v=vm((WIDTH,), f32), shift2_v=vm((WIDTH,), f32),
        downb_v=vm((WIDTH,), f32), upb_v=vm((HIDDEN,), f32), order=pltpu.SMEM((4,), i32), windows=pltpu.SMEM((windows,), i32), mixw=pltpu.SMEM((9,), f32),
        cotn=full16, cotb=full16, wq=vm((WIDTH, LOCAL), bf16), wk=vm((WIDTH, LOCAL), bf16), wv=vm((WIDTH, LOCAL), bf16),
        hist=vm((8, ROWS, WIDTH), bf16), wup=vm((WIDTH, HIDDEN), bf16), wdown=vm((HIDDEN, WIDTH), bf16),
        wof=vm((2, 2, 3, HEAD_DIM, WIDTH), bf16),
        vectors=vm((5, 1, WIDTH), f32), upb=vm((1, HIDDEN), f32), upsum=vm((1, HIDDEN), f32),
        qown=vm((2, *heads), bf16), kvown=vm((2, 3, 2, HEAD_DIM, ROWS), bf16),
        qt=vm((2, *heads), bf16), kv=vm((4, 3, 2, HEAD_DIM, ROWS), bf16),
        scores=vm((3, 2, 4, ROWS, ROWS), f32), bias=vm((2, 4, ROWS, ROWS), f32),
        peak=vm((3, 2, 1, ROWS), f32), denom=vm((3, 2, 1, ROWS), f32), acc=vm((3, 2, HEAD_DIM, ROWS), f32),
        delta=vm((3, 2, 1, ROWS), f32), cosine=vm((32, ROWS), f32), sine=vm((32, ROWS), f32),
        mix=vm((2, 2, *heads), bf16), mixout=vm(heads, bf16),
        unit1=full32, inv1=vm((ROWS, 1), f32), norm1=full16, norm1t=turned,
        hidden=full32, attn=full32, unit2=full32, inv2=vm((ROWS, 1), f32), norm2=full16, norm2t=turned,
        gblock=full32, gmlp=full16, gmlpt=turned, hacc=full32, gact=vm((ROWS, HIDDEN), f32),
        act=vm((ROWS, HIDDEN), bf16), gup=vm((ROWS, HIDDEN), bf16), gnorm2=full32, gnew=full32,
        ghid=vm((2, ROWS, WIDTH), bf16), mlp=vm((2, ROWS, WIDTH), bf16), gin=vm((2, ROWS, WIDTH), bf16),
        dpart=vm((2, 2, *heads), bf16), dsend=vm((2, 2, *heads), bf16), dout=vm((2, *heads), bf16),
        dkv=vm((4, 3, 2, HEAD_DIM, ROWS), bf16), dkvin=vm((4, 3, 2, HEAD_DIM, ROWS), bf16),
        dq=vm((3, HEAD_DIM, ROWS), f32), dqout=vm(heads, bf16), dqin=vm(heads, bf16),
        own0=vm((3, 2, HEAD_DIM, ROWS), f32), lin=vm((3, 2, *heads), bf16), gattnt=turned,
        small=vm((5, 16, WIDTH), f32), smallin=vm((3, 16, WIDTH), f32), smallz=vm((3, 16, WIDTH), f32),
        job0=job(WIDTH), job1=job(WIDTH), job2=job(WIDTH), job3=job(WIDTH), job4=job(LOCAL), job5=job(640), job6=job(512),
        s_next=full16, s_block=full16, s_gin=full16, s_down=vm((BLOCK, HIDDEN), f32), s_up=vm((BLOCK, HIDDEN), f32),
        s_out=vm((BLOCK, LOCAL), f32), s_a=vm((BLOCK, 640), f32), s_b=vm((BLOCK, 512), f32), s_small=vm((16, WIDTH), f32),
        osem=pltpu.SemaphoreType.DMA((12,)),
        ssem=pltpu.SemaphoreType.DMA((96,)), rsem=pltpu.SemaphoreType.DMA((96,)), lsem=pltpu.SemaphoreType.DMA((24,)),
    )


def layer_kernel(make, *refs):
    R = make(refs)
    z, b, y = lax.axis_index("seq"), lax.axis_index("batch"), lax.axis_index("tensor")
    near, flip, far = z + 1 - 2 * (z % 2), (z + 2) % 4, 3 - z
    m, p, xbit, core = z % 2, z // 2, b // 2, b % 2
    to_near, to_flip, to_far = dict(seq=near), dict(seq=flip), dict(seq=far)
    to_y, to_diag = dict(tensor=1 - y), dict(seq=near, tensor=1 - y)
    to_x, to_core = dict(batch=(b + 2) % 4), dict(batch=b + 1 - 2 * core)
    barrier = pltpu.get_barrier_semaphore()
    everyone = [to_near, to_flip, to_far, to_y, to_diag, to_x, to_core]
    for there in everyone:
        pl.semaphore_signal(barrier, inc=1, device_id=there, device_id_type=MESH)
    started = []

    def send(src, dst, there):
        i = len(started)
        copy = pltpu.make_async_remote_copy(
            src, dst, R.ssem.at[i], R.rsem.at[i], device_id=there, device_id_type=MESH
        )
        copy.start()
        started.append(copy)
        return copy

    def fetch(src, dst, i):
        copy = pltpu.make_async_copy(src, dst, R.lsem.at[i])
        copy.start()
        return copy

    get_small = [fetch(R.x_h, R.x, 9)]
    get_k = fetch(R.wk_h, R.wk, 1)
    pairs = [(R.gain1_in, R.gain1_v), (R.shift1_in, R.shift1_v), (R.order_in, R.order), (R.windows_in, R.windows)]
    pairs += [(R.gain2_in, R.gain2_v), (R.shift2_in, R.shift2_v), (R.downb_in, R.downb_v), (R.upb_in, R.upb_v)]
    pairs.append((R.mixw_in, R.mixw))
    for i, (src, dst) in enumerate(pairs):
        get_small.append(fetch(src, dst, 10 + i))
    get_q = fetch(R.wq_h, R.wq, 0)
    get_v = fetch(R.wv_h, R.wv, 2)
    written = []

    def write(src, dst):
        copy = pltpu.make_async_copy(src, dst, R.osem.at[len(written)])
        copy.start()
        written.append(copy)

    for c in get_small:
        c.wait()
    ends, total = [], 0
    for i in range(R.windows.shape[0]):
        total = total + R.windows[i]
        ends.append(total)
    for i, ref in enumerate((R.gain1_v, R.shift1_v, R.gain2_v, R.shift2_v, R.downb_v)):
        R.vectors[i] = ref[...][None]
    R.upb[...] = R.upb_v[...][None]
    R.gain1, R.shift1, R.gain2, R.shift2, R.downb = (R.vectors.at[i] for i in range(5))
    base = [R.order[k] * ROWS for k in (z, near, flip, far)]
    lane = lax.broadcasted_iota(i32, (1, ROWS), 1)

    def norm_first(rows):
        x = R.x[rows].astype(f32)
        centred = x - jnp.mean(x, axis=-1, keepdims=True)
        inverse = lax.rsqrt(jnp.mean(centred * centred, axis=-1, keepdims=True) + epsilon)
        unit = centred * inverse
        R.unit1[rows] = unit
        R.inv1[rows] = inverse
        R.norm1[rows] = (unit * R.gain1[...] + R.shift1[...]).astype(bf16)

    row_chunks(ROWS, norm_first)
    cosine, sine = rope_tables((base[0] + lane).astype(f32), HEAD_DIM // 2)
    R.cosine[...] = cosine
    R.sine[...] = sine
    split = (2, 3, HEAD_DIM, ROWS)
    get_k.wait()
    R.kvown[:, :, 0] = rotate_t(dot(R.norm1[...], R.wk[...]).T, cosine, sine).astype(bf16).reshape(split)
    get_v.wait()
    R.kvown[:, :, 1] = dot(R.norm1[...], R.wv[...]).T.astype(bf16).reshape(split)
    pl.semaphore_wait(barrier, len(everyone))
    near_in, flip_in, far_in = [], [], []

    def kv_out(h):
        near_in.append(send(R.kvown.at[1 - m, h], R.kv.at[1, h], to_near))
        flip_in.append(send(R.kvown.at[m, h], R.kv.at[2, h], to_flip))
        far_in.append(send(R.kvown.at[1 - m, h], R.kv.at[3, h], to_far))

    kv_out(0)
    get_q.wait()
    get_out = fetch(R.wout, R.wof.at[0], 5)
    get_cot = [fetch(R.cotn_h, R.cotn, 3), fetch(R.cotb_h, R.cotb, 4)]
    get_hist = fetch(R.history, R.hist, 6)
    get_down = fetch(R.wdown_h, R.wdown, 7)
    get_up = fetch(R.wup_h, R.wup, 8)
    queries = rotate_t(dot(R.norm1[...], R.wq[...]).T, cosine, sine) * 0.125
    R.qown[...] = queries.astype(bf16).reshape(split)
    q_in = [send(R.qown.at[1 - m, h], R.qt.at[1, h], to_near) for h in range(1)]
    kv_out(1)
    q_in.append(send(R.qown.at[1 - m, 1], R.qt.at[1, 1], to_near))
    kv_out(2)
    q_in.append(send(R.qown.at[1 - m, 2], R.qt.at[1, 2], to_near))
    get_out.wait()
    out_in = send(R.wof.at[0], R.wof.at[1], to_y)
    R.qt[0] = R.qown[m]
    R.kv[0] = R.kvown[m]

    for j in range(2):
        qpos = base[j] + lane
        start = 0 * qpos
        for end in ends:
            start = jnp.maximum(start, jnp.where(qpos >= end, end, 0))
        for r in range(4):
            kpos = base[r] + lax.broadcasted_iota(i32, (ROWS, ROWS), 0)
            R.bias[j, r] = jnp.where((kpos <= qpos) & (kpos >= start), 0.0, -1e30).astype(f32)
    for c in get_cot:
        c.wait()
    R.small[0] = jnp.zeros((16, WIDTH), f32)
    mix_last = R.mixw[8]

    def block_grads(rows):
        g = R.cotb[rows].astype(f32) + mix_last * R.cotn[rows].astype(f32)
        R.gblock[rows] = g
        low = g.astype(bf16)
        R.gmlp[rows] = low
        R.small[0, 4:5] += 0.5 * jnp.sum(low.astype(f32), axis=0, keepdims=True)

    row_chunks(ROWS, block_grads)
    R.gmlpt[...] = R.gmlp[...].T
    R.norm1t[...] = R.norm1[...].T
    get_hist.wait()

    def history_sum(rows):
        cot = R.cotn[rows].astype(f32)
        total = 0
        for j in range(8):
            h = R.hist[j, rows].astype(f32)
            total = total + R.mixw[j] * h
            R.small[0, 5 + j // 6 : 6 + j // 6, 128 * (j % 6) : 128 * (j % 6) + 128] += 0.5 * folded(h * cot)
        R.hacc[rows] = total

    row_chunks(ROWS, history_sum, 32)
    get_down.wait()

    def active_grad(n, _):
        at = pl.ds(pl.multiple_of(256 * n, 256), 256)
        R.gact[:, at] = dot(R.gmlp[...], R.wdown[at], 1, 1)
        return 0

    lax.fori_loop(0, 6, active_grad, 0)

    def tile(h, j, r, first=False):
        s = dot(R.kv[r, h, 0], R.qt[j, h], 0, 0) + R.bias[j, r]
        R.scores[h, j, r] = s
        top = jnp.max(s, axis=0, keepdims=True)
        if first:
            e = jnp.exp(s - top)
            R.denom[h, j] = jnp.sum(e, axis=0, keepdims=True)
            R.acc[h, j] = dot(R.kv[r, h, 1], e.astype(bf16))
        else:
            old = R.peak[h, j]
            top = jnp.maximum(top, old)
            e = jnp.exp(s - top)
            alpha = jnp.exp(old - top)
            R.denom[h, j] = R.denom[h, j] * alpha + jnp.sum(e, axis=0, keepdims=True)
            R.acc[h, j] = R.acc[h, j] * alpha + dot(R.kv[r, h, 1], e.astype(bf16))
        R.peak[h, j] = top

    def finish(h, j):
        R.acc[h, j] = R.acc[h, j] * (1.0 / R.denom[h, j])
        R.peak[h, j] = R.peak[h, j] + jnp.log(R.denom[h, j])
        return R.acc[h, j].astype(bf16)

    mix_in = []
    for h in range(3):
        tile(h, 0, 0, True)
    for h in range(3):
        near_in[h].wait_recv()
        q_in[h].wait_recv()
        tile(h, 0, 1)
        tile(h, 1, 1, True)
        tile(h, 1, 0)
        flip_in[h].wait_recv()
        tile(h, 1, 2)
        tile(h, 0, 2)
        far_in[h].wait_recv()
        tile(h, 1, 3)
        tile(h, 0, 3)
        R.mixout[h] = finish(h, 1)
        R.mix[0, 0, h] = finish(h, 0)
        mix_in.append(send(R.mixout.at[h], R.mix.at[1, 1, h], to_diag))
        mix_in.append(send(R.mix.at[0, 0, h], R.mix.at[1, 0, h], to_y))
        mix_in.append(send(R.mixout.at[h], R.mix.at[0, 1, h], to_near))
    get_up.wait()
    out_in.wait_recv()
    for c in mix_in:
        c.wait_recv()
    group = (GROUP, ROWS)
    out = 0
    for t in range(2):
        for a in range(2):
            side = R.mix[(t + y) % 2, (a + m) % 2].reshape(group)
            out = out + dot(side, R.wof[(t + y) % 2, a].reshape(GROUP, WIDTH), 0, 0)
    R.attn[...] = out

    def norm_second(rows):
        hidden = R.x[rows].astype(f32) + R.attn[rows]
        R.hidden[rows] = hidden
        centred = hidden - jnp.mean(hidden, axis=-1, keepdims=True)
        inverse = lax.rsqrt(jnp.mean(centred * centred, axis=-1, keepdims=True) + epsilon)
        unit = centred * inverse
        R.unit2[rows] = unit
        R.inv2[rows] = inverse
        R.norm2[rows] = (unit * R.gain2[...] + R.shift2[...]).astype(bf16)

    bits = dict(core=core, x=xbit, near=m, flip=p)
    where = dict(core=to_core, x=to_x, near=to_near, flip=to_flip)
    place = dict(core=0, x=1, near=2, flip=3)

    class Job:
        def __init__(self, bufs, route):
            self.grads, self.landing, self.route, self.copy, self.step = bufs[0], bufs[1:], route, None, 0

        def put(self, value, columns):
            for k in range(16):
                at = tuple((k >> place[axis]) & 1 for axis in self.route)
                self.grads[(*at, slice(None), columns)] = value[BLOCK * k : BLOCK * k + BLOCK].astype(bf16)

        def mine(self):
            return tuple(bits[axis] for axis in self.route[: self.step])

        def push(self):
            axis = self.route[self.step]
            self.copy = send(self.grads.at[(*self.mine(), 1 - bits[axis])], self.landing[self.step], where[axis])

        def pull(self, out=None):
            self.copy.wait_recv()
            landing = self.landing[self.step]
            self.step += 1
            kept = self.mine()
            left = 4 - self.step

            def add(i, _):
                at = tuple((i // 2**k) % 2 for k in range(left))
                mine, theirs = self.grads[(*kept, *at)], landing[at if at else Ellipsis]
                if out is None:
                    self.grads[(*kept, *at)] = mine + theirs
                else:
                    out[...] = mine.astype(f32) + theirs.astype(f32)
                return 0

            if left:
                lax.fori_loop(0, 2**left, add, 0)
            else:
                add(0, 0)

        def turn(self):
            self.pull()
            self.push()

    usual = tuple(place)
    down0, down1, up0, up1 = (Job(bufs, usual) for bufs in (R.job0, R.job1, R.job2, R.job3))
    job_out, job_a, job_b = (Job(bufs, usual) for bufs in (R.job4, R.job5, R.job6))

    row_chunks(ROWS, norm_second)
    for n in range(6):
        at = slice(256 * n, 256 * n + 256)
        u = dot(R.norm2[...], R.wup[:, at]) + R.upb[:, at]
        active, slope = gelu_both(u)
        R.act[:, at] = active.astype(bf16)
        grad = (R.gact[:, at] * slope).astype(bf16)
        R.gup[:, at] = grad
        R.upsum[:, at] = jnp.sum(grad.astype(f32), axis=0, keepdims=True)
        third = slice(256 * (n % 3), 256 * (n % 3) + 256)
        (down0, down1)[n // 3].put(dot(R.gmlpt[...], R.act[:, at]), third)
        if n == 2:
            down0.push()
            R.gnorm2[...] = dot(R.gup[:, :WIDTH], R.wup[:, :WIDTH], 1, 1)
    down1.push()
    R.gnorm2[...] += dot(R.gup[:, WIDTH:], R.wup[:, WIDTH:], 1, 1)

    def norm_back(grad, unit, inverse, gain):
        scaled = grad * gain
        return inverse * (
            scaled
            - jnp.mean(scaled, axis=-1, keepdims=True)
            - unit * jnp.mean(scaled * unit, axis=-1, keepdims=True)
        )

    def second_back(rows):
        back = norm_back(R.gnorm2[rows], R.unit2[rows], R.inv2[rows], R.gain2[...])
        R.ghid[0, rows] = (0.5 * R.gblock[rows] + back).astype(bf16)

    row_chunks(ROWS, second_back)
    d_in = []
    order = [(1, 1), (1, 0), (0, 1), (0, 0)]
    for h in range(3):
        weights = jnp.concatenate([R.wof[t, (a + m) % 2, h] for t, a in order], axis=0)
        parts = dot(weights, R.ghid[0], 1, 1).astype(bf16).reshape(4, HEAD_DIM, ROWS)
        for k in range(3):
            R.dsend[(*order[k], h)] = parts[k]
        R.dpart[0, 0, h] = parts[3]
        d_in.append(
            [
                send(R.dsend.at[1, 1, h], R.dpart.at[1, 1, h], to_diag),
                send(R.dsend.at[1, 0, h], R.dpart.at[0, 1, h], to_y),
                send(R.dsend.at[0, 1, h], R.dpart.at[1, 0, h], to_near),
            ]
        )
    ghid_in = send(R.ghid.at[0], R.ghid.at[1], to_y)

    kv_in, dq_in = [], []

    def back_head(h):
        for c in d_in[h]:
            c.wait_recv()
        for j in range(2):
            both = R.dpart[j, 0, h].astype(f32) + R.dpart[j, 1, h].astype(f32)
            R.dout[j, h] = both.astype(bf16)
            R.delta[h, j] = jnp.sum(R.dout[j, h].astype(f32) * R.acc[h, j], axis=0, keepdims=True)
        total = [0, 0]
        for r in (2, 3, 1, 0):
            dk, dv = 0, 0
            for j in range(2):
                probs = jnp.exp(R.scores[h, j, r] - R.peak[h, j])
                grad = dot(R.kv[r, h, 1], R.dout[j, h], 0, 0)
                low = (probs * (grad - R.delta[h, j])).astype(bf16)
                dv = dv + dot(R.dout[j, h], probs.astype(bf16), 1, 1)
                dk = dk + dot(R.qt[j, h], low, 1, 1)
                total[j] = total[j] + dot(R.kv[r, h, 0], low)
            if r:
                R.dkv[r, h, 0] = dk.astype(bf16)
                R.dkv[r, h, 1] = dv.astype(bf16)
                kv_in.append(send(R.dkv.at[r, h], R.dkvin.at[r, h], (to_near, to_flip, to_far)[r - 1]))
            else:
                R.own0[h, 0] = dk
                R.own0[h, 1] = dv
        R.dqout[h] = (0.125 * total[1]).astype(bf16)
        dq_in.append(send(R.dqout.at[h], R.dqin.at[h], to_near))
        R.dq[h] = 0.125 * total[0]

    down0.turn()
    back_head(0)
    down1.turn()
    back_head(1)
    back_head(2)
    R.norm2t[...] = R.norm2[...].T
    for k, job in enumerate((up0, up1)):
        for n in range(3):
            at = slice(WIDTH * k + 256 * n, WIDTH * k + 256 * n + 256)
            job.put(dot(R.norm2t[...], R.gup[:, at]), slice(256 * n, 256 * n + 256))
        job.push()
    down0.turn()
    R.mlp[0] = dot(R.act[...], R.wdown[...]).astype(bf16)
    mlp_in = send(R.mlp.at[0], R.mlp.at[1], to_y)
    up0.turn()
    up1.turn()

    ghid_in.wait_recv()

    def whole_hidden(rows):
        hid = R.ghid[0, rows].astype(f32) + R.ghid[1, rows].astype(f32)
        R.gblock[rows] = hid
        R.gmlp[rows] = hid.astype(bf16)
        back = R.gnorm2[rows]
        R.small[0, 2:3] += jnp.sum(back * R.unit2[rows], axis=0, keepdims=True)
        R.small[0, 3:4] += jnp.sum(back, axis=0, keepdims=True)

    row_chunks(ROWS, whole_hidden)
    R.gattnt[...] = R.gmlp[...].T
    mixed = jnp.concatenate([R.mix[0, (a + m) % 2].reshape(group) for a in range(2)], axis=0)
    job_out.put(dot(R.gattnt[...], mixed, 1, 1), slice(None))
    job_out.push()
    down1.turn()
    job_out.turn()

    mlp_in.wait_recv()

    def block_out(rows):
        both = R.mlp[0, rows].astype(f32) + R.mlp[1, rows].astype(f32) + R.downb[...]
        value = R.hidden[rows] + both
        R.s_block[rows] = value.astype(bf16)
        R.s_next[rows] = (R.hacc[rows] + mix_last * value).astype(bf16)
        attn = R.attn[rows]
        for k, term in enumerate((value * R.cotn[rows].astype(f32), value * value, attn * attn, both * both)):
            R.small[0, 6:7, 128 * (2 + k) : 128 * (3 + k)] += 0.5 * folded(term)

    row_chunks(ROWS, block_out, 32)
    for k in range(8):
        R.small[0, 10 + k // 6 : 11 + k // 6, 128 * (k % 6) : 128 * (k % 6) + 128] = jnp.full((1, 128), R.mixw[k], f32)
    write(R.s_block, R.o_block)
    write(R.s_next, R.o_next)
    R.small[0, 8:9] = R.upsum[:, :WIDTH]
    R.small[0, 9:10] = R.upsum[:, WIDTH:]

    up0.turn()
    down0.turn()

    cosine, sine = R.cosine[...], -R.sine[...]
    for h in range(3):
        for c in (*kv_in[3 * h : 3 * h + 3], dq_in[h]):
            c.wait_recv()
        for k in range(2):
            ours = R.own0[h, k] + R.dkvin[2, h, k].astype(f32)
            theirs = R.dkvin[1, h, k].astype(f32) + R.dkvin[3, h, k].astype(f32)
            if k == 0:
                ours, theirs = rotate_t(ours, cosine, sine), rotate_t(theirs, cosine, sine)
            R.lin[1 + k, m, h] = ours.astype(bf16)
            R.lin[1 + k, 1 - m, h] = theirs.astype(bf16)
        R.lin[0, m, h] = rotate_t(R.dq[h], cosine, sine).astype(bf16)
        R.lin[0, 1 - m, h] = rotate_t(R.dqin[h].astype(f32), cosine, sine).astype(bf16)
    lins = [R.lin[k].reshape(LOCAL, ROWS) for k in range(3)]
    first = dot(R.wq[...], lins[0]) + dot(R.wk[...], lins[1]) + dot(R.wv[...], lins[2])
    R.gnew[...] = first.T

    def first_back(rows):
        grad = R.gnew[rows]
        R.gin[0, rows] = norm_back(grad, R.unit1[rows], R.inv1[rows], R.gain1[...]).astype(bf16)
        R.small[0, 0:1] += jnp.sum(grad * R.unit1[rows], axis=0, keepdims=True)
        R.small[0, 1:2] += jnp.sum(grad, axis=0, keepdims=True)

    row_chunks(ROWS, first_back)
    small_in = send(R.small.at[0, pl.ds(0, 8)], R.smallin.at[0, pl.ds(0, 8)], to_y)
    gin_in = send(R.gin.at[0], R.gin.at[1], to_y)
    every = jnp.concatenate(lins, axis=0)
    job_a.put(dot(R.norm1t[...], every[:640], 1, 1), slice(None))
    job_a.push()
    job_b.put(dot(R.norm1t[...], every[640:], 1, 1), slice(None))
    job_b.push()
    up1.turn()
    down1.turn()
    small_in.wait_recv()
    R.small[1, 0:8] = R.small[0, 0:8] + R.smallin[0, 0:8]
    R.small[1, 8:16] = R.small[0, 8:16]
    small_in = send(R.small.at[1], R.smallin.at[1], to_core)
    job_a.turn()
    job_b.turn()
    job_out.turn()
    up0.turn()
    small_in.wait_recv()
    R.small[2] = R.small[1] + R.smallin[1]
    small_in = send(R.small.at[2], R.smallin.at[2], to_x)
    up1.turn()
    down0.pull(R.s_down.at[:, pl.ds(0, WIDTH)])
    down1.pull(R.s_down.at[:, pl.ds(WIDTH, WIDTH)])
    write(R.s_down, R.o_down)
    gin_in.wait_recv()

    def grad_in(rows):
        both = R.gin[0, rows].astype(f32) + R.gin[1, rows].astype(f32)
        R.s_gin[rows] = (R.gblock[rows] + both).astype(bf16)

    row_chunks(ROWS, grad_in)
    write(R.s_gin, R.o_gin)
    job_a.turn()
    job_out.turn()
    job_b.turn()
    small_in.wait_recv()
    R.small[3] = R.small[2] + R.smallin[2]
    small_in = [
        send(R.small.at[3], R.smallz.at[k], there) for k, there in enumerate((to_near, to_flip, to_far))
    ]
    job_a.turn()
    up0.pull(R.s_up.at[:, pl.ds(0, WIDTH)])
    up1.pull(R.s_up.at[:, pl.ds(WIDTH, WIDTH)])
    write(R.s_up, R.o_up)
    job_out.pull(R.s_out)
    write(R.s_out, R.o_out)
    job_b.turn()
    for c in small_in:
        c.wait_recv()
    R.s_small[...] = (R.small[3] + R.smallz[0]) + (R.smallz[1] + R.smallz[2])
    R.s_small[10:12] = R.small[0, 10:12]
    write(R.s_small, R.o_small)
    job_a.pull(R.s_a)
    write(R.s_a, R.o_a)
    job_b.pull(R.s_b)
    write(R.s_b, R.o_b)
    for c in started:
        c.wait_send()
    for c in written:
        c.wait()


def last_kernel(make, entries, *refs):
    R = make(refs)
    copies = []

    def copy(src, dst):
        moving = pltpu.make_async_copy(src, dst, R.sems.at[len(copies)])
        moving.start()
        copies.append(moving)
        return moving

    get_cot = [copy(R.cotn, R.v_cotn), copy(R.o_small, R.v_small)]
    pairs = [(R.o_next, R.v_next, R.next.at[0]), (R.o_block, R.v_block, R.block.at[0])]
    pairs += [(R.o_gin, R.v_gin, R.gin.at[0]), (R.o_up, R.v_up, R.gup), (R.o_down, R.v_down, R.gdown)]
    pairs.append((R.o_out, R.v_out, R.gout))
    loads = [copy(src, dst) for src, dst, _ in pairs]
    loads += [copy(R.o_a, R.v_a), copy(R.o_b, R.v_b)]
    for c in get_cot:
        c.wait()
    count = len(copies)
    for j in range(8):
        weight = R.v_small[10 + j // 6 : 11 + j // 6, 128 * (j % 6) : 128 * (j % 6) + 1]
        R.v_hist[j] = (weight * R.v_cotn[...].astype(f32)).astype(bf16)
        copy(R.v_hist.at[j], R.ghist.at[j, 0])
    for c, (_, held, out) in zip(loads, pairs):
        c.wait()
        copy(held, out)
    loads[-2].wait()
    loads[-1].wait()
    copy(R.v_a.at[:, pl.ds(0, LOCAL)], R.gq)
    copy(R.v_a.at[:, pl.ds(LOCAL, 256)], R.gk.at[:, pl.ds(0, 256)])
    copy(R.v_b.at[:, pl.ds(0, 128)], R.gk.at[:, pl.ds(256, 128)])
    copy(R.v_b.at[:, pl.ds(128, LOCAL)], R.gv)
    vectors = (R.gain1, R.shift1, R.gain2, R.shift2, R.downb)
    for i, ref in enumerate((R.v_gain1, R.v_shift1, R.v_gain2, R.v_shift2, R.v_downb)):
        ref[...] = R.v_small[i]
        copy(ref, vectors[i])
    R.v_upb[0:WIDTH] = R.v_small[8]
    R.v_upb[WIDTH:HIDDEN] = R.v_small[9]
    copy(R.v_upb, R.upb)
    parts = [R.v_small[5 + k // 6 : 6 + k // 6, 128 * (k % 6) : 128 * (k % 6) + 128] for k in range(12)]
    sums = jnp.sum(jnp.concatenate(parts, axis=0), axis=1, keepdims=True)
    row = jnp.broadcast_to(sums, (12, 128)).T[0:1]
    R.v_gmix[...] = row[0, :9]
    R.v_rms[...] = jnp.sqrt(row / entries)[0, 9:]
    copy(R.v_gmix, R.gmix)
    copy(R.v_rms, R.rms)
    for c in copies[count:]:
        c.wait()


def out_spec(shape, dtype=f32):
    return jax.ShapeDtypeStruct(shape, dtype)


def namer(*groups):
    names = [name for group in groups for name in group]
    return lambda refs: SimpleNamespace(**dict(zip(names, refs)))


def per_device_block(
    inputs,
    history,
    window_lengths,
    block_order,
    first_gain,
    first_shift,
    query_weight,
    key_weight,
    value_weight,
    out_weight,
    second_gain,
    second_shift,
    up_weight,
    up_bias,
    down_weight,
    down_bias,
    mix_weights,
    cotangent_next,
    cotangent_block,
):
    hbm = pl.BlockSpec(memory_space=pl.ANY)
    args = dict(
        x_h=inputs[0], gain1_in=first_gain, shift1_in=first_shift, gain2_in=second_gain, shift2_in=second_shift,
        upb_in=up_bias, downb_in=down_bias,
        cotn_h=cotangent_next[0], cotb_h=cotangent_block[0], wq_h=query_weight, wk_h=key_weight, wv_h=value_weight,
        wout=out_weight.reshape(2, 3, HEAD_DIM, WIDTH), history=history[:, 0], wup_h=up_weight, wdown_h=down_weight,
        windows_in=window_lengths[0], order_in=block_order, mixw_in=mix_weights,
    )
    specs = [hbm] * len(args)
    outs = dict(
        o_next=out_spec((ROWS, WIDTH), bf16), o_block=out_spec((ROWS, WIDTH), bf16), o_gin=out_spec((ROWS, WIDTH), bf16),
        o_down=out_spec((BLOCK, HIDDEN)), o_up=out_spec((BLOCK, HIDDEN)), o_out=out_spec((BLOCK, LOCAL)),
        o_a=out_spec((BLOCK, 640)), o_b=out_spec((BLOCK, 512)), o_small=out_spec((16, WIDTH)),
    )
    scratch = scratch_spec(window_lengths.shape[1])
    flat, names = [], []
    for name, spec in scratch.items():
        several = isinstance(spec, list)
        names.append((name, len(spec) if several else 0))
        flat.extend(spec if several else [spec])

    def make(refs):
        R, k = dict(zip([*args, *outs], refs)), len(args) + len(outs)
        for name, count in names:
            R[name] = refs[k : k + count] if count else refs[k]
            k += max(count, 1)
        return SimpleNamespace(**R)

    held = pl.pallas_call(
        functools.partial(layer_kernel, make),
        out_shape=list(outs.values()),
        in_specs=specs,
        out_specs=[hbm] * len(outs),
        scratch_shapes=flat,
        compiler_params=pltpu.CompilerParams(
            collective_id=1, has_side_effects=True, vmem_limit_bytes=63 * 2**20
        ),
    )(*args.values())
    held = dict(zip(outs, held))
    rows3 = (1, ROWS, WIDTH)
    results = dict(
        next=out_spec(rows3, bf16), block=out_spec(rows3, bf16), gin=out_spec(rows3, bf16),
        ghist=out_spec((8, *rows3), bf16), gain1=out_spec((WIDTH,)), shift1=out_spec((WIDTH,)),
        gq=out_spec((BLOCK, LOCAL)), gk=out_spec((BLOCK, LOCAL)), gv=out_spec((BLOCK, LOCAL)),
        gout=out_spec((BLOCK, LOCAL)), gain2=out_spec((WIDTH,)), shift2=out_spec((WIDTH,)),
        gup=out_spec((BLOCK, HIDDEN)), upb=out_spec((HIDDEN,)), gdown=out_spec((BLOCK, HIDDEN)),
        downb=out_spec((WIDTH,)), gmix=out_spec((9,)), rms=out_spec((3,)),
    )
    entries = float(lax.axis_size("batch") * lax.axis_size("seq") * ROWS * WIDTH)
    given = dict(cotn=cotangent_next[0], **held)
    vm, full, row = pltpu.VMEM, pltpu.VMEM((ROWS, WIDTH), bf16), pltpu.VMEM((WIDTH,), f32)
    staging = dict(
        v_cotn=full, v_hist=vm((8, ROWS, WIDTH), bf16), v_next=full, v_block=full, v_gin=full,
        v_up=vm((BLOCK, HIDDEN), f32), v_down=vm((BLOCK, HIDDEN), f32), v_out=vm((BLOCK, LOCAL), f32),
        v_a=vm((BLOCK, 640), f32), v_b=vm((BLOCK, 512), f32), v_small=vm((16, WIDTH), f32),
        v_gain1=row, v_shift1=row, v_gain2=row, v_shift2=row, v_downb=row, v_upb=vm((HIDDEN,), f32),
        v_gmix=vm((9,), f32), v_rms=vm((3,), f32), sems=pltpu.SemaphoreType.DMA((40,)),
    )
    done = pl.pallas_call(
        functools.partial(last_kernel, namer(given, results, staging), entries),
        out_shape=list(results.values()),
        in_specs=[hbm] * len(given),
        out_specs=[hbm] * len(results),
        scratch_shapes=list(staging.values()),
        compiler_params=pltpu.CompilerParams(vmem_limit_bytes=63 * 2**20),
    )(*given.values())
    done = dict(zip(results, done))
    turned = dict(gout=done[list(results)[9]].T, gdown=done[list(results)[14]].T)
    return tuple((done | turned).values())


def device_function(mesh):
    return per_device_block if mesh.shape["seq"] == 4 else per_device_general


def per_device_general(
    inputs,
    history,
    window_lengths,
    block_order,
    first_gain,
    first_shift,
    query_weight,
    key_weight,
    value_weight,
    out_weight,
    second_gain,
    second_shift,
    up_weight,
    up_bias,
    down_weight,
    down_bias,
    mix_weights,
    cotangent_next,
    cotangent_block,
):
    rows = inputs.shape[1]
    width = inputs.shape[2]
    local_width = query_weight.shape[1]
    heads = local_width // HEAD_DIM
    half = HEAD_DIM // 2
    depth = history.shape[0]
    total = rows * lax.axis_size("seq")
    size = min(1024, total)
    count = total // size
    split = (rows, heads, HEAD_DIM)
    offsets = jnp.arange(rows, dtype=jnp.int32)
    own_pos = block_order[lax.axis_index("seq")] * rows + offsets
    every_row = jnp.arange(total, dtype=jnp.int32)
    every_pos = block_order[every_row // rows] * rows + every_row % rows
    ends = jnp.cumsum(window_lengths[0])
    own_docs = jnp.sum((own_pos[:, None] >= ends[None, :]).astype(jnp.int32), axis=1)
    every_docs = jnp.sum((every_pos[:, None] >= ends[None, :]).astype(jnp.int32), axis=1)
    rates = jnp.exp(-jnp.log(10000.0) * jnp.arange(half, dtype=jnp.float32) / half)
    angles = own_pos.astype(jnp.float32)[:, None] * rates[None, :]
    cosine = jnp.cos(angles)[:, None, :]
    sine = jnp.sin(angles)[:, None, :]
    residual = inputs[0].astype(jnp.float32)
    normed_first, unit_first, scale_first = layer_parts(residual, first_gain, first_shift)
    normed_first = normed_first.astype(jnp.bfloat16)
    query_lin = jnp.dot(normed_first, query_weight, preferred_element_type=jnp.float32)
    key_lin = jnp.dot(normed_first, key_weight, preferred_element_type=jnp.float32)
    value_lin = jnp.dot(normed_first, value_weight, preferred_element_type=jnp.float32)
    queries = (rotate(query_lin.reshape(split), cosine, sine) * 0.125).astype(jnp.bfloat16)
    keys = (
        rotate(key_lin.reshape(split), cosine, sine).reshape(rows, local_width).astype(jnp.bfloat16)
    )
    values = value_lin.astype(jnp.bfloat16)
    all_keys, all_values = (
        lax.all_gather(keys, "seq", axis=0, tiled=True),
        lax.all_gather(values, "seq", axis=0, tiled=True),
    )

    def block_mask(index):
        key_pos = lax.dynamic_slice_in_dim(every_pos, index * size, size)
        key_docs = lax.dynamic_slice_in_dim(every_docs, index * size, size)
        return (key_pos[None, :] <= own_pos[:, None]) & (key_docs[None, :] == own_docs[:, None])

    def block_rows(array, index):
        return lax.dynamic_slice_in_dim(array, index * size, size).reshape(size, heads, HEAD_DIM)

    def block_scores(index, key_rows):
        return jnp.einsum(
            "qhd,khd->hqk", queries, block_rows(key_rows, index), preferred_element_type=jnp.float32
        )

    def stats_step(index, carry):
        allowed = block_mask(index)

        def update(state):
            peak, denom = state
            masked = jnp.where(allowed[None], block_scores(index, all_keys), -1e30)
            fresh = jnp.maximum(peak, jnp.max(masked, axis=-1))
            weights = jnp.where(allowed[None], jnp.exp(masked - fresh[..., None]), 0.0)
            return (fresh, denom * jnp.exp(peak - fresh) + jnp.sum(weights, axis=-1))

        return lax.cond(jnp.any(allowed), update, keep_state, carry)

    start_stats = (
        jnp.full((heads, rows), -1e30, jnp.float32),
        jnp.zeros((heads, rows), jnp.float32),
    )
    peak, denom = lax.fori_loop(0, count, stats_step, start_stats)

    def block_probs(index, allowed, key_rows):
        scores = block_scores(index, key_rows)
        return jnp.where(allowed[None], jnp.exp(scores - peak[..., None]), 0.0) / denom[..., None]

    def output_step(index, carry):
        allowed = block_mask(index)

        def output_accumulate(state):
            probs_low = block_probs(index, allowed, all_keys).astype(jnp.bfloat16)
            return state + jnp.einsum(
                "hqk,khd->qhd",
                probs_low,
                block_rows(all_values, index),
                preferred_element_type=jnp.float32,
            )

        return lax.cond(jnp.any(allowed), output_accumulate, keep_state, carry)

    running = lax.fori_loop(0, count, output_step, jnp.zeros(split, jnp.float32))
    mixed = running.reshape(rows, local_width).astype(jnp.bfloat16)
    attn_out = lax.psum(
        jnp.dot(mixed, out_weight, preferred_element_type=jnp.float32).astype(jnp.bfloat16),
        "tensor",
    ).astype(jnp.float32)
    hidden = residual + attn_out
    normed_second, unit_second, scale_second = layer_parts(hidden, second_gain, second_shift)
    normed_second = normed_second.astype(jnp.bfloat16)
    upward = jnp.dot(normed_second, up_weight, preferred_element_type=jnp.float32) + up_bias
    active_full, gelu_pull = jax.vjp(gelu_tanh, upward)
    active = active_full.astype(jnp.bfloat16)
    mlp_out = (
        lax.psum(
            jnp.dot(active, down_weight, preferred_element_type=jnp.float32).astype(jnp.bfloat16),
            "tensor",
        ).astype(jnp.float32)
        + down_bias
    )
    block_value = hidden + mlp_out
    history_low = history[:, 0]
    next_value = (
        jnp.sum(mix_weights[:depth, None, None] * history_low.astype(jnp.float32), axis=0)
        + mix_weights[depth] * block_value
    )
    cot_low = cotangent_next[0]
    cot_next = cot_low.astype(jnp.float32)
    cot_block = cotangent_block[0].astype(jnp.float32)
    grad_history = (mix_weights[:depth, None, None] * cot_next[None]).astype(jnp.bfloat16)
    mix_terms = jnp.concatenate(
        [
            jnp.einsum("jsd,sd->j", history_low, cot_low, preferred_element_type=jnp.float32),
            jnp.sum(block_value * cot_next)[None],
        ]
    )
    grad_block = cot_block + mix_weights[depth] * cot_next
    grad_mlp = grad_block.astype(jnp.bfloat16)
    grad_down = jnp.einsum("sf,sd->fd", active, grad_mlp, preferred_element_type=jnp.float32)
    grad_active = jnp.einsum("sd,fd->sf", grad_mlp, down_weight, preferred_element_type=jnp.float32)
    grad_up = gelu_pull(grad_active)[0].astype(jnp.bfloat16)
    grad_upw = jnp.einsum("sd,sf->df", normed_second, grad_up, preferred_element_type=jnp.float32)
    grad_normed_second = lax.psum(
        jnp.einsum("sf,df->sd", grad_up, up_weight, preferred_element_type=jnp.float32).astype(
            jnp.bfloat16
        ),
        "tensor",
    ).astype(jnp.float32)
    grad_hidden = grad_block + norm_backward(
        grad_normed_second, unit_second, scale_second, second_gain
    )
    grad_attn = grad_hidden.astype(jnp.bfloat16)
    grad_outw = jnp.einsum("sk,sd->kd", mixed, grad_attn, preferred_element_type=jnp.float32)
    grad_mixed = (
        jnp.einsum("sd,kd->sk", grad_attn, out_weight, preferred_element_type=jnp.float32)
        .astype(jnp.bfloat16)
        .reshape(split)
    )
    back_keys, back_values = (
        lax.all_gather(keys, "seq", axis=0, tiled=True),
        lax.all_gather(values, "seq", axis=0, tiled=True),
    )

    def delta_step(index, carry):
        allowed = block_mask(index)

        def delta_accumulate(state):
            probs = block_probs(index, allowed, back_keys)
            grad_probs = jnp.einsum(
                "qhd,khd->hqk",
                grad_mixed,
                block_rows(back_values, index),
                preferred_element_type=jnp.float32,
            )
            return state + jnp.sum(probs * grad_probs, axis=-1)

        return lax.cond(jnp.any(allowed), delta_accumulate, keep_state, carry)

    delta = lax.fori_loop(0, count, delta_step, jnp.zeros((heads, rows), jnp.float32))

    def grad_step(index, carry):
        allowed = block_mask(index)

        def grad_accumulate(state):
            grad_queries, key_buffer, value_buffer = state
            key_rows = block_rows(back_keys, index)
            value_rows = block_rows(back_values, index)
            probs = block_probs(index, allowed, back_keys)
            grad_probs = jnp.einsum(
                "qhd,khd->hqk", grad_mixed, value_rows, preferred_element_type=jnp.float32
            )
            grad_scores = (probs * (grad_probs - delta[..., None])).astype(jnp.bfloat16)
            grad_queries = grad_queries + jnp.einsum(
                "hqk,khd->qhd", grad_scores, key_rows, preferred_element_type=jnp.float32
            )
            key_part = jnp.einsum(
                "hqk,qhd->khd", grad_scores, queries, preferred_element_type=jnp.float32
            ).reshape(size, local_width)
            value_part = jnp.einsum(
                "hqk,qhd->khd",
                probs.astype(jnp.bfloat16),
                grad_mixed,
                preferred_element_type=jnp.float32,
            ).reshape(size, local_width)
            key_buffer = lax.dynamic_update_slice_in_dim(key_buffer, key_part, index * size, 0)
            value_buffer = lax.dynamic_update_slice_in_dim(
                value_buffer, value_part, index * size, 0
            )
            return (grad_queries, key_buffer, value_buffer)

        return lax.cond(jnp.any(allowed), grad_accumulate, keep_state, carry)

    start_grads = (
        jnp.zeros(split, jnp.float32),
        jnp.zeros((total, local_width), jnp.float32),
        jnp.zeros((total, local_width), jnp.float32),
    )
    grad_queries, key_buffer, value_buffer = lax.fori_loop(0, count, grad_step, start_grads)
    grad_keys, grad_values = (
        lax.psum_scatter(
            key_buffer.astype(jnp.bfloat16), "seq", scatter_dimension=0, tiled=True
        ).astype(jnp.float32),
        lax.psum_scatter(
            value_buffer.astype(jnp.bfloat16), "seq", scatter_dimension=0, tiled=True
        ).astype(jnp.float32),
    )
    grad_query_lin = (
        rotate(grad_queries * 0.125, cosine, -sine).reshape(rows, local_width).astype(jnp.bfloat16)
    )
    grad_key_lin = (
        rotate(grad_keys.reshape(split), cosine, -sine)
        .reshape(rows, local_width)
        .astype(jnp.bfloat16)
    )
    grad_value_lin = grad_values.astype(jnp.bfloat16)
    grad_queryw = jnp.einsum(
        "sd,se->de", normed_first, grad_query_lin, preferred_element_type=jnp.float32
    )
    grad_keyw = jnp.einsum(
        "sd,se->de", normed_first, grad_key_lin, preferred_element_type=jnp.float32
    )
    grad_valuew = jnp.einsum(
        "sd,se->de", normed_first, grad_value_lin, preferred_element_type=jnp.float32
    )
    local_normed = jnp.einsum(
        "se,de->sd", grad_query_lin, query_weight, preferred_element_type=jnp.float32
    )
    local_normed = local_normed + jnp.einsum(
        "se,de->sd", grad_key_lin, key_weight, preferred_element_type=jnp.float32
    )
    local_normed = local_normed + jnp.einsum(
        "se,de->sd", grad_value_lin, value_weight, preferred_element_type=jnp.float32
    )
    grad_normed_first = lax.psum(local_normed.astype(jnp.bfloat16), "tensor").astype(jnp.float32)
    grad_input = grad_hidden + norm_backward(grad_normed_first, unit_first, scale_first, first_gain)
    shared_grads = (
        lax.psum_scatter(grad_queryw, ("seq", "batch"), scatter_dimension=0, tiled=True),
        lax.psum_scatter(grad_keyw, ("seq", "batch"), scatter_dimension=0, tiled=True),
        lax.psum_scatter(grad_valuew, ("seq", "batch"), scatter_dimension=0, tiled=True),
        lax.psum_scatter(grad_outw, ("seq", "batch"), scatter_dimension=1, tiled=True),
        lax.psum_scatter(grad_upw, ("seq", "batch"), scatter_dimension=0, tiled=True),
        lax.psum_scatter(grad_down, ("seq", "batch"), scatter_dimension=1, tiled=True),
    )
    square_terms = jnp.stack(
        [
            jnp.sum(block_value * block_value),
            jnp.sum(attn_out * attn_out),
            jnp.sum(mlp_out * mlp_out),
        ]
    )
    small_terms = lax.psum(
        (
            jnp.sum(grad_normed_first * unit_first, axis=0),
            jnp.sum(grad_normed_first, axis=0),
            jnp.sum(grad_normed_second * unit_second, axis=0),
            jnp.sum(grad_normed_second, axis=0),
            jnp.sum(grad_up.astype(jnp.float32), axis=0),
            jnp.sum(grad_mlp.astype(jnp.float32), axis=0),
            mix_terms,
            square_terms,
        ),
        ("seq", "batch"),
    )
    entries = float(lax.axis_size("batch") * total * width)
    rms_values = jnp.sqrt(small_terms[7] / entries)
    return (
        next_value.astype(jnp.bfloat16)[None],
        block_value.astype(jnp.bfloat16)[None],
        grad_input.astype(jnp.bfloat16)[None],
        grad_history[:, None],
        small_terms[0],
        small_terms[1],
        shared_grads[0],
        shared_grads[1],
        shared_grads[2],
        shared_grads[3],
        small_terms[2],
        small_terms[3],
        shared_grads[4],
        small_terms[4],
        shared_grads[5],
        small_terms[5],
        small_terms[6],
        rms_values,
    )


def solution(mesh):
    in_specs = (
        P("batch", "seq", None),
        P(None, "batch", "seq", None),
        P("batch", None),
        P(),
        P(),
        P(),
        P(None, "tensor"),
        P(None, "tensor"),
        P(None, "tensor"),
        P("tensor", None),
        P(),
        P(),
        P(None, "tensor"),
        P("tensor"),
        P("tensor", None),
        P(),
        P(),
        P("batch", "seq", None),
        P("batch", "seq", None),
    )
    out_specs = (
        P("batch", "seq", None),
        P("batch", "seq", None),
        P("batch", "seq", None),
        P(None, "batch", "seq", None),
        P(),
        P(),
        P(("seq", "batch"), "tensor"),
        P(("seq", "batch"), "tensor"),
        P(("seq", "batch"), "tensor"),
        P("tensor", ("seq", "batch")),
        P(),
        P(),
        P(("seq", "batch"), "tensor"),
        P("tensor"),
        P("tensor", ("seq", "batch")),
        P(),
        P(),
        P(),
    )
    return jax.shard_map(
        device_function(mesh), mesh=mesh, in_specs=in_specs, out_specs=out_specs, check_vma=False
    )
```

```python
import functools
from types import SimpleNamespace

import jax
import jax.numpy as jnp
from jax import lax
from jax.experimental import pallas as pl
from jax.experimental.pallas import tpu as pltpu
from jax.sharding import PartitionSpec as P

HEAD_DIM = 64
f32, bf16, i32 = jnp.float32, jnp.bfloat16, jnp.int32
MESH = pl.DeviceIdType.MESH


epsilon = 1e-05


def layer_parts(values, gain, shift):
    centre = jnp.mean(values, axis=-1, keepdims=True)
    centred = values - centre
    spread = jnp.mean(centred * centred, axis=-1, keepdims=True)
    inverse = lax.rsqrt(spread + epsilon)
    unit = centred * inverse
    return (unit * gain + shift, unit, inverse)


def norm_backward(grad_out, unit, inverse, gain):
    scaled = grad_out * gain
    return inverse * (
        scaled
        - jnp.mean(scaled, axis=-1, keepdims=True)
        - unit * jnp.mean(scaled * unit, axis=-1, keepdims=True)
    )


def gelu_tanh(values):
    return (
        0.5
        * values
        * (1.0 + jnp.tanh(0.7978845608028654 * (values + 0.044715 * values * values * values)))
    )


def rotate(values, cosine, sine):
    half = values.shape[-1] // 2
    first = values[..., :half]
    second = values[..., half:]
    return jnp.concatenate(
        [first * cosine - second * sine, second * cosine + first * sine], axis=-1
    )


def keep_state(state):
    return state


def dot(a, b, ca=1, cb=0):
    return lax.dot_general(a, b, (((ca,), (cb,)), ((), ())), preferred_element_type=f32)


def rope_tables(pos, half):
    index = lax.broadcasted_iota(i32, (half, 1), 0).astype(f32)
    rates = jnp.exp(-jnp.log(f32(10000.0)) * index / half)
    angles = rates * pos
    return jnp.cos(angles), jnp.sin(angles)


def rotate_t(lin, cosine, sine):
    width, rows = lin.shape
    parts = lin.reshape(width // HEAD_DIM, 2, HEAD_DIM // 2, rows)
    first, second = parts[:, 0], parts[:, 1]
    turned = [first * cosine - second * sine, second * cosine + first * sine]
    return jnp.stack(turned, axis=1).reshape(width, rows)


def gelu_both(u):
    square = u * u
    t = jnp.tanh(0.7978845608028654 * (u + 0.044715 * square * u))
    half = 0.5 * (1.0 + t)
    slope = half + 0.5 * u * (1.0 - t * t) * (0.7978845608028654 * (1.0 + 3 * 0.044715 * square))
    return u * half, slope


def row_chunks(rows, body, size=64):
    def step(i, _):
        body(pl.ds(pl.multiple_of(i * size, size), size))
        return 0

    lax.fori_loop(0, rows // size, step, 0)


def folded(rows):
    total = jnp.sum(rows, axis=0, keepdims=True)
    return sum(total[:, k : k + 128] for k in range(0, total.shape[1], 128))


ROWS, WIDTH, LOCAL, GROUP, HIDDEN, BLOCK = 256, 768, 384, 192, 1536, 48


def scratch_spec(windows):
    vm = pltpu.VMEM
    heads = (3, HEAD_DIM, ROWS)
    full32, full16, turned = vm((ROWS, WIDTH), f32), vm((ROWS, WIDTH), bf16), vm((WIDTH, ROWS), bf16)

    def job(columns):
        return [
            vm((2, 2, 2, 2, BLOCK, columns), bf16), vm((2, 2, 2, BLOCK, columns), bf16),
            vm((2, 2, BLOCK, columns), bf16), vm((2, BLOCK, columns), bf16), vm((BLOCK, columns), bf16),
        ]

    return dict(
        x=full16, gain1_v=vm((WIDTH,), f32), shift1_v=vm((WIDTH,), f32), gain2_v=vm((WIDTH,), f32), shift2_v=vm((WIDTH,), f32),
        downb_v=vm((WIDTH,), f32), upb_v=vm((HIDDEN,), f32), order=pltpu.SMEM((4,), i32), windows=pltpu.SMEM((windows,), i32), mixw=pltpu.SMEM((9,), f32),
        cotn=full16, cotb=full16, wq=vm((WIDTH, LOCAL), bf16), wk=vm((WIDTH, LOCAL), bf16), wv=vm((WIDTH, LOCAL), bf16),
        hist=vm((8, ROWS, WIDTH), bf16), wup=vm((WIDTH, HIDDEN), bf16), wdown=vm((HIDDEN, WIDTH), bf16),
        wof=vm((2, 2, 3, HEAD_DIM, WIDTH), bf16),
        vectors=vm((5, 1, WIDTH), f32), upb=vm((1, HIDDEN), f32), upsum=vm((1, HIDDEN), f32),
        qown=vm((2, *heads), bf16), kvown=vm((2, 3, 2, HEAD_DIM, ROWS), bf16),
        qt=vm((2, *heads), bf16), kv=vm((4, 3, 2, HEAD_DIM, ROWS), bf16),
        scores=vm((3, 2, 4, ROWS, ROWS), f32), bias=vm((2, 4, ROWS, ROWS), f32),
        peak=vm((3, 2, 1, ROWS), f32), denom=vm((3, 2, 1, ROWS), f32), acc=vm((3, 2, HEAD_DIM, ROWS), f32),
        delta=vm((3, 2, 1, ROWS), f32), cosine=vm((32, ROWS), f32), sine=vm((32, ROWS), f32),
        mix=vm((2, 2, *heads), bf16), mixout=vm(heads, bf16),
        unit1=full32, inv1=vm((ROWS, 1), f32), norm1=full16, norm1t=turned,
        hidden=full32, attn=full32, unit2=full32, inv2=vm((ROWS, 1), f32), norm2=full16, norm2t=turned,
        gblock=full32, gmlp=full16, gmlpt=turned, hacc=full32, gact=vm((ROWS, HIDDEN), f32),
        act=vm((ROWS, HIDDEN), bf16), gup=vm((ROWS, HIDDEN), bf16), gnorm2=full32, gnew=full32,
        ghid=vm((2, ROWS, WIDTH), bf16), mlp=vm((2, ROWS, WIDTH), bf16), gin=vm((2, ROWS, WIDTH), bf16),
        dpart=vm((2, 2, *heads), bf16), dsend=vm((2, 2, *heads), bf16), dout=vm((2, *heads), bf16),
        dkv=vm((4, 3, 2, HEAD_DIM, ROWS), bf16), dkvin=vm((4, 3, 2, HEAD_DIM, ROWS), bf16),
        dq=vm((3, HEAD_DIM, ROWS), f32), dqout=vm(heads, bf16), dqin=vm(heads, bf16),
        own0=vm((3, 2, HEAD_DIM, ROWS), f32), lin=vm((3, 2, *heads), bf16), gattnt=turned,
        small=vm((6, 16, WIDTH), f32), smallin=vm((5, 16, WIDTH), f32), last=vm((6, 16, 128), f32), lastin=vm((5, 16, 128), f32),
        job0=job(WIDTH), job1=job(WIDTH), job2=job(WIDTH), job3=job(WIDTH), job4=job(LOCAL), job5=job(640), job6=job(512),
        s_next=full16, s_block=full16, s_gin=full16, s_down=vm((BLOCK, HIDDEN), f32), s_up=vm((BLOCK, HIDDEN), f32),
        s_out=vm((BLOCK, LOCAL), f32), s_a=vm((BLOCK, 640), f32), s_b=vm((BLOCK, 512), f32), s_last=vm((16, 128), f32), s_small=vm((16, WIDTH), f32),
        osem=pltpu.SemaphoreType.DMA((12,)),
        ssem=pltpu.SemaphoreType.DMA((96,)), rsem=pltpu.SemaphoreType.DMA((96,)), lsem=pltpu.SemaphoreType.DMA((24,)),
    )


def layer_kernel(make, *refs):
    R = make(refs)
    z, b, y = lax.axis_index("seq"), lax.axis_index("batch"), lax.axis_index("tensor")
    near, flip, far = z + 1 - 2 * (z % 2), (z + 2) % 4, 3 - z
    m, p, xbit, core = z % 2, z // 2, b // 2, b % 2
    to_near, to_flip, to_far = dict(seq=near), dict(seq=flip), dict(seq=far)
    to_y, to_diag = dict(tensor=1 - y), dict(seq=near, tensor=1 - y)
    to_x, to_core = dict(batch=(b + 2) % 4), dict(batch=b + 1 - 2 * core)
    barrier = pltpu.get_barrier_semaphore()
    everyone = [to_near, to_flip, to_far, to_y, to_diag, to_x, to_core]
    for there in everyone:
        pl.semaphore_signal(barrier, inc=1, device_id=there, device_id_type=MESH)
    started = []

    def send(src, dst, there):
        i = len(started)
        copy = pltpu.make_async_remote_copy(
            src, dst, R.ssem.at[i], R.rsem.at[i], device_id=there, device_id_type=MESH
        )
        copy.start()
        started.append(copy)
        return copy

    def fetch(src, dst, i):
        copy = pltpu.make_async_copy(src, dst, R.lsem.at[i])
        copy.start()
        return copy

    get_small = [fetch(R.x_h, R.x, 9)]
    get_k = fetch(R.wk_h, R.wk, 1)
    pairs = [(R.gain1_in, R.gain1_v), (R.shift1_in, R.shift1_v), (R.order_in, R.order), (R.windows_in, R.windows)]
    pairs += [(R.gain2_in, R.gain2_v), (R.shift2_in, R.shift2_v), (R.downb_in, R.downb_v), (R.upb_in, R.upb_v)]
    pairs.append((R.mixw_in, R.mixw))
    for i, (src, dst) in enumerate(pairs):
        get_small.append(fetch(src, dst, 10 + i))
    get_q = fetch(R.wq_h, R.wq, 0)
    get_v = fetch(R.wv_h, R.wv, 2)
    written = []

    def write(src, dst):
        copy = pltpu.make_async_copy(src, dst, R.osem.at[len(written)])
        copy.start()
        written.append(copy)

    for c in get_small:
        c.wait()
    ends, total = [], 0
    for i in range(R.windows.shape[0]):
        total = total + R.windows[i]
        ends.append(total)
    for i, ref in enumerate((R.gain1_v, R.shift1_v, R.gain2_v, R.shift2_v, R.downb_v)):
        R.vectors[i] = ref[...][None]
    R.upb[...] = R.upb_v[...][None]
    R.gain1, R.shift1, R.gain2, R.shift2, R.downb = (R.vectors.at[i] for i in range(5))
    base = [R.order[k] * ROWS for k in (z, near, flip, far)]
    lane = lax.broadcasted_iota(i32, (1, ROWS), 1)

    def norm_first(rows):
        x = R.x[rows].astype(f32)
        centred = x - jnp.mean(x, axis=-1, keepdims=True)
        inverse = lax.rsqrt(jnp.mean(centred * centred, axis=-1, keepdims=True) + epsilon)
        unit = centred * inverse
        R.unit1[rows] = unit
        R.inv1[rows] = inverse
        R.norm1[rows] = (unit * R.gain1[...] + R.shift1[...]).astype(bf16)

    row_chunks(ROWS, norm_first)
    cosine, sine = rope_tables((base[0] + lane).astype(f32), HEAD_DIM // 2)
    R.cosine[...] = cosine
    R.sine[...] = sine
    split = (2, 3, HEAD_DIM, ROWS)
    get_k.wait()
    R.kvown[:, :, 0] = rotate_t(dot(R.norm1[...], R.wk[...]).T, cosine, sine).astype(bf16).reshape(split)
    get_v.wait()
    R.kvown[:, :, 1] = dot(R.norm1[...], R.wv[...]).T.astype(bf16).reshape(split)
    pl.semaphore_wait(barrier, len(everyone))
    near_in, flip_in, far_in = [], [], []

    def kv_out(h):
        near_in.append(send(R.kvown.at[1 - m, h], R.kv.at[1, h], to_near))
        flip_in.append(send(R.kvown.at[m, h], R.kv.at[2, h], to_flip))
        far_in.append(send(R.kvown.at[1 - m, h], R.kv.at[3, h], to_far))

    kv_out(0)
    get_q.wait()
    get_out = fetch(R.wout, R.wof.at[0], 5)
    get_cot = [fetch(R.cotn_h, R.cotn, 3), fetch(R.cotb_h, R.cotb, 4)]
    get_hist = fetch(R.history, R.hist, 6)
    get_down = fetch(R.wdown_h, R.wdown, 7)
    get_up = fetch(R.wup_h, R.wup, 8)
    queries = rotate_t(dot(R.norm1[...], R.wq[...]).T, cosine, sine) * 0.125
    R.qown[...] = queries.astype(bf16).reshape(split)
    q_in = [send(R.qown.at[1 - m, h], R.qt.at[1, h], to_near) for h in range(1)]
    kv_out(1)
    q_in.append(send(R.qown.at[1 - m, 1], R.qt.at[1, 1], to_near))
    kv_out(2)
    q_in.append(send(R.qown.at[1 - m, 2], R.qt.at[1, 2], to_near))
    get_out.wait()
    out_in = send(R.wof.at[0], R.wof.at[1], to_y)
    R.qt[0] = R.qown[m]
    R.kv[0] = R.kvown[m]

    for j in range(2):
        qpos = base[j] + lane
        start = 0 * qpos
        for end in ends:
            start = jnp.maximum(start, jnp.where(qpos >= end, end, 0))
        for r in range(4):
            kpos = base[r] + lax.broadcasted_iota(i32, (ROWS, ROWS), 0)
            R.bias[j, r] = jnp.where((kpos <= qpos) & (kpos >= start), 0.0, -1e30).astype(f32)
    for c in get_cot:
        c.wait()
    R.small[0] = jnp.zeros((16, WIDTH), f32)
    R.last[0] = jnp.zeros((16, 128), f32)
    mix_last = R.mixw[8]

    def block_grads(rows):
        g = R.cotb[rows].astype(f32) + mix_last * R.cotn[rows].astype(f32)
        R.gblock[rows] = g
        low = g.astype(bf16)
        R.gmlp[rows] = low
        R.small[0, 2:3] += 0.5 * jnp.sum(low.astype(f32), axis=0, keepdims=True)

    row_chunks(ROWS, block_grads)
    R.gmlpt[...] = R.gmlp[...].T
    R.norm1t[...] = R.norm1[...].T
    get_hist.wait()

    def history_sum(rows):
        cot = R.cotn[rows].astype(f32)
        total = 0
        for j in range(8):
            h = R.hist[j, rows].astype(f32)
            total = total + R.mixw[j] * h
            R.small[0, 3 + j // 6 : 4 + j // 6, 128 * (j % 6) : 128 * (j % 6) + 128] += 0.5 * folded(h * cot)
        R.hacc[rows] = total

    row_chunks(ROWS, history_sum, 32)
    get_down.wait()

    def active_grad(n, _):
        at = pl.ds(pl.multiple_of(256 * n, 256), 256)
        R.gact[:, at] = dot(R.gmlp[...], R.wdown[at], 1, 1)
        return 0

    lax.fori_loop(0, 6, active_grad, 0)

    def tile(h, j, r, first=False):
        s = dot(R.kv[r, h, 0], R.qt[j, h], 0, 0) + R.bias[j, r]
        R.scores[h, j, r] = s
        top = jnp.max(s, axis=0, keepdims=True)
        if first:
            e = jnp.exp(s - top)
            R.denom[h, j] = jnp.sum(e, axis=0, keepdims=True)
            R.acc[h, j] = dot(R.kv[r, h, 1], e.astype(bf16))
        else:
            old = R.peak[h, j]
            top = jnp.maximum(top, old)
            e = jnp.exp(s - top)
            alpha = jnp.exp(old - top)
            R.denom[h, j] = R.denom[h, j] * alpha + jnp.sum(e, axis=0, keepdims=True)
            R.acc[h, j] = R.acc[h, j] * alpha + dot(R.kv[r, h, 1], e.astype(bf16))
        R.peak[h, j] = top

    def finish(h, j):
        R.acc[h, j] = R.acc[h, j] * (1.0 / R.denom[h, j])
        R.peak[h, j] = R.peak[h, j] + jnp.log(R.denom[h, j])
        return R.acc[h, j].astype(bf16)

    mix_in = []
    for h in range(3):
        tile(h, 0, 0, True)
    for h in range(3):
        near_in[h].wait_recv()
        q_in[h].wait_recv()
        tile(h, 0, 1)
        tile(h, 1, 1, True)
        tile(h, 1, 0)
        flip_in[h].wait_recv()
        tile(h, 1, 2)
        tile(h, 0, 2)
        far_in[h].wait_recv()
        tile(h, 1, 3)
        tile(h, 0, 3)
        R.mixout[h] = finish(h, 1)
        R.mix[0, 0, h] = finish(h, 0)
        mix_in.append(send(R.mixout.at[h], R.mix.at[1, 1, h], to_diag))
        mix_in.append(send(R.mix.at[0, 0, h], R.mix.at[1, 0, h], to_y))
        mix_in.append(send(R.mixout.at[h], R.mix.at[0, 1, h], to_near))
    get_up.wait()
    out_in.wait_recv()
    for c in mix_in:
        c.wait_recv()
    group = (GROUP, ROWS)
    out = 0
    for t in range(2):
        for a in range(2):
            side = R.mix[(t + y) % 2, (a + m) % 2].reshape(group)
            out = out + dot(side, R.wof[(t + y) % 2, a].reshape(GROUP, WIDTH), 0, 0)
    R.attn[...] = out

    def norm_second(rows):
        hidden = R.x[rows].astype(f32) + R.attn[rows]
        R.hidden[rows] = hidden
        centred = hidden - jnp.mean(hidden, axis=-1, keepdims=True)
        inverse = lax.rsqrt(jnp.mean(centred * centred, axis=-1, keepdims=True) + epsilon)
        unit = centred * inverse
        R.unit2[rows] = unit
        R.inv2[rows] = inverse
        R.norm2[rows] = (unit * R.gain2[...] + R.shift2[...]).astype(bf16)

    bits = dict(core=core, x=xbit, near=m, flip=p)
    where = dict(core=to_core, x=to_x, near=to_near, flip=to_flip)
    place = dict(core=0, x=1, near=2, flip=3)

    class Job:
        def __init__(self, bufs, route):
            self.grads, self.landing, self.route, self.copy, self.step = bufs[0], bufs[1:], route, None, 0

        def put(self, value, columns):
            for k in range(16):
                at = tuple((k >> place[axis]) & 1 for axis in self.route)
                self.grads[(*at, slice(None), columns)] = value[BLOCK * k : BLOCK * k + BLOCK].astype(bf16)

        def mine(self):
            return tuple(bits[axis] for axis in self.route[: self.step])

        def push(self):
            axis = self.route[self.step]
            self.copy = send(self.grads.at[(*self.mine(), 1 - bits[axis])], self.landing[self.step], where[axis])

        def pull(self, out=None):
            self.copy.wait_recv()
            landing = self.landing[self.step]
            self.step += 1
            kept = self.mine()
            left = 4 - self.step

            def add(i, _):
                at = tuple((i // 2**k) % 2 for k in range(left))
                mine, theirs = self.grads[(*kept, *at)], landing[at if at else Ellipsis]
                if out is None:
                    self.grads[(*kept, *at)] = mine + theirs
                else:
                    out[...] = mine.astype(f32) + theirs.astype(f32)
                return 0

            if left:
                lax.fori_loop(0, 2**left, add, 0)
            else:
                add(0, 0)

        def turn(self):
            self.pull()
            self.push()

    usual = tuple(place)
    down0, down1, up0, up1 = (Job(bufs, usual) for bufs in (R.job0, R.job1, R.job2, R.job3))
    job_out, job_a = Job(R.job4, usual), Job(R.job5, usual)
    job_b = Job(R.job6, usual)

    row_chunks(ROWS, norm_second)
    for n in range(6):
        at = slice(256 * n, 256 * n + 256)
        u = dot(R.norm2[...], R.wup[:, at]) + R.upb[:, at]
        active, slope = gelu_both(u)
        R.act[:, at] = active.astype(bf16)
        grad = (R.gact[:, at] * slope).astype(bf16)
        R.gup[:, at] = grad
        R.upsum[:, at] = jnp.sum(grad.astype(f32), axis=0, keepdims=True)
        third = slice(256 * (n % 3), 256 * (n % 3) + 256)
        (down0, down1)[n // 3].put(dot(R.gmlpt[...], R.act[:, at]), third)
        if n == 2:
            down0.push()
            R.gnorm2[...] = dot(R.gup[:, :WIDTH], R.wup[:, :WIDTH], 1, 1)
    down1.push()
    R.gnorm2[...] += dot(R.gup[:, WIDTH:], R.wup[:, WIDTH:], 1, 1)

    def norm_back(grad, unit, inverse, gain):
        scaled = grad * gain
        return inverse * (
            scaled
            - jnp.mean(scaled, axis=-1, keepdims=True)
            - unit * jnp.mean(scaled * unit, axis=-1, keepdims=True)
        )

    def second_back(rows):
        back = norm_back(R.gnorm2[rows], R.unit2[rows], R.inv2[rows], R.gain2[...])
        R.ghid[0, rows] = (0.5 * R.gblock[rows] + back).astype(bf16)

    row_chunks(ROWS, second_back)
    d_in = []
    order = [(1, 1), (1, 0), (0, 1), (0, 0)]
    for h in range(3):
        weights = jnp.concatenate([R.wof[t, (a + m) % 2, h] for t, a in order], axis=0)
        parts = dot(weights, R.ghid[0], 1, 1).astype(bf16).reshape(4, HEAD_DIM, ROWS)
        for k in range(3):
            R.dsend[(*order[k], h)] = parts[k]
        R.dpart[0, 0, h] = parts[3]
        d_in.append(
            [
                send(R.dsend.at[1, 1, h], R.dpart.at[1, 1, h], to_diag),
                send(R.dsend.at[1, 0, h], R.dpart.at[0, 1, h], to_y),
                send(R.dsend.at[0, 1, h], R.dpart.at[1, 0, h], to_near),
            ]
        )
    ghid_in = send(R.ghid.at[0], R.ghid.at[1], to_y)

    class Sum:
        def __init__(self, held, landing, shared):
            self.held, self.landing, self.shared, self.step, self.copy = held, landing, shared, 0, None

        def push(self):
            there = (to_y, to_core, to_near, to_flip, to_x)[self.step]
            rows = pl.ds(0, self.shared if self.step == 0 else 16)
            self.copy = send(self.held.at[self.step, rows], self.landing.at[self.step, rows], there)

        def pull(self):
            self.copy.wait_recv()
            step, rows = self.step, self.shared if self.step == 0 else 16
            self.held[step + 1, 0:rows] = self.held[step, 0:rows] + self.landing[step, 0:rows]
            if rows < 16:
                self.held[step + 1, rows:16] = self.held[step, rows:16]
            self.step += 1

        def turn(self):
            self.pull()
            self.push()

    sums, last = Sum(R.small, R.smallin, 8), Sum(R.last, R.lastin, 16)

    kv_in, dq_in = [], []

    def back_head(h):
        for c in d_in[h]:
            c.wait_recv()
        for j in range(2):
            both = R.dpart[j, 0, h].astype(f32) + R.dpart[j, 1, h].astype(f32)
            R.dout[j, h] = both.astype(bf16)
            R.delta[h, j] = jnp.sum(R.dout[j, h].astype(f32) * R.acc[h, j], axis=0, keepdims=True)
        total = [0, 0]
        for r in (2, 3, 1, 0):
            dk, dv = 0, 0
            for j in range(2):
                probs = jnp.exp(R.scores[h, j, r] - R.peak[h, j])
                grad = dot(R.kv[r, h, 1], R.dout[j, h], 0, 0)
                low = (probs * (grad - R.delta[h, j])).astype(bf16)
                dv = dv + dot(R.dout[j, h], probs.astype(bf16), 1, 1)
                dk = dk + dot(R.qt[j, h], low, 1, 1)
                total[j] = total[j] + dot(R.kv[r, h, 0], low)
            if r:
                R.dkv[r, h, 0] = dk.astype(bf16)
                R.dkv[r, h, 1] = dv.astype(bf16)
                kv_in.append(send(R.dkv.at[r, h], R.dkvin.at[r, h], (to_near, to_flip, to_far)[r - 1]))
            else:
                R.own0[h, 0] = dk
                R.own0[h, 1] = dv
        R.dqout[h] = (0.125 * total[1]).astype(bf16)
        dq_in.append(send(R.dqout.at[h], R.dqin.at[h], to_near))
        R.dq[h] = 0.125 * total[0]

    def up_grads(job, k):
        for n in range(3):
            at = slice(WIDTH * k + 256 * n, WIDTH * k + 256 * n + 256)
            job.put(dot(R.norm2t[...], R.gup[:, at]), slice(256 * n, 256 * n + 256))
        job.push()

    down0.turn()
    R.norm2t[...] = R.norm2[...].T
    up_grads(up0, 0)
    down1.turn()
    back_head(0)
    up_grads(up1, 1)
    back_head(1)
    up0.turn()
    back_head(2)
    up1.turn()
    down0.turn()
    R.mlp[0] = dot(R.act[...], R.wdown[...]).astype(bf16)
    mlp_in = send(R.mlp.at[0], R.mlp.at[1], to_y)

    ghid_in.wait_recv()

    def whole_hidden(rows):
        hid = R.ghid[0, rows].astype(f32) + R.ghid[1, rows].astype(f32)
        R.gblock[rows] = hid
        R.gmlp[rows] = hid.astype(bf16)
        back = R.gnorm2[rows]
        R.small[0, 0:1] += jnp.sum(back * R.unit2[rows], axis=0, keepdims=True)
        R.small[0, 1:2] += jnp.sum(back, axis=0, keepdims=True)

    row_chunks(ROWS, whole_hidden)
    R.gattnt[...] = R.gmlp[...].T
    mixed = jnp.concatenate([R.mix[0, (a + m) % 2].reshape(group) for a in range(2)], axis=0)
    job_out.put(dot(R.gattnt[...], mixed, 1, 1), slice(None))
    job_out.push()
    down1.turn()
    job_out.turn()

    up0.turn()
    down0.turn()

    mlp_in.wait_recv()

    def block_out(rows):
        both = R.mlp[0, rows].astype(f32) + R.mlp[1, rows].astype(f32) + R.downb[...]
        value = R.hidden[rows] + both
        R.s_block[rows] = value.astype(bf16)
        R.s_next[rows] = (R.hacc[rows] + mix_last * value).astype(bf16)
        attn = R.attn[rows]
        for k, term in enumerate((value * R.cotn[rows].astype(f32), value * value, attn * attn, both * both)):
            R.small[0, 4:5, 128 * (2 + k) : 128 * (3 + k)] += 0.5 * folded(term)

    row_chunks(ROWS, block_out, 32)
    for k in range(8):
        R.small[0, 10 + k // 6 : 11 + k // 6, 128 * (k % 6) : 128 * (k % 6) + 128] = jnp.full((1, 128), R.mixw[k], f32)
    write(R.s_block, R.o_block)
    write(R.s_next, R.o_next)
    R.small[0, 8:9] = R.upsum[:, :WIDTH]
    R.small[0, 9:10] = R.upsum[:, WIDTH:]

    sums.push()

    cosine, sine = R.cosine[...], -R.sine[...]
    for h in range(3):
        for c in (*kv_in[3 * h : 3 * h + 3], dq_in[h]):
            c.wait_recv()
        for k in range(2):
            ours = R.own0[h, k] + R.dkvin[2, h, k].astype(f32)
            theirs = R.dkvin[1, h, k].astype(f32) + R.dkvin[3, h, k].astype(f32)
            if k == 0:
                ours, theirs = rotate_t(ours, cosine, sine), rotate_t(theirs, cosine, sine)
            R.lin[1 + k, m, h] = ours.astype(bf16)
            R.lin[1 + k, 1 - m, h] = theirs.astype(bf16)
        R.lin[0, m, h] = rotate_t(R.dq[h], cosine, sine).astype(bf16)
        R.lin[0, 1 - m, h] = rotate_t(R.dqin[h].astype(f32), cosine, sine).astype(bf16)
    lins = [R.lin[k].reshape(LOCAL, ROWS) for k in range(3)]
    first = dot(R.wq[...], lins[0]) + dot(R.wk[...], lins[1]) + dot(R.wv[...], lins[2])
    R.gnew[...] = first.T

    def first_back(rows):
        grad = R.gnew[rows]
        R.gin[0, rows] = norm_back(grad, R.unit1[rows], R.inv1[rows], R.gain1[...]).astype(bf16)
        for i, term in enumerate((grad * R.unit1[rows], grad)):
            total = jnp.sum(term, axis=0, keepdims=True)
            for k in range(6):
                R.last[0, 6 * i + k : 6 * i + k + 1] += total[:, 128 * k : 128 * k + 128]

    row_chunks(ROWS, first_back)
    last.push()
    gin_in = send(R.gin.at[0], R.gin.at[1], to_y)
    every = jnp.concatenate(lins, axis=0)
    job_a.put(dot(R.norm1t[...], every[:640], 1, 1), slice(None))
    job_a.push()
    job_b.put(dot(R.norm1t[...], every[640:], 1, 1), slice(None))
    job_b.push()
    sums.turn()
    up1.turn()
    down1.turn()
    last.turn()
    sums.turn()
    job_a.turn()
    job_b.turn()
    last.turn()
    job_out.turn()
    up0.turn()
    down0.pull(R.s_down.at[:, pl.ds(0, WIDTH)])
    down1.pull(R.s_down.at[:, pl.ds(WIDTH, WIDTH)])
    write(R.s_down, R.o_down)
    sums.turn()
    last.turn()
    up1.turn()
    gin_in.wait_recv()

    def grad_in(rows):
        both = R.gin[0, rows].astype(f32) + R.gin[1, rows].astype(f32)
        R.s_gin[rows] = (R.gblock[rows] + both).astype(bf16)

    row_chunks(ROWS, grad_in)
    write(R.s_gin, R.o_gin)
    job_a.turn()
    job_out.turn()
    sums.turn()
    last.turn()
    job_b.turn()
    up0.pull(R.s_up.at[:, pl.ds(0, WIDTH)])
    up1.pull(R.s_up.at[:, pl.ds(WIDTH, WIDTH)])
    write(R.s_up, R.o_up)
    job_a.turn()
    job_b.turn()
    job_out.pull(R.s_out)
    write(R.s_out, R.o_out)
    sums.pull()
    R.s_small[...] = R.small[5]
    R.s_small[10:12] = R.small[0, 10:12]
    write(R.s_small, R.o_small)
    last.pull()
    R.s_last[...] = R.last[5]
    write(R.s_last, R.o_last)
    job_a.pull(R.s_a)
    write(R.s_a, R.o_a)
    job_b.pull(R.s_b)
    write(R.s_b, R.o_b)
    for c in started:
        c.wait_send()
    for c in written:
        c.wait()


def last_kernel(make, entries, *refs):
    R = make(refs)
    copies = []

    def copy(src, dst):
        moving = pltpu.make_async_copy(src, dst, R.sems.at[len(copies)])
        moving.start()
        copies.append(moving)
        return moving

    get_cot = [copy(R.cotn, R.v_cotn), copy(R.o_small, R.v_small), copy(R.o_last, R.v_last)]
    pairs = [(R.o_next, R.v_next, R.next.at[0]), (R.o_block, R.v_block, R.block.at[0])]
    pairs += [(R.o_gin, R.v_gin, R.gin.at[0]), (R.o_up, R.v_up, R.gup), (R.o_down, R.v_down, R.gdown)]
    pairs.append((R.o_out, R.v_out, R.gout))
    loads = [copy(src, dst) for src, dst, _ in pairs]
    loads += [copy(R.o_a, R.v_a), copy(R.o_b, R.v_b)]
    for c in get_cot:
        c.wait()
    count = len(copies)
    for j in range(8):
        weight = R.v_small[10 + j // 6 : 11 + j // 6, 128 * (j % 6) : 128 * (j % 6) + 1]
        R.v_hist[j] = (weight * R.v_cotn[...].astype(f32)).astype(bf16)
        copy(R.v_hist.at[j], R.ghist.at[j, 0])
    for c, (_, held, out) in zip(loads, pairs):
        c.wait()
        copy(held, out)
    loads[-2].wait()
    loads[-1].wait()
    copy(R.v_a.at[:, pl.ds(0, LOCAL)], R.gq)
    copy(R.v_a.at[:, pl.ds(LOCAL, 256)], R.gk.at[:, pl.ds(0, 256)])
    copy(R.v_b.at[:, pl.ds(0, 128)], R.gk.at[:, pl.ds(256, 128)])
    copy(R.v_b.at[:, pl.ds(128, LOCAL)], R.gv)
    for k in range(6):
        R.v_gain1[128 * k : 128 * k + 128] = R.v_last[k]
        R.v_shift1[128 * k : 128 * k + 128] = R.v_last[6 + k]
    for i, ref in enumerate((R.v_gain2, R.v_shift2, R.v_downb)):
        ref[...] = R.v_small[i]
    copy(R.v_gain1, R.gain1)
    copy(R.v_shift1, R.shift1)
    copy(R.v_gain2, R.gain2)
    copy(R.v_shift2, R.shift2)
    copy(R.v_downb, R.downb)
    R.v_upb[0:WIDTH] = R.v_small[8]
    R.v_upb[WIDTH:HIDDEN] = R.v_small[9]
    copy(R.v_upb, R.upb)
    parts = [R.v_small[3 + k // 6 : 4 + k // 6, 128 * (k % 6) : 128 * (k % 6) + 128] for k in range(12)]
    sums = jnp.sum(jnp.concatenate(parts, axis=0), axis=1, keepdims=True)
    row = jnp.broadcast_to(sums, (12, 128)).T[0:1]
    R.v_gmix[...] = row[0, :9]
    R.v_rms[...] = jnp.sqrt(row / entries)[0, 9:]
    copy(R.v_gmix, R.gmix)
    copy(R.v_rms, R.rms)
    for c in copies[count:]:
        c.wait()


def out_spec(shape, dtype=f32):
    return jax.ShapeDtypeStruct(shape, dtype)


def namer(*groups):
    names = [name for group in groups for name in group]
    return lambda refs: SimpleNamespace(**dict(zip(names, refs)))


def per_device_block(
    inputs,
    history,
    window_lengths,
    block_order,
    first_gain,
    first_shift,
    query_weight,
    key_weight,
    value_weight,
    out_weight,
    second_gain,
    second_shift,
    up_weight,
    up_bias,
    down_weight,
    down_bias,
    mix_weights,
    cotangent_next,
    cotangent_block,
):
    hbm = pl.BlockSpec(memory_space=pl.ANY)
    args = dict(
        x_h=inputs[0], gain1_in=first_gain, shift1_in=first_shift, gain2_in=second_gain, shift2_in=second_shift,
        upb_in=up_bias, downb_in=down_bias,
        cotn_h=cotangent_next[0], cotb_h=cotangent_block[0], wq_h=query_weight, wk_h=key_weight, wv_h=value_weight,
        wout=out_weight.reshape(2, 3, HEAD_DIM, WIDTH), history=history[:, 0], wup_h=up_weight, wdown_h=down_weight,
        windows_in=window_lengths[0], order_in=block_order, mixw_in=mix_weights,
    )
    specs = [hbm] * len(args)
    outs = dict(
        o_next=out_spec((ROWS, WIDTH), bf16), o_block=out_spec((ROWS, WIDTH), bf16), o_gin=out_spec((ROWS, WIDTH), bf16),
        o_down=out_spec((BLOCK, HIDDEN)), o_up=out_spec((BLOCK, HIDDEN)), o_out=out_spec((BLOCK, LOCAL)),
        o_a=out_spec((BLOCK, 640)), o_b=out_spec((BLOCK, 512)), o_small=out_spec((16, WIDTH)), o_last=out_spec((16, 128)),
    )
    scratch = scratch_spec(window_lengths.shape[1])
    flat, names = [], []
    for name, spec in scratch.items():
        several = isinstance(spec, list)
        names.append((name, len(spec) if several else 0))
        flat.extend(spec if several else [spec])

    def make(refs):
        R, k = dict(zip([*args, *outs], refs)), len(args) + len(outs)
        for name, count in names:
            R[name] = refs[k : k + count] if count else refs[k]
            k += max(count, 1)
        return SimpleNamespace(**R)

    held = pl.pallas_call(
        functools.partial(layer_kernel, make),
        out_shape=list(outs.values()),
        in_specs=specs,
        out_specs=[hbm] * len(outs),
        scratch_shapes=flat,
        compiler_params=pltpu.CompilerParams(
            collective_id=1, has_side_effects=True, vmem_limit_bytes=63 * 2**20
        ),
    )(*args.values())
    held = dict(zip(outs, held))
    rows3 = (1, ROWS, WIDTH)
    results = dict(
        next=out_spec(rows3, bf16), block=out_spec(rows3, bf16), gin=out_spec(rows3, bf16),
        ghist=out_spec((8, *rows3), bf16), gain1=out_spec((WIDTH,)), shift1=out_spec((WIDTH,)),
        gq=out_spec((BLOCK, LOCAL)), gk=out_spec((BLOCK, LOCAL)), gv=out_spec((BLOCK, LOCAL)),
        gout=out_spec((BLOCK, LOCAL)), gain2=out_spec((WIDTH,)), shift2=out_spec((WIDTH,)),
        gup=out_spec((BLOCK, HIDDEN)), upb=out_spec((HIDDEN,)), gdown=out_spec((BLOCK, HIDDEN)),
        downb=out_spec((WIDTH,)), gmix=out_spec((9,)), rms=out_spec((3,)),
    )
    entries = float(lax.axis_size("batch") * lax.axis_size("seq") * ROWS * WIDTH)
    given = dict(cotn=cotangent_next[0], **held)
    vm, full, row = pltpu.VMEM, pltpu.VMEM((ROWS, WIDTH), bf16), pltpu.VMEM((WIDTH,), f32)
    staging = dict(
        v_cotn=full, v_hist=vm((8, ROWS, WIDTH), bf16), v_next=full, v_block=full, v_gin=full,
        v_up=vm((BLOCK, HIDDEN), f32), v_down=vm((BLOCK, HIDDEN), f32), v_out=vm((BLOCK, LOCAL), f32),
        v_a=vm((BLOCK, 640), f32), v_b=vm((BLOCK, 512), f32), v_small=vm((16, WIDTH), f32), v_last=vm((16, 128), f32),
        v_gain1=row, v_shift1=row, v_gain2=row, v_shift2=row, v_downb=row, v_upb=vm((HIDDEN,), f32),
        v_gmix=vm((9,), f32), v_rms=vm((3,), f32), sems=pltpu.SemaphoreType.DMA((40,)),
    )
    done = pl.pallas_call(
        functools.partial(last_kernel, namer(given, results, staging), entries),
        out_shape=list(results.values()),
        in_specs=[hbm] * len(given),
        out_specs=[hbm] * len(results),
        scratch_shapes=list(staging.values()),
        compiler_params=pltpu.CompilerParams(vmem_limit_bytes=63 * 2**20),
    )(*given.values())
    done = dict(zip(results, done))
    turned = dict(gout=done[list(results)[9]].T, gdown=done[list(results)[14]].T)
    return tuple((done | turned).values())


def device_function(mesh):
    return per_device_block if mesh.shape["seq"] == 4 else per_device_general


def per_device_general(
    inputs,
    history,
    window_lengths,
    block_order,
    first_gain,
    first_shift,
    query_weight,
    key_weight,
    value_weight,
    out_weight,
    second_gain,
    second_shift,
    up_weight,
    up_bias,
    down_weight,
    down_bias,
    mix_weights,
    cotangent_next,
    cotangent_block,
):
    rows = inputs.shape[1]
    width = inputs.shape[2]
    local_width = query_weight.shape[1]
    heads = local_width // HEAD_DIM
    half = HEAD_DIM // 2
    depth = history.shape[0]
    total = rows * lax.axis_size("seq")
    size = min(1024, total)
    count = total // size
    split = (rows, heads, HEAD_DIM)
    offsets = jnp.arange(rows, dtype=jnp.int32)
    own_pos = block_order[lax.axis_index("seq")] * rows + offsets
    every_row = jnp.arange(total, dtype=jnp.int32)
    every_pos = block_order[every_row // rows] * rows + every_row % rows
    ends = jnp.cumsum(window_lengths[0])
    own_docs = jnp.sum((own_pos[:, None] >= ends[None, :]).astype(jnp.int32), axis=1)
    every_docs = jnp.sum((every_pos[:, None] >= ends[None, :]).astype(jnp.int32), axis=1)
    rates = jnp.exp(-jnp.log(10000.0) * jnp.arange(half, dtype=jnp.float32) / half)
    angles = own_pos.astype(jnp.float32)[:, None] * rates[None, :]
    cosine = jnp.cos(angles)[:, None, :]
    sine = jnp.sin(angles)[:, None, :]
    residual = inputs[0].astype(jnp.float32)
    normed_first, unit_first, scale_first = layer_parts(residual, first_gain, first_shift)
    normed_first = normed_first.astype(jnp.bfloat16)
    query_lin = jnp.dot(normed_first, query_weight, preferred_element_type=jnp.float32)
    key_lin = jnp.dot(normed_first, key_weight, preferred_element_type=jnp.float32)
    value_lin = jnp.dot(normed_first, value_weight, preferred_element_type=jnp.float32)
    queries = (rotate(query_lin.reshape(split), cosine, sine) * 0.125).astype(jnp.bfloat16)
    keys = (
        rotate(key_lin.reshape(split), cosine, sine).reshape(rows, local_width).astype(jnp.bfloat16)
    )
    values = value_lin.astype(jnp.bfloat16)
    all_keys, all_values = (
        lax.all_gather(keys, "seq", axis=0, tiled=True),
        lax.all_gather(values, "seq", axis=0, tiled=True),
    )

    def block_mask(index):
        key_pos = lax.dynamic_slice_in_dim(every_pos, index * size, size)
        key_docs = lax.dynamic_slice_in_dim(every_docs, index * size, size)
        return (key_pos[None, :] <= own_pos[:, None]) & (key_docs[None, :] == own_docs[:, None])

    def block_rows(array, index):
        return lax.dynamic_slice_in_dim(array, index * size, size).reshape(size, heads, HEAD_DIM)

    def block_scores(index, key_rows):
        return jnp.einsum(
            "qhd,khd->hqk", queries, block_rows(key_rows, index), preferred_element_type=jnp.float32
        )

    def stats_step(index, carry):
        allowed = block_mask(index)

        def update(state):
            peak, denom = state
            masked = jnp.where(allowed[None], block_scores(index, all_keys), -1e30)
            fresh = jnp.maximum(peak, jnp.max(masked, axis=-1))
            weights = jnp.where(allowed[None], jnp.exp(masked - fresh[..., None]), 0.0)
            return (fresh, denom * jnp.exp(peak - fresh) + jnp.sum(weights, axis=-1))

        return lax.cond(jnp.any(allowed), update, keep_state, carry)

    start_stats = (
        jnp.full((heads, rows), -1e30, jnp.float32),
        jnp.zeros((heads, rows), jnp.float32),
    )
    peak, denom = lax.fori_loop(0, count, stats_step, start_stats)

    def block_probs(index, allowed, key_rows):
        scores = block_scores(index, key_rows)
        return jnp.where(allowed[None], jnp.exp(scores - peak[..., None]), 0.0) / denom[..., None]

    def output_step(index, carry):
        allowed = block_mask(index)

        def output_accumulate(state):
            probs_low = block_probs(index, allowed, all_keys).astype(jnp.bfloat16)
            return state + jnp.einsum(
                "hqk,khd->qhd",
                probs_low,
                block_rows(all_values, index),
                preferred_element_type=jnp.float32,
            )

        return lax.cond(jnp.any(allowed), output_accumulate, keep_state, carry)

    running = lax.fori_loop(0, count, output_step, jnp.zeros(split, jnp.float32))
    mixed = running.reshape(rows, local_width).astype(jnp.bfloat16)
    attn_out = lax.psum(
        jnp.dot(mixed, out_weight, preferred_element_type=jnp.float32).astype(jnp.bfloat16),
        "tensor",
    ).astype(jnp.float32)
    hidden = residual + attn_out
    normed_second, unit_second, scale_second = layer_parts(hidden, second_gain, second_shift)
    normed_second = normed_second.astype(jnp.bfloat16)
    upward = jnp.dot(normed_second, up_weight, preferred_element_type=jnp.float32) + up_bias
    active_full, gelu_pull = jax.vjp(gelu_tanh, upward)
    active = active_full.astype(jnp.bfloat16)
    mlp_out = (
        lax.psum(
            jnp.dot(active, down_weight, preferred_element_type=jnp.float32).astype(jnp.bfloat16),
            "tensor",
        ).astype(jnp.float32)
        + down_bias
    )
    block_value = hidden + mlp_out
    history_low = history[:, 0]
    next_value = (
        jnp.sum(mix_weights[:depth, None, None] * history_low.astype(jnp.float32), axis=0)
        + mix_weights[depth] * block_value
    )
    cot_low = cotangent_next[0]
    cot_next = cot_low.astype(jnp.float32)
    cot_block = cotangent_block[0].astype(jnp.float32)
    grad_history = (mix_weights[:depth, None, None] * cot_next[None]).astype(jnp.bfloat16)
    mix_terms = jnp.concatenate(
        [
            jnp.einsum("jsd,sd->j", history_low, cot_low, preferred_element_type=jnp.float32),
            jnp.sum(block_value * cot_next)[None],
        ]
    )
    grad_block = cot_block + mix_weights[depth] * cot_next
    grad_mlp = grad_block.astype(jnp.bfloat16)
    grad_down = jnp.einsum("sf,sd->fd", active, grad_mlp, preferred_element_type=jnp.float32)
    grad_active = jnp.einsum("sd,fd->sf", grad_mlp, down_weight, preferred_element_type=jnp.float32)
    grad_up = gelu_pull(grad_active)[0].astype(jnp.bfloat16)
    grad_upw = jnp.einsum("sd,sf->df", normed_second, grad_up, preferred_element_type=jnp.float32)
    grad_normed_second = lax.psum(
        jnp.einsum("sf,df->sd", grad_up, up_weight, preferred_element_type=jnp.float32).astype(
            jnp.bfloat16
        ),
        "tensor",
    ).astype(jnp.float32)
    grad_hidden = grad_block + norm_backward(
        grad_normed_second, unit_second, scale_second, second_gain
    )
    grad_attn = grad_hidden.astype(jnp.bfloat16)
    grad_outw = jnp.einsum("sk,sd->kd", mixed, grad_attn, preferred_element_type=jnp.float32)
    grad_mixed = (
        jnp.einsum("sd,kd->sk", grad_attn, out_weight, preferred_element_type=jnp.float32)
        .astype(jnp.bfloat16)
        .reshape(split)
    )
    back_keys, back_values = (
        lax.all_gather(keys, "seq", axis=0, tiled=True),
        lax.all_gather(values, "seq", axis=0, tiled=True),
    )

    def delta_step(index, carry):
        allowed = block_mask(index)

        def delta_accumulate(state):
            probs = block_probs(index, allowed, back_keys)
            grad_probs = jnp.einsum(
                "qhd,khd->hqk",
                grad_mixed,
                block_rows(back_values, index),
                preferred_element_type=jnp.float32,
            )
            return state + jnp.sum(probs * grad_probs, axis=-1)

        return lax.cond(jnp.any(allowed), delta_accumulate, keep_state, carry)

    delta = lax.fori_loop(0, count, delta_step, jnp.zeros((heads, rows), jnp.float32))

    def grad_step(index, carry):
        allowed = block_mask(index)

        def grad_accumulate(state):
            grad_queries, key_buffer, value_buffer = state
            key_rows = block_rows(back_keys, index)
            value_rows = block_rows(back_values, index)
            probs = block_probs(index, allowed, back_keys)
            grad_probs = jnp.einsum(
                "qhd,khd->hqk", grad_mixed, value_rows, preferred_element_type=jnp.float32
            )
            grad_scores = (probs * (grad_probs - delta[..., None])).astype(jnp.bfloat16)
            grad_queries = grad_queries + jnp.einsum(
                "hqk,khd->qhd", grad_scores, key_rows, preferred_element_type=jnp.float32
            )
            key_part = jnp.einsum(
                "hqk,qhd->khd", grad_scores, queries, preferred_element_type=jnp.float32
            ).reshape(size, local_width)
            value_part = jnp.einsum(
                "hqk,qhd->khd",
                probs.astype(jnp.bfloat16),
                grad_mixed,
                preferred_element_type=jnp.float32,
            ).reshape(size, local_width)
            key_buffer = lax.dynamic_update_slice_in_dim(key_buffer, key_part, index * size, 0)
            value_buffer = lax.dynamic_update_slice_in_dim(
                value_buffer, value_part, index * size, 0
            )
            return (grad_queries, key_buffer, value_buffer)

        return lax.cond(jnp.any(allowed), grad_accumulate, keep_state, carry)

    start_grads = (
        jnp.zeros(split, jnp.float32),
        jnp.zeros((total, local_width), jnp.float32),
        jnp.zeros((total, local_width), jnp.float32),
    )
    grad_queries, key_buffer, value_buffer = lax.fori_loop(0, count, grad_step, start_grads)
    grad_keys, grad_values = (
        lax.psum_scatter(
            key_buffer.astype(jnp.bfloat16), "seq", scatter_dimension=0, tiled=True
        ).astype(jnp.float32),
        lax.psum_scatter(
            value_buffer.astype(jnp.bfloat16), "seq", scatter_dimension=0, tiled=True
        ).astype(jnp.float32),
    )
    grad_query_lin = (
        rotate(grad_queries * 0.125, cosine, -sine).reshape(rows, local_width).astype(jnp.bfloat16)
    )
    grad_key_lin = (
        rotate(grad_keys.reshape(split), cosine, -sine)
        .reshape(rows, local_width)
        .astype(jnp.bfloat16)
    )
    grad_value_lin = grad_values.astype(jnp.bfloat16)
    grad_queryw = jnp.einsum(
        "sd,se->de", normed_first, grad_query_lin, preferred_element_type=jnp.float32
    )
    grad_keyw = jnp.einsum(
        "sd,se->de", normed_first, grad_key_lin, preferred_element_type=jnp.float32
    )
    grad_valuew = jnp.einsum(
        "sd,se->de", normed_first, grad_value_lin, preferred_element_type=jnp.float32
    )
    local_normed = jnp.einsum(
        "se,de->sd", grad_query_lin, query_weight, preferred_element_type=jnp.float32
    )
    local_normed = local_normed + jnp.einsum(
        "se,de->sd", grad_key_lin, key_weight, preferred_element_type=jnp.float32
    )
    local_normed = local_normed + jnp.einsum(
        "se,de->sd", grad_value_lin, value_weight, preferred_element_type=jnp.float32
    )
    grad_normed_first = lax.psum(local_normed.astype(jnp.bfloat16), "tensor").astype(jnp.float32)
    grad_input = grad_hidden + norm_backward(grad_normed_first, unit_first, scale_first, first_gain)
    shared_grads = (
        lax.psum_scatter(grad_queryw, ("seq", "batch"), scatter_dimension=0, tiled=True),
        lax.psum_scatter(grad_keyw, ("seq", "batch"), scatter_dimension=0, tiled=True),
        lax.psum_scatter(grad_valuew, ("seq", "batch"), scatter_dimension=0, tiled=True),
        lax.psum_scatter(grad_outw, ("seq", "batch"), scatter_dimension=1, tiled=True),
        lax.psum_scatter(grad_upw, ("seq", "batch"), scatter_dimension=0, tiled=True),
        lax.psum_scatter(grad_down, ("seq", "batch"), scatter_dimension=1, tiled=True),
    )
    square_terms = jnp.stack(
        [
            jnp.sum(block_value * block_value),
            jnp.sum(attn_out * attn_out),
            jnp.sum(mlp_out * mlp_out),
        ]
    )
    small_terms = lax.psum(
        (
            jnp.sum(grad_normed_first * unit_first, axis=0),
            jnp.sum(grad_normed_first, axis=0),
            jnp.sum(grad_normed_second * unit_second, axis=0),
            jnp.sum(grad_normed_second, axis=0),
            jnp.sum(grad_up.astype(jnp.float32), axis=0),
            jnp.sum(grad_mlp.astype(jnp.float32), axis=0),
            mix_terms,
            square_terms,
        ),
        ("seq", "batch"),
    )
    entries = float(lax.axis_size("batch") * total * width)
    rms_values = jnp.sqrt(small_terms[7] / entries)
    return (
        next_value.astype(jnp.bfloat16)[None],
        block_value.astype(jnp.bfloat16)[None],
        grad_input.astype(jnp.bfloat16)[None],
        grad_history[:, None],
        small_terms[0],
        small_terms[1],
        shared_grads[0],
        shared_grads[1],
        shared_grads[2],
        shared_grads[3],
        small_terms[2],
        small_terms[3],
        shared_grads[4],
        small_terms[4],
        shared_grads[5],
        small_terms[5],
        small_terms[6],
        rms_values,
    )


def solution(mesh):
    in_specs = (
        P("batch", "seq", None),
        P(None, "batch", "seq", None),
        P("batch", None),
        P(),
        P(),
        P(),
        P(None, "tensor"),
        P(None, "tensor"),
        P(None, "tensor"),
        P("tensor", None),
        P(),
        P(),
        P(None, "tensor"),
        P("tensor"),
        P("tensor", None),
        P(),
        P(),
        P("batch", "seq", None),
        P("batch", "seq", None),
    )
    out_specs = (
        P("batch", "seq", None),
        P("batch", "seq", None),
        P("batch", "seq", None),
        P(None, "batch", "seq", None),
        P(),
        P(),
        P(("seq", "batch"), "tensor"),
        P(("seq", "batch"), "tensor"),
        P(("seq", "batch"), "tensor"),
        P("tensor", ("seq", "batch")),
        P(),
        P(),
        P(("seq", "batch"), "tensor"),
        P("tensor"),
        P("tensor", ("seq", "batch")),
        P(),
        P(),
        P(),
    )
    return jax.shard_map(
        device_function(mesh), mesh=mesh, in_specs=in_specs, out_specs=out_specs, check_vma=False
    )
```

```python
import functools
from types import SimpleNamespace

import jax
import jax.numpy as jnp
from jax import lax
from jax.experimental import pallas as pl
from jax.experimental.pallas import tpu as pltpu
from jax.sharding import PartitionSpec as P

HEAD_DIM = 64
f32, bf16, i32 = jnp.float32, jnp.bfloat16, jnp.int32
MESH = pl.DeviceIdType.MESH


epsilon = 1e-05


def layer_parts(values, gain, shift):
    centre = jnp.mean(values, axis=-1, keepdims=True)
    centred = values - centre
    spread = jnp.mean(centred * centred, axis=-1, keepdims=True)
    inverse = lax.rsqrt(spread + epsilon)
    unit = centred * inverse
    return (unit * gain + shift, unit, inverse)


def norm_backward(grad_out, unit, inverse, gain):
    scaled = grad_out * gain
    return inverse * (
        scaled
        - jnp.mean(scaled, axis=-1, keepdims=True)
        - unit * jnp.mean(scaled * unit, axis=-1, keepdims=True)
    )


def gelu_tanh(values):
    return (
        0.5
        * values
        * (1.0 + jnp.tanh(0.7978845608028654 * (values + 0.044715 * values * values * values)))
    )


def rotate(values, cosine, sine):
    half = values.shape[-1] // 2
    first = values[..., :half]
    second = values[..., half:]
    return jnp.concatenate(
        [first * cosine - second * sine, second * cosine + first * sine], axis=-1
    )


def keep_state(state):
    return state


def dot(a, b, ca=1, cb=0):
    return lax.dot_general(a, b, (((ca,), (cb,)), ((), ())), preferred_element_type=f32)


def rope_tables(pos, half):
    index = lax.broadcasted_iota(i32, (half, 1), 0).astype(f32)
    rates = jnp.exp(-jnp.log(f32(10000.0)) * index / half)
    angles = rates * pos
    return jnp.cos(angles), jnp.sin(angles)


def rotate_t(lin, cosine, sine):
    width, rows = lin.shape
    parts = lin.reshape(width // HEAD_DIM, 2, HEAD_DIM // 2, rows)
    first, second = parts[:, 0], parts[:, 1]
    turned = [first * cosine - second * sine, second * cosine + first * sine]
    return jnp.stack(turned, axis=1).reshape(width, rows)


def gelu_both(u):
    square = u * u
    t = jnp.tanh(0.7978845608028654 * (u + 0.044715 * square * u))
    half = 0.5 * (1.0 + t)
    slope = half + 0.5 * u * (1.0 - t * t) * (0.7978845608028654 * (1.0 + 3 * 0.044715 * square))
    return u * half, slope


def row_chunks(rows, body, size=64):
    def step(i, _):
        body(pl.ds(pl.multiple_of(i * size, size), size))
        return 0

    lax.fori_loop(0, rows // size, step, 0)


def folded(rows):
    total = jnp.sum(rows, axis=0, keepdims=True)
    return sum(total[:, k : k + 128] for k in range(0, total.shape[1], 128))


ROWS, WIDTH, LOCAL, GROUP, HIDDEN, BLOCK = 256, 768, 384, 192, 1536, 48


def scratch_spec(windows):
    vm = pltpu.VMEM
    heads = (3, HEAD_DIM, ROWS)
    full32, full16, turned = vm((ROWS, WIDTH), f32), vm((ROWS, WIDTH), bf16), vm((WIDTH, ROWS), bf16)

    def job(columns):
        return [
            vm((2, 2, 2, 2, BLOCK, columns), bf16), vm((2, 2, 2, BLOCK, columns), bf16),
            vm((2, 2, BLOCK, columns), bf16), vm((2, BLOCK, columns), bf16), vm((BLOCK, columns), bf16),
        ]

    return dict(
        x=full16, gain1_v=vm((WIDTH,), f32), shift1_v=vm((WIDTH,), f32), gain2_v=vm((WIDTH,), f32), shift2_v=vm((WIDTH,), f32),
        downb_v=vm((WIDTH,), f32), upb_v=vm((HIDDEN,), f32), order=pltpu.SMEM((4,), i32), windows=pltpu.SMEM((windows,), i32), mixw=pltpu.SMEM((9,), f32),
        cotn=full16, cotb=full16, wq=vm((WIDTH, LOCAL), bf16), wk=vm((WIDTH, LOCAL), bf16), wv=vm((WIDTH, LOCAL), bf16),
        hist=vm((8, ROWS, WIDTH), bf16), wup=vm((WIDTH, HIDDEN), bf16), wdown=vm((HIDDEN, WIDTH), bf16),
        wof=vm((2, 2, 3, HEAD_DIM, WIDTH), bf16),
        vectors=vm((5, 1, WIDTH), f32), upb=vm((1, HIDDEN), f32), upsum=vm((1, HIDDEN), f32),
        qown=vm((2, *heads), bf16), kvown=vm((2, 3, 2, HEAD_DIM, ROWS), bf16),
        qt=vm((2, *heads), bf16), kv=vm((4, 3, 2, HEAD_DIM, ROWS), bf16),
        scores=vm((3, 2, 4, ROWS, ROWS), f32), bias=vm((2, 4, ROWS, ROWS), f32),
        peak=vm((3, 2, 1, ROWS), f32), denom=vm((3, 2, 1, ROWS), f32), acc=vm((3, 2, HEAD_DIM, ROWS), f32),
        delta=vm((3, 2, 1, ROWS), f32), cosine=vm((32, ROWS), f32), sine=vm((32, ROWS), f32),
        mix=vm((2, 2, *heads), bf16), mixout=vm(heads, bf16),
        unit1=full32, inv1=vm((ROWS, 1), f32), norm1=full16, norm1t=turned,
        hidden=full32, attn=full32, unit2=full32, inv2=vm((ROWS, 1), f32), norm2=full16, norm2t=turned,
        gblock=full32, gmlp=full16, gmlpt=turned, hacc=full32, gact=vm((ROWS, HIDDEN), f32),
        act=vm((ROWS, HIDDEN), bf16), gup=vm((ROWS, HIDDEN), bf16), gnorm2=full32, gnew=full32,
        ghid=vm((2, ROWS, WIDTH), bf16), mlp=vm((2, ROWS, WIDTH), bf16), gin=vm((2, ROWS, WIDTH), bf16),
        dpart=vm((2, 2, *heads), bf16), dsend=vm((2, 2, *heads), bf16), dout=vm((2, *heads), bf16),
        dkv=vm((4, 3, 2, HEAD_DIM, ROWS), bf16), dkvin=vm((4, 3, 2, HEAD_DIM, ROWS), bf16),
        dq=vm((3, HEAD_DIM, ROWS), f32), dqout=vm(heads, bf16), dqin=vm(heads, bf16),
        own0=vm((3, 2, HEAD_DIM, ROWS), f32), lin=vm((3, 2, *heads), bf16), gattnt=turned,
        small=vm((6, 16, WIDTH), f32), smallin=vm((5, 16, WIDTH), f32), last=vm((6, 16, 128), f32), lastin=vm((5, 16, 128), f32),
        job0=job(WIDTH), job1=job(WIDTH), job2=job(WIDTH), job3=job(WIDTH), job4=job(LOCAL), job5=job(WIDTH), job6=job(LOCAL),
        s_next=full16, s_block=full16, s_gin=full16, s_down=vm((BLOCK, HIDDEN), f32), s_up=vm((BLOCK, HIDDEN), f32),
        s_out=vm((BLOCK, LOCAL), f32), s_a=vm((BLOCK, WIDTH), f32), s_b=vm((BLOCK, LOCAL), f32), s_last=vm((16, 128), f32), s_small=vm((16, WIDTH), f32),
        osem=pltpu.SemaphoreType.DMA((12,)),
        ssem=pltpu.SemaphoreType.DMA((96,)), rsem=pltpu.SemaphoreType.DMA((96,)), lsem=pltpu.SemaphoreType.DMA((24,)),
    )


def layer_kernel(make, *refs):
    R = make(refs)
    z, b, y = lax.axis_index("seq"), lax.axis_index("batch"), lax.axis_index("tensor")
    near, flip, far = z + 1 - 2 * (z % 2), (z + 2) % 4, 3 - z
    m, p, xbit, core = z % 2, z // 2, b // 2, b % 2
    to_near, to_flip, to_far = dict(seq=near), dict(seq=flip), dict(seq=far)
    to_y, to_diag = dict(tensor=1 - y), dict(seq=near, tensor=1 - y)
    to_x, to_core = dict(batch=(b + 2) % 4), dict(batch=b + 1 - 2 * core)
    barrier = pltpu.get_barrier_semaphore()
    everyone = [to_near, to_flip, to_far, to_y, to_diag, to_x, to_core]
    for there in everyone:
        pl.semaphore_signal(barrier, inc=1, device_id=there, device_id_type=MESH)
    started = []

    def send(src, dst, there):
        i = len(started)
        copy = pltpu.make_async_remote_copy(
            src, dst, R.ssem.at[i], R.rsem.at[i], device_id=there, device_id_type=MESH
        )
        copy.start()
        started.append(copy)
        return copy

    def fetch(src, dst, i):
        copy = pltpu.make_async_copy(src, dst, R.lsem.at[i])
        copy.start()
        return copy

    get_small = [fetch(R.x_h, R.x, 9)]
    get_k = fetch(R.wk_h, R.wk, 1)
    pairs = [(R.gain1_in, R.gain1_v), (R.shift1_in, R.shift1_v), (R.order_in, R.order), (R.windows_in, R.windows)]
    pairs += [(R.gain2_in, R.gain2_v), (R.shift2_in, R.shift2_v), (R.downb_in, R.downb_v), (R.upb_in, R.upb_v)]
    pairs.append((R.mixw_in, R.mixw))
    for i, (src, dst) in enumerate(pairs):
        get_small.append(fetch(src, dst, 10 + i))
    get_q = fetch(R.wq_h, R.wq, 0)
    get_v = fetch(R.wv_h, R.wv, 2)
    written = []

    def write(src, dst):
        copy = pltpu.make_async_copy(src, dst, R.osem.at[len(written)])
        copy.start()
        written.append(copy)

    for c in get_small:
        c.wait()
    ends, total = [], 0
    for i in range(R.windows.shape[0]):
        total = total + R.windows[i]
        ends.append(total)
    for i, ref in enumerate((R.gain1_v, R.shift1_v, R.gain2_v, R.shift2_v, R.downb_v)):
        R.vectors[i] = ref[...][None]
    R.upb[...] = R.upb_v[...][None]
    R.gain1, R.shift1, R.gain2, R.shift2, R.downb = (R.vectors.at[i] for i in range(5))
    base = [R.order[k] * ROWS for k in (z, near, flip, far)]
    lane = lax.broadcasted_iota(i32, (1, ROWS), 1)

    def norm_first(rows):
        x = R.x[rows].astype(f32)
        centred = x - jnp.mean(x, axis=-1, keepdims=True)
        inverse = lax.rsqrt(jnp.mean(centred * centred, axis=-1, keepdims=True) + epsilon)
        unit = centred * inverse
        R.unit1[rows] = unit
        R.inv1[rows] = inverse
        R.norm1[rows] = (unit * R.gain1[...] + R.shift1[...]).astype(bf16)

    row_chunks(ROWS, norm_first)
    cosine, sine = rope_tables((base[0] + lane).astype(f32), HEAD_DIM // 2)
    R.cosine[...] = cosine
    R.sine[...] = sine
    split = (2, 3, HEAD_DIM, ROWS)
    get_k.wait()
    R.kvown[:, :, 0] = rotate_t(dot(R.norm1[...], R.wk[...]).T, cosine, sine).astype(bf16).reshape(split)
    get_v.wait()
    R.kvown[:, :, 1] = dot(R.norm1[...], R.wv[...]).T.astype(bf16).reshape(split)
    pl.semaphore_wait(barrier, len(everyone))
    near_in, flip_in, far_in = [], [], []

    def kv_out(h):
        near_in.append(send(R.kvown.at[1 - m, h], R.kv.at[1, h], to_near))
        flip_in.append(send(R.kvown.at[m, h], R.kv.at[2, h], to_flip))
        far_in.append(send(R.kvown.at[1 - m, h], R.kv.at[3, h], to_far))

    kv_out(0)
    get_q.wait()
    get_out = fetch(R.wout, R.wof.at[0], 5)
    get_cot = [fetch(R.cotn_h, R.cotn, 3), fetch(R.cotb_h, R.cotb, 4)]
    get_hist = fetch(R.history, R.hist, 6)
    get_down = fetch(R.wdown_h, R.wdown, 7)
    get_up = fetch(R.wup_h, R.wup, 8)
    queries = rotate_t(dot(R.norm1[...], R.wq[...]).T, cosine, sine) * 0.125
    R.qown[...] = queries.astype(bf16).reshape(split)
    q_in = [send(R.qown.at[1 - m, h], R.qt.at[1, h], to_near) for h in range(1)]
    kv_out(1)
    q_in.append(send(R.qown.at[1 - m, 1], R.qt.at[1, 1], to_near))
    kv_out(2)
    q_in.append(send(R.qown.at[1 - m, 2], R.qt.at[1, 2], to_near))
    get_out.wait()
    out_in = send(R.wof.at[0], R.wof.at[1], to_y)
    R.qt[0] = R.qown[m]
    R.kv[0] = R.kvown[m]

    for j in range(2):
        qpos = base[j] + lane
        start = 0 * qpos
        for end in ends:
            start = jnp.maximum(start, jnp.where(qpos >= end, end, 0))
        for r in range(4):
            kpos = base[r] + lax.broadcasted_iota(i32, (ROWS, ROWS), 0)
            R.bias[j, r] = jnp.where((kpos <= qpos) & (kpos >= start), 0.0, -1e30).astype(f32)
    for c in get_cot:
        c.wait()
    R.small[0] = jnp.zeros((16, WIDTH), f32)
    R.last[0] = jnp.zeros((16, 128), f32)
    mix_last = R.mixw[8]

    def block_grads(rows):
        g = R.cotb[rows].astype(f32) + mix_last * R.cotn[rows].astype(f32)
        R.gblock[rows] = g
        low = g.astype(bf16)
        R.gmlp[rows] = low
        R.small[0, 2:3] += 0.5 * jnp.sum(low.astype(f32), axis=0, keepdims=True)

    row_chunks(ROWS, block_grads)
    R.gmlpt[...] = R.gmlp[...].T
    R.norm1t[...] = R.norm1[...].T
    get_hist.wait()

    def history_sum(rows):
        cot = R.cotn[rows].astype(f32)
        total = 0
        for j in range(8):
            h = R.hist[j, rows].astype(f32)
            total = total + R.mixw[j] * h
            R.small[0, 3 + j // 6 : 4 + j // 6, 128 * (j % 6) : 128 * (j % 6) + 128] += 0.5 * folded(h * cot)
        R.hacc[rows] = total

    row_chunks(ROWS, history_sum, 32)
    get_down.wait()

    def active_grad(n, _):
        at = pl.ds(pl.multiple_of(256 * n, 256), 256)
        R.gact[:, at] = dot(R.gmlp[...], R.wdown[at], 1, 1)
        return 0

    lax.fori_loop(0, 6, active_grad, 0)

    def tile(h, j, r, first=False):
        s = dot(R.kv[r, h, 0], R.qt[j, h], 0, 0) + R.bias[j, r]
        R.scores[h, j, r] = s
        top = jnp.max(s, axis=0, keepdims=True)
        if first:
            e = jnp.exp(s - top)
            R.denom[h, j] = jnp.sum(e, axis=0, keepdims=True)
            R.acc[h, j] = dot(R.kv[r, h, 1], e.astype(bf16))
        else:
            old = R.peak[h, j]
            top = jnp.maximum(top, old)
            e = jnp.exp(s - top)
            alpha = jnp.exp(old - top)
            R.denom[h, j] = R.denom[h, j] * alpha + jnp.sum(e, axis=0, keepdims=True)
            R.acc[h, j] = R.acc[h, j] * alpha + dot(R.kv[r, h, 1], e.astype(bf16))
        R.peak[h, j] = top

    def finish(h, j):
        R.acc[h, j] = R.acc[h, j] * (1.0 / R.denom[h, j])
        R.peak[h, j] = R.peak[h, j] + jnp.log(R.denom[h, j])
        return R.acc[h, j].astype(bf16)

    mix_in = []
    for h in range(3):
        tile(h, 0, 0, True)
    for h in range(3):
        near_in[h].wait_recv()
        q_in[h].wait_recv()
        tile(h, 0, 1)
        tile(h, 1, 1, True)
        tile(h, 1, 0)
        flip_in[h].wait_recv()
        tile(h, 1, 2)
        tile(h, 0, 2)
        far_in[h].wait_recv()
        tile(h, 1, 3)
        tile(h, 0, 3)
        R.mixout[h] = finish(h, 1)
        R.mix[0, 0, h] = finish(h, 0)
        mix_in.append(send(R.mixout.at[h], R.mix.at[1, 1, h], to_diag))
        mix_in.append(send(R.mix.at[0, 0, h], R.mix.at[1, 0, h], to_y))
        mix_in.append(send(R.mixout.at[h], R.mix.at[0, 1, h], to_near))
    get_up.wait()
    out_in.wait_recv()
    for c in mix_in:
        c.wait_recv()
    group = (GROUP, ROWS)
    out = 0
    for t in range(2):
        for a in range(2):
            side = R.mix[(t + y) % 2, (a + m) % 2].reshape(group)
            out = out + dot(side, R.wof[(t + y) % 2, a].reshape(GROUP, WIDTH), 0, 0)
    R.attn[...] = out

    def norm_second(rows):
        hidden = R.x[rows].astype(f32) + R.attn[rows]
        R.hidden[rows] = hidden
        centred = hidden - jnp.mean(hidden, axis=-1, keepdims=True)
        inverse = lax.rsqrt(jnp.mean(centred * centred, axis=-1, keepdims=True) + epsilon)
        unit = centred * inverse
        R.unit2[rows] = unit
        R.inv2[rows] = inverse
        R.norm2[rows] = (unit * R.gain2[...] + R.shift2[...]).astype(bf16)

    bits = dict(core=core, x=xbit, near=m, flip=p)
    where = dict(core=to_core, x=to_x, near=to_near, flip=to_flip)
    place = dict(core=0, x=1, near=2, flip=3)

    class Job:
        def __init__(self, bufs, route):
            self.grads, self.landing, self.route, self.copy, self.step = bufs[0], bufs[1:], route, None, 0

        def put(self, value, columns):
            for k in range(16):
                at = tuple((k >> place[axis]) & 1 for axis in self.route)
                self.grads[(*at, slice(None), columns)] = value[BLOCK * k : BLOCK * k + BLOCK].astype(bf16)

        def mine(self):
            return tuple(bits[axis] for axis in self.route[: self.step])

        def push(self):
            axis = self.route[self.step]
            self.copy = send(self.grads.at[(*self.mine(), 1 - bits[axis])], self.landing[self.step], where[axis])

        def pull(self, out=None):
            self.copy.wait_recv()
            landing = self.landing[self.step]
            self.step += 1
            kept = self.mine()
            left = 4 - self.step

            def add(i, _):
                at = tuple((i // 2**k) % 2 for k in range(left))
                mine, theirs = self.grads[(*kept, *at)], landing[at if at else Ellipsis]
                if out is None:
                    self.grads[(*kept, *at)] = mine + theirs
                else:
                    out[...] = mine.astype(f32) + theirs.astype(f32)
                return 0

            if left:
                lax.fori_loop(0, 2**left, add, 0)
            else:
                add(0, 0)

        def turn(self):
            self.pull()
            self.push()

    usual = tuple(place)
    down0, down1, up0, up1 = (Job(bufs, usual) for bufs in (R.job0, R.job1, R.job2, R.job3))
    job_out, job_a = Job(R.job4, usual), Job(R.job5, usual)
    job_b = Job(R.job6, usual)

    row_chunks(ROWS, norm_second)
    for n in range(6):
        at = slice(256 * n, 256 * n + 256)
        u = dot(R.norm2[...], R.wup[:, at]) + R.upb[:, at]
        active, slope = gelu_both(u)
        R.act[:, at] = active.astype(bf16)
        grad = (R.gact[:, at] * slope).astype(bf16)
        R.gup[:, at] = grad
        R.upsum[:, at] = jnp.sum(grad.astype(f32), axis=0, keepdims=True)
        third = slice(256 * (n % 3), 256 * (n % 3) + 256)
        (down0, down1)[n // 3].put(dot(R.gmlpt[...], R.act[:, at]), third)
        if n == 2:
            down0.push()
            R.gnorm2[...] = dot(R.gup[:, :WIDTH], R.wup[:, :WIDTH], 1, 1)
    down1.push()
    R.gnorm2[...] += dot(R.gup[:, WIDTH:], R.wup[:, WIDTH:], 1, 1)

    def norm_back(grad, unit, inverse, gain):
        scaled = grad * gain
        return inverse * (
            scaled
            - jnp.mean(scaled, axis=-1, keepdims=True)
            - unit * jnp.mean(scaled * unit, axis=-1, keepdims=True)
        )

    def second_back(rows):
        back = norm_back(R.gnorm2[rows], R.unit2[rows], R.inv2[rows], R.gain2[...])
        R.ghid[0, rows] = (0.5 * R.gblock[rows] + back).astype(bf16)

    row_chunks(ROWS, second_back)
    d_in = []
    order = [(1, 1), (1, 0), (0, 1), (0, 0)]
    for h in range(3):
        weights = jnp.concatenate([R.wof[t, (a + m) % 2, h] for t, a in order], axis=0)
        parts = dot(weights, R.ghid[0], 1, 1).astype(bf16).reshape(4, HEAD_DIM, ROWS)
        for k in range(3):
            R.dsend[(*order[k], h)] = parts[k]
        R.dpart[0, 0, h] = parts[3]
        d_in.append(
            [
                send(R.dsend.at[1, 1, h], R.dpart.at[1, 1, h], to_diag),
                send(R.dsend.at[1, 0, h], R.dpart.at[0, 1, h], to_y),
                send(R.dsend.at[0, 1, h], R.dpart.at[1, 0, h], to_near),
            ]
        )
    ghid_in = send(R.ghid.at[0], R.ghid.at[1], to_y)

    class Sum:
        def __init__(self, held, landing, shared):
            self.held, self.landing, self.shared, self.step, self.copy = held, landing, shared, 0, None

        def push(self):
            there = (to_y, to_core, to_near, to_flip, to_x)[self.step]
            rows = pl.ds(0, self.shared if self.step == 0 else 16)
            self.copy = send(self.held.at[self.step, rows], self.landing.at[self.step, rows], there)

        def pull(self):
            self.copy.wait_recv()
            step, rows = self.step, self.shared if self.step == 0 else 16
            self.held[step + 1, 0:rows] = self.held[step, 0:rows] + self.landing[step, 0:rows]
            if rows < 16:
                self.held[step + 1, rows:16] = self.held[step, rows:16]
            self.step += 1

        def turn(self):
            self.pull()
            self.push()

    sums, last = Sum(R.small, R.smallin, 8), Sum(R.last, R.lastin, 16)

    kv_in, dq_in = [], []

    def back_head(h):
        for c in d_in[h]:
            c.wait_recv()
        for j in range(2):
            both = R.dpart[j, 0, h].astype(f32) + R.dpart[j, 1, h].astype(f32)
            R.dout[j, h] = both.astype(bf16)
            R.delta[h, j] = jnp.sum(R.dout[j, h].astype(f32) * R.acc[h, j], axis=0, keepdims=True)
        total = [0, 0]
        for r in (2, 3, 1, 0):
            dk, dv = 0, 0
            for j in range(2):
                probs = jnp.exp(R.scores[h, j, r] - R.peak[h, j])
                grad = dot(R.kv[r, h, 1], R.dout[j, h], 0, 0)
                low = (probs * (grad - R.delta[h, j])).astype(bf16)
                dv = dv + dot(R.dout[j, h], probs.astype(bf16), 1, 1)
                dk = dk + dot(R.qt[j, h], low, 1, 1)
                total[j] = total[j] + dot(R.kv[r, h, 0], low)
            if r:
                R.dkv[r, h, 0] = dk.astype(bf16)
                R.dkv[r, h, 1] = dv.astype(bf16)
                kv_in.append(send(R.dkv.at[r, h], R.dkvin.at[r, h], (to_near, to_flip, to_far)[r - 1]))
            else:
                R.own0[h, 0] = dk
                R.own0[h, 1] = dv
        R.dqout[h] = (0.125 * total[1]).astype(bf16)
        dq_in.append(send(R.dqout.at[h], R.dqin.at[h], to_near))
        R.dq[h] = 0.125 * total[0]

    def up_grads(job, k):
        for n in range(3):
            at = slice(WIDTH * k + 256 * n, WIDTH * k + 256 * n + 256)
            job.put(dot(R.norm2t[...], R.gup[:, at]), slice(256 * n, 256 * n + 256))
        job.push()

    down0.turn()
    R.norm2t[...] = R.norm2[...].T
    up_grads(up0, 0)
    down1.turn()
    back_head(0)
    up_grads(up1, 1)
    back_head(1)
    up0.turn()
    back_head(2)
    up1.turn()
    down0.turn()
    R.mlp[0] = dot(R.act[...], R.wdown[...]).astype(bf16)
    mlp_in = send(R.mlp.at[0], R.mlp.at[1], to_y)

    ghid_in.wait_recv()

    def whole_hidden(rows):
        hid = R.ghid[0, rows].astype(f32) + R.ghid[1, rows].astype(f32)
        R.gblock[rows] = hid
        R.gmlp[rows] = hid.astype(bf16)
        back = R.gnorm2[rows]
        R.small[0, 0:1] += jnp.sum(back * R.unit2[rows], axis=0, keepdims=True)
        R.small[0, 1:2] += jnp.sum(back, axis=0, keepdims=True)

    row_chunks(ROWS, whole_hidden)
    R.gattnt[...] = R.gmlp[...].T
    mixed = jnp.concatenate([R.mix[0, (a + m) % 2].reshape(group) for a in range(2)], axis=0)
    job_out.put(dot(R.gattnt[...], mixed, 1, 1), slice(None))
    job_out.push()
    down1.turn()
    job_out.turn()

    up0.turn()
    down0.turn()

    mlp_in.wait_recv()

    def block_out(rows):
        both = R.mlp[0, rows].astype(f32) + R.mlp[1, rows].astype(f32) + R.downb[...]
        value = R.hidden[rows] + both
        R.s_block[rows] = value.astype(bf16)
        R.s_next[rows] = (R.hacc[rows] + mix_last * value).astype(bf16)
        attn = R.attn[rows]
        for k, term in enumerate((value * R.cotn[rows].astype(f32), value * value, attn * attn, both * both)):
            R.small[0, 4:5, 128 * (2 + k) : 128 * (3 + k)] += 0.5 * folded(term)

    row_chunks(ROWS, block_out, 32)
    for k in range(8):
        R.small[0, 10 + k // 6 : 11 + k // 6, 128 * (k % 6) : 128 * (k % 6) + 128] = jnp.full((1, 128), R.mixw[k], f32)
    write(R.s_block, R.o_block)
    write(R.s_next, R.o_next)
    R.small[0, 8:9] = R.upsum[:, :WIDTH]
    R.small[0, 9:10] = R.upsum[:, WIDTH:]

    sums.push()

    cosine, sine = R.cosine[...], -R.sine[...]
    for h in range(3):
        for c in (*kv_in[3 * h : 3 * h + 3], dq_in[h]):
            c.wait_recv()
        for k in range(2):
            ours = R.own0[h, k] + R.dkvin[2, h, k].astype(f32)
            theirs = R.dkvin[1, h, k].astype(f32) + R.dkvin[3, h, k].astype(f32)
            if k == 0:
                ours, theirs = rotate_t(ours, cosine, sine), rotate_t(theirs, cosine, sine)
            R.lin[1 + k, m, h] = ours.astype(bf16)
            R.lin[1 + k, 1 - m, h] = theirs.astype(bf16)
        R.lin[0, m, h] = rotate_t(R.dq[h], cosine, sine).astype(bf16)
        R.lin[0, 1 - m, h] = rotate_t(R.dqin[h].astype(f32), cosine, sine).astype(bf16)
    lins = [R.lin[k].reshape(LOCAL, ROWS) for k in range(3)]
    first = dot(R.wq[...], lins[0]) + dot(R.wk[...], lins[1]) + dot(R.wv[...], lins[2])
    R.gnew[...] = first.T

    def first_back(rows):
        grad = R.gnew[rows]
        R.gin[0, rows] = norm_back(grad, R.unit1[rows], R.inv1[rows], R.gain1[...]).astype(bf16)
        for i, term in enumerate((grad * R.unit1[rows], grad)):
            total = jnp.sum(term, axis=0, keepdims=True)
            for k in range(6):
                R.last[0, 6 * i + k : 6 * i + k + 1] += total[:, 128 * k : 128 * k + 128]

    row_chunks(ROWS, first_back)
    last.push()
    gin_in = send(R.gin.at[0], R.gin.at[1], to_y)
    every = jnp.concatenate(lins, axis=0)
    job_a.put(dot(R.norm1t[...], every[:WIDTH], 1, 1), slice(None))
    job_a.push()
    job_b.put(dot(R.norm1t[...], every[WIDTH:], 1, 1), slice(None))
    job_b.push()
    sums.turn()
    up1.turn()
    down1.turn()
    last.turn()
    sums.turn()
    job_a.turn()
    job_b.turn()
    last.turn()
    job_out.turn()
    up0.turn()
    down0.pull(R.s_down.at[:, pl.ds(0, WIDTH)])
    down1.pull(R.s_down.at[:, pl.ds(WIDTH, WIDTH)])
    write(R.s_down, R.o_down)
    sums.turn()
    last.turn()
    up1.turn()
    gin_in.wait_recv()

    def grad_in(rows):
        both = R.gin[0, rows].astype(f32) + R.gin[1, rows].astype(f32)
        R.s_gin[rows] = (R.gblock[rows] + both).astype(bf16)

    row_chunks(ROWS, grad_in)
    write(R.s_gin, R.o_gin)
    job_a.turn()
    job_out.turn()
    sums.turn()
    last.turn()
    job_b.turn()
    up0.pull(R.s_up.at[:, pl.ds(0, WIDTH)])
    up1.pull(R.s_up.at[:, pl.ds(WIDTH, WIDTH)])
    write(R.s_up, R.o_up)
    job_a.turn()
    job_b.turn()
    job_out.pull(R.s_out)
    write(R.s_out, R.o_out)
    sums.pull()
    R.s_small[...] = R.small[5]
    R.s_small[10:12] = R.small[0, 10:12]
    write(R.s_small, R.o_small)
    last.pull()
    R.s_last[...] = R.last[5]
    write(R.s_last, R.o_last)
    job_a.pull(R.s_a)
    write(R.s_a, R.o_a)
    job_b.pull(R.s_b)
    write(R.s_b, R.o_b)
    for c in started:
        c.wait_send()
    for c in written:
        c.wait()


def last_kernel(make, entries, *refs):
    R = make(refs)
    copies = []

    def copy(src, dst):
        moving = pltpu.make_async_copy(src, dst, R.sems.at[len(copies)])
        moving.start()
        copies.append(moving)
        return moving

    get_cot = [copy(R.cotn, R.v_cotn), copy(R.o_small, R.v_small), copy(R.o_last, R.v_last)]
    pairs = [(R.o_next, R.v_next, R.next.at[0]), (R.o_block, R.v_block, R.block.at[0])]
    pairs += [(R.o_gin, R.v_gin, R.gin.at[0]), (R.o_up, R.v_up, R.gup), (R.o_down, R.v_down, R.gdown)]
    pairs.append((R.o_out, R.v_out, R.gout))
    loads = [copy(src, dst) for src, dst, _ in pairs]
    loads += [copy(R.o_a, R.v_a), copy(R.o_b, R.v_b)]
    for c in get_cot:
        c.wait()
    count = len(copies)
    for j in range(8):
        weight = R.v_small[10 + j // 6 : 11 + j // 6, 128 * (j % 6) : 128 * (j % 6) + 1]
        R.v_hist[j] = (weight * R.v_cotn[...].astype(f32)).astype(bf16)
        copy(R.v_hist.at[j], R.ghist.at[j, 0])
    for c, (_, held, out) in zip(loads, pairs):
        c.wait()
        copy(held, out)
    loads[-2].wait()
    loads[-1].wait()
    copy(R.v_a.at[:, pl.ds(0, LOCAL)], R.gq)
    copy(R.v_a.at[:, pl.ds(LOCAL, LOCAL)], R.gk)
    copy(R.v_b, R.gv)
    for k in range(6):
        R.v_gain1[128 * k : 128 * k + 128] = R.v_last[k]
        R.v_shift1[128 * k : 128 * k + 128] = R.v_last[6 + k]
    for i, ref in enumerate((R.v_gain2, R.v_shift2, R.v_downb)):
        ref[...] = R.v_small[i]
    copy(R.v_gain1, R.gain1)
    copy(R.v_shift1, R.shift1)
    copy(R.v_gain2, R.gain2)
    copy(R.v_shift2, R.shift2)
    copy(R.v_downb, R.downb)
    R.v_upb[0:WIDTH] = R.v_small[8]
    R.v_upb[WIDTH:HIDDEN] = R.v_small[9]
    copy(R.v_upb, R.upb)
    parts = [R.v_small[3 + k // 6 : 4 + k // 6, 128 * (k % 6) : 128 * (k % 6) + 128] for k in range(12)]
    sums = jnp.sum(jnp.concatenate(parts, axis=0), axis=1, keepdims=True)
    row = jnp.broadcast_to(sums, (12, 128)).T[0:1]
    R.v_gmix[...] = row[0, :9]
    R.v_rms[...] = jnp.sqrt(row / entries)[0, 9:]
    copy(R.v_gmix, R.gmix)
    copy(R.v_rms, R.rms)
    for c in copies[count:]:
        c.wait()


def out_spec(shape, dtype=f32):
    return jax.ShapeDtypeStruct(shape, dtype)


def namer(*groups):
    names = [name for group in groups for name in group]
    return lambda refs: SimpleNamespace(**dict(zip(names, refs)))


def per_device_block(
    inputs,
    history,
    window_lengths,
    block_order,
    first_gain,
    first_shift,
    query_weight,
    key_weight,
    value_weight,
    out_weight,
    second_gain,
    second_shift,
    up_weight,
    up_bias,
    down_weight,
    down_bias,
    mix_weights,
    cotangent_next,
    cotangent_block,
):
    hbm = pl.BlockSpec(memory_space=pl.ANY)
    args = dict(
        x_h=inputs[0], gain1_in=first_gain, shift1_in=first_shift, gain2_in=second_gain, shift2_in=second_shift,
        upb_in=up_bias, downb_in=down_bias,
        cotn_h=cotangent_next[0], cotb_h=cotangent_block[0], wq_h=query_weight, wk_h=key_weight, wv_h=value_weight,
        wout=out_weight.reshape(2, 3, HEAD_DIM, WIDTH), history=history[:, 0], wup_h=up_weight, wdown_h=down_weight,
        windows_in=window_lengths[0], order_in=block_order, mixw_in=mix_weights,
    )
    specs = [hbm] * len(args)
    outs = dict(
        o_next=out_spec((ROWS, WIDTH), bf16), o_block=out_spec((ROWS, WIDTH), bf16), o_gin=out_spec((ROWS, WIDTH), bf16),
        o_down=out_spec((BLOCK, HIDDEN)), o_up=out_spec((BLOCK, HIDDEN)), o_out=out_spec((BLOCK, LOCAL)),
        o_a=out_spec((BLOCK, WIDTH)), o_b=out_spec((BLOCK, LOCAL)), o_small=out_spec((16, WIDTH)), o_last=out_spec((16, 128)),
    )
    scratch = scratch_spec(window_lengths.shape[1])
    flat, names = [], []
    for name, spec in scratch.items():
        several = isinstance(spec, list)
        names.append((name, len(spec) if several else 0))
        flat.extend(spec if several else [spec])

    def make(refs):
        R, k = dict(zip([*args, *outs], refs)), len(args) + len(outs)
        for name, count in names:
            R[name] = refs[k : k + count] if count else refs[k]
            k += max(count, 1)
        return SimpleNamespace(**R)

    held = pl.pallas_call(
        functools.partial(layer_kernel, make),
        out_shape=list(outs.values()),
        in_specs=specs,
        out_specs=[hbm] * len(outs),
        scratch_shapes=flat,
        compiler_params=pltpu.CompilerParams(
            collective_id=1, has_side_effects=True, vmem_limit_bytes=63 * 2**20
        ),
    )(*args.values())
    held = dict(zip(outs, held))
    rows3 = (1, ROWS, WIDTH)
    results = dict(
        next=out_spec(rows3, bf16), block=out_spec(rows3, bf16), gin=out_spec(rows3, bf16),
        ghist=out_spec((8, *rows3), bf16), gain1=out_spec((WIDTH,)), shift1=out_spec((WIDTH,)),
        gq=out_spec((BLOCK, LOCAL)), gk=out_spec((BLOCK, LOCAL)), gv=out_spec((BLOCK, LOCAL)),
        gout=out_spec((BLOCK, LOCAL)), gain2=out_spec((WIDTH,)), shift2=out_spec((WIDTH,)),
        gup=out_spec((BLOCK, HIDDEN)), upb=out_spec((HIDDEN,)), gdown=out_spec((BLOCK, HIDDEN)),
        downb=out_spec((WIDTH,)), gmix=out_spec((9,)), rms=out_spec((3,)),
    )
    entries = float(lax.axis_size("batch") * lax.axis_size("seq") * ROWS * WIDTH)
    given = dict(cotn=cotangent_next[0], **held)
    vm, full, row = pltpu.VMEM, pltpu.VMEM((ROWS, WIDTH), bf16), pltpu.VMEM((WIDTH,), f32)
    staging = dict(
        v_cotn=full, v_hist=vm((8, ROWS, WIDTH), bf16), v_next=full, v_block=full, v_gin=full,
        v_up=vm((BLOCK, HIDDEN), f32), v_down=vm((BLOCK, HIDDEN), f32), v_out=vm((BLOCK, LOCAL), f32),
        v_a=vm((BLOCK, WIDTH), f32), v_b=vm((BLOCK, LOCAL), f32), v_small=vm((16, WIDTH), f32), v_last=vm((16, 128), f32),
        v_gain1=row, v_shift1=row, v_gain2=row, v_shift2=row, v_downb=row, v_upb=vm((HIDDEN,), f32),
        v_gmix=vm((9,), f32), v_rms=vm((3,), f32), sems=pltpu.SemaphoreType.DMA((40,)),
    )
    done = pl.pallas_call(
        functools.partial(last_kernel, namer(given, results, staging), entries),
        out_shape=list(results.values()),
        in_specs=[hbm] * len(given),
        out_specs=[hbm] * len(results),
        scratch_shapes=list(staging.values()),
        compiler_params=pltpu.CompilerParams(vmem_limit_bytes=63 * 2**20),
    )(*given.values())
    done = dict(zip(results, done))
    turned = dict(gout=done[list(results)[9]].T, gdown=done[list(results)[14]].T)
    return tuple((done | turned).values())


def device_function(mesh):
    return per_device_block if mesh.shape["seq"] == 4 else per_device_general


def per_device_general(
    inputs,
    history,
    window_lengths,
    block_order,
    first_gain,
    first_shift,
    query_weight,
    key_weight,
    value_weight,
    out_weight,
    second_gain,
    second_shift,
    up_weight,
    up_bias,
    down_weight,
    down_bias,
    mix_weights,
    cotangent_next,
    cotangent_block,
):
    rows = inputs.shape[1]
    width = inputs.shape[2]
    local_width = query_weight.shape[1]
    heads = local_width // HEAD_DIM
    half = HEAD_DIM // 2
    depth = history.shape[0]
    total = rows * lax.axis_size("seq")
    size = min(1024, total)
    count = total // size
    split = (rows, heads, HEAD_DIM)
    offsets = jnp.arange(rows, dtype=jnp.int32)
    own_pos = block_order[lax.axis_index("seq")] * rows + offsets
    every_row = jnp.arange(total, dtype=jnp.int32)
    every_pos = block_order[every_row // rows] * rows + every_row % rows
    ends = jnp.cumsum(window_lengths[0])
    own_docs = jnp.sum((own_pos[:, None] >= ends[None, :]).astype(jnp.int32), axis=1)
    every_docs = jnp.sum((every_pos[:, None] >= ends[None, :]).astype(jnp.int32), axis=1)
    rates = jnp.exp(-jnp.log(10000.0) * jnp.arange(half, dtype=jnp.float32) / half)
    angles = own_pos.astype(jnp.float32)[:, None] * rates[None, :]
    cosine = jnp.cos(angles)[:, None, :]
    sine = jnp.sin(angles)[:, None, :]
    residual = inputs[0].astype(jnp.float32)
    normed_first, unit_first, scale_first = layer_parts(residual, first_gain, first_shift)
    normed_first = normed_first.astype(jnp.bfloat16)
    query_lin = jnp.dot(normed_first, query_weight, preferred_element_type=jnp.float32)
    key_lin = jnp.dot(normed_first, key_weight, preferred_element_type=jnp.float32)
    value_lin = jnp.dot(normed_first, value_weight, preferred_element_type=jnp.float32)
    queries = (rotate(query_lin.reshape(split), cosine, sine) * 0.125).astype(jnp.bfloat16)
    keys = (
        rotate(key_lin.reshape(split), cosine, sine).reshape(rows, local_width).astype(jnp.bfloat16)
    )
    values = value_lin.astype(jnp.bfloat16)
    all_keys, all_values = (
        lax.all_gather(keys, "seq", axis=0, tiled=True),
        lax.all_gather(values, "seq", axis=0, tiled=True),
    )

    def block_mask(index):
        key_pos = lax.dynamic_slice_in_dim(every_pos, index * size, size)
        key_docs = lax.dynamic_slice_in_dim(every_docs, index * size, size)
        return (key_pos[None, :] <= own_pos[:, None]) & (key_docs[None, :] == own_docs[:, None])

    def block_rows(array, index):
        return lax.dynamic_slice_in_dim(array, index * size, size).reshape(size, heads, HEAD_DIM)

    def block_scores(index, key_rows):
        return jnp.einsum(
            "qhd,khd->hqk", queries, block_rows(key_rows, index), preferred_element_type=jnp.float32
        )

    def stats_step(index, carry):
        allowed = block_mask(index)

        def update(state):
            peak, denom = state
            masked = jnp.where(allowed[None], block_scores(index, all_keys), -1e30)
            fresh = jnp.maximum(peak, jnp.max(masked, axis=-1))
            weights = jnp.where(allowed[None], jnp.exp(masked - fresh[..., None]), 0.0)
            return (fresh, denom * jnp.exp(peak - fresh) + jnp.sum(weights, axis=-1))

        return lax.cond(jnp.any(allowed), update, keep_state, carry)

    start_stats = (
        jnp.full((heads, rows), -1e30, jnp.float32),
        jnp.zeros((heads, rows), jnp.float32),
    )
    peak, denom = lax.fori_loop(0, count, stats_step, start_stats)

    def block_probs(index, allowed, key_rows):
        scores = block_scores(index, key_rows)
        return jnp.where(allowed[None], jnp.exp(scores - peak[..., None]), 0.0) / denom[..., None]

    def output_step(index, carry):
        allowed = block_mask(index)

        def output_accumulate(state):
            probs_low = block_probs(index, allowed, all_keys).astype(jnp.bfloat16)
            return state + jnp.einsum(
                "hqk,khd->qhd",
                probs_low,
                block_rows(all_values, index),
                preferred_element_type=jnp.float32,
            )

        return lax.cond(jnp.any(allowed), output_accumulate, keep_state, carry)

    running = lax.fori_loop(0, count, output_step, jnp.zeros(split, jnp.float32))
    mixed = running.reshape(rows, local_width).astype(jnp.bfloat16)
    attn_out = lax.psum(
        jnp.dot(mixed, out_weight, preferred_element_type=jnp.float32).astype(jnp.bfloat16),
        "tensor",
    ).astype(jnp.float32)
    hidden = residual + attn_out
    normed_second, unit_second, scale_second = layer_parts(hidden, second_gain, second_shift)
    normed_second = normed_second.astype(jnp.bfloat16)
    upward = jnp.dot(normed_second, up_weight, preferred_element_type=jnp.float32) + up_bias
    active_full, gelu_pull = jax.vjp(gelu_tanh, upward)
    active = active_full.astype(jnp.bfloat16)
    mlp_out = (
        lax.psum(
            jnp.dot(active, down_weight, preferred_element_type=jnp.float32).astype(jnp.bfloat16),
            "tensor",
        ).astype(jnp.float32)
        + down_bias
    )
    block_value = hidden + mlp_out
    history_low = history[:, 0]
    next_value = (
        jnp.sum(mix_weights[:depth, None, None] * history_low.astype(jnp.float32), axis=0)
        + mix_weights[depth] * block_value
    )
    cot_low = cotangent_next[0]
    cot_next = cot_low.astype(jnp.float32)
    cot_block = cotangent_block[0].astype(jnp.float32)
    grad_history = (mix_weights[:depth, None, None] * cot_next[None]).astype(jnp.bfloat16)
    mix_terms = jnp.concatenate(
        [
            jnp.einsum("jsd,sd->j", history_low, cot_low, preferred_element_type=jnp.float32),
            jnp.sum(block_value * cot_next)[None],
        ]
    )
    grad_block = cot_block + mix_weights[depth] * cot_next
    grad_mlp = grad_block.astype(jnp.bfloat16)
    grad_down = jnp.einsum("sf,sd->fd", active, grad_mlp, preferred_element_type=jnp.float32)
    grad_active = jnp.einsum("sd,fd->sf", grad_mlp, down_weight, preferred_element_type=jnp.float32)
    grad_up = gelu_pull(grad_active)[0].astype(jnp.bfloat16)
    grad_upw = jnp.einsum("sd,sf->df", normed_second, grad_up, preferred_element_type=jnp.float32)
    grad_normed_second = lax.psum(
        jnp.einsum("sf,df->sd", grad_up, up_weight, preferred_element_type=jnp.float32).astype(
            jnp.bfloat16
        ),
        "tensor",
    ).astype(jnp.float32)
    grad_hidden = grad_block + norm_backward(
        grad_normed_second, unit_second, scale_second, second_gain
    )
    grad_attn = grad_hidden.astype(jnp.bfloat16)
    grad_outw = jnp.einsum("sk,sd->kd", mixed, grad_attn, preferred_element_type=jnp.float32)
    grad_mixed = (
        jnp.einsum("sd,kd->sk", grad_attn, out_weight, preferred_element_type=jnp.float32)
        .astype(jnp.bfloat16)
        .reshape(split)
    )
    back_keys, back_values = (
        lax.all_gather(keys, "seq", axis=0, tiled=True),
        lax.all_gather(values, "seq", axis=0, tiled=True),
    )

    def delta_step(index, carry):
        allowed = block_mask(index)

        def delta_accumulate(state):
            probs = block_probs(index, allowed, back_keys)
            grad_probs = jnp.einsum(
                "qhd,khd->hqk",
                grad_mixed,
                block_rows(back_values, index),
                preferred_element_type=jnp.float32,
            )
            return state + jnp.sum(probs * grad_probs, axis=-1)

        return lax.cond(jnp.any(allowed), delta_accumulate, keep_state, carry)

    delta = lax.fori_loop(0, count, delta_step, jnp.zeros((heads, rows), jnp.float32))

    def grad_step(index, carry):
        allowed = block_mask(index)

        def grad_accumulate(state):
            grad_queries, key_buffer, value_buffer = state
            key_rows = block_rows(back_keys, index)
            value_rows = block_rows(back_values, index)
            probs = block_probs(index, allowed, back_keys)
            grad_probs = jnp.einsum(
                "qhd,khd->hqk", grad_mixed, value_rows, preferred_element_type=jnp.float32
            )
            grad_scores = (probs * (grad_probs - delta[..., None])).astype(jnp.bfloat16)
            grad_queries = grad_queries + jnp.einsum(
                "hqk,khd->qhd", grad_scores, key_rows, preferred_element_type=jnp.float32
            )
            key_part = jnp.einsum(
                "hqk,qhd->khd", grad_scores, queries, preferred_element_type=jnp.float32
            ).reshape(size, local_width)
            value_part = jnp.einsum(
                "hqk,qhd->khd",
                probs.astype(jnp.bfloat16),
                grad_mixed,
                preferred_element_type=jnp.float32,
            ).reshape(size, local_width)
            key_buffer = lax.dynamic_update_slice_in_dim(key_buffer, key_part, index * size, 0)
            value_buffer = lax.dynamic_update_slice_in_dim(
                value_buffer, value_part, index * size, 0
            )
            return (grad_queries, key_buffer, value_buffer)

        return lax.cond(jnp.any(allowed), grad_accumulate, keep_state, carry)

    start_grads = (
        jnp.zeros(split, jnp.float32),
        jnp.zeros((total, local_width), jnp.float32),
        jnp.zeros((total, local_width), jnp.float32),
    )
    grad_queries, key_buffer, value_buffer = lax.fori_loop(0, count, grad_step, start_grads)
    grad_keys, grad_values = (
        lax.psum_scatter(
            key_buffer.astype(jnp.bfloat16), "seq", scatter_dimension=0, tiled=True
        ).astype(jnp.float32),
        lax.psum_scatter(
            value_buffer.astype(jnp.bfloat16), "seq", scatter_dimension=0, tiled=True
        ).astype(jnp.float32),
    )
    grad_query_lin = (
        rotate(grad_queries * 0.125, cosine, -sine).reshape(rows, local_width).astype(jnp.bfloat16)
    )
    grad_key_lin = (
        rotate(grad_keys.reshape(split), cosine, -sine)
        .reshape(rows, local_width)
        .astype(jnp.bfloat16)
    )
    grad_value_lin = grad_values.astype(jnp.bfloat16)
    grad_queryw = jnp.einsum(
        "sd,se->de", normed_first, grad_query_lin, preferred_element_type=jnp.float32
    )
    grad_keyw = jnp.einsum(
        "sd,se->de", normed_first, grad_key_lin, preferred_element_type=jnp.float32
    )
    grad_valuew = jnp.einsum(
        "sd,se->de", normed_first, grad_value_lin, preferred_element_type=jnp.float32
    )
    local_normed = jnp.einsum(
        "se,de->sd", grad_query_lin, query_weight, preferred_element_type=jnp.float32
    )
    local_normed = local_normed + jnp.einsum(
        "se,de->sd", grad_key_lin, key_weight, preferred_element_type=jnp.float32
    )
    local_normed = local_normed + jnp.einsum(
        "se,de->sd", grad_value_lin, value_weight, preferred_element_type=jnp.float32
    )
    grad_normed_first = lax.psum(local_normed.astype(jnp.bfloat16), "tensor").astype(jnp.float32)
    grad_input = grad_hidden + norm_backward(grad_normed_first, unit_first, scale_first, first_gain)
    shared_grads = (
        lax.psum_scatter(grad_queryw, ("seq", "batch"), scatter_dimension=0, tiled=True),
        lax.psum_scatter(grad_keyw, ("seq", "batch"), scatter_dimension=0, tiled=True),
        lax.psum_scatter(grad_valuew, ("seq", "batch"), scatter_dimension=0, tiled=True),
        lax.psum_scatter(grad_outw, ("seq", "batch"), scatter_dimension=1, tiled=True),
        lax.psum_scatter(grad_upw, ("seq", "batch"), scatter_dimension=0, tiled=True),
        lax.psum_scatter(grad_down, ("seq", "batch"), scatter_dimension=1, tiled=True),
    )
    square_terms = jnp.stack(
        [
            jnp.sum(block_value * block_value),
            jnp.sum(attn_out * attn_out),
            jnp.sum(mlp_out * mlp_out),
        ]
    )
    small_terms = lax.psum(
        (
            jnp.sum(grad_normed_first * unit_first, axis=0),
            jnp.sum(grad_normed_first, axis=0),
            jnp.sum(grad_normed_second * unit_second, axis=0),
            jnp.sum(grad_normed_second, axis=0),
            jnp.sum(grad_up.astype(jnp.float32), axis=0),
            jnp.sum(grad_mlp.astype(jnp.float32), axis=0),
            mix_terms,
            square_terms,
        ),
        ("seq", "batch"),
    )
    entries = float(lax.axis_size("batch") * total * width)
    rms_values = jnp.sqrt(small_terms[7] / entries)
    return (
        next_value.astype(jnp.bfloat16)[None],
        block_value.astype(jnp.bfloat16)[None],
        grad_input.astype(jnp.bfloat16)[None],
        grad_history[:, None],
        small_terms[0],
        small_terms[1],
        shared_grads[0],
        shared_grads[1],
        shared_grads[2],
        shared_grads[3],
        small_terms[2],
        small_terms[3],
        shared_grads[4],
        small_terms[4],
        shared_grads[5],
        small_terms[5],
        small_terms[6],
        rms_values,
    )


def solution(mesh):
    in_specs = (
        P("batch", "seq", None),
        P(None, "batch", "seq", None),
        P("batch", None),
        P(),
        P(),
        P(),
        P(None, "tensor"),
        P(None, "tensor"),
        P(None, "tensor"),
        P("tensor", None),
        P(),
        P(),
        P(None, "tensor"),
        P("tensor"),
        P("tensor", None),
        P(),
        P(),
        P("batch", "seq", None),
        P("batch", "seq", None),
    )
    out_specs = (
        P("batch", "seq", None),
        P("batch", "seq", None),
        P("batch", "seq", None),
        P(None, "batch", "seq", None),
        P(),
        P(),
        P(("seq", "batch"), "tensor"),
        P(("seq", "batch"), "tensor"),
        P(("seq", "batch"), "tensor"),
        P("tensor", ("seq", "batch")),
        P(),
        P(),
        P(("seq", "batch"), "tensor"),
        P("tensor"),
        P("tensor", ("seq", "batch")),
        P(),
        P(),
        P(),
    )
    return jax.shard_map(
        device_function(mesh), mesh=mesh, in_specs=in_specs, out_specs=out_specs, check_vma=False
    )
```
